512 devices in a mesh: ctx: 64 (over x, y_lo, z), tp: 8 (over y_hi, core).
Axes of the slice: x: 4, y: 8 (y_hi: 4, y_lo: 2; y = y_hi * 2 + y_lo), z: 8, core: 2. Of those that a mesh axis runs over, the one named last changes fastest.
Arguments:
- query_vectors: bfloat16 [8192, 3072], P(('ctx', 'tp')), may hold values from -20 to 20
- key_vectors: bfloat16 [8192, 3072], P(('ctx', 'tp')), may hold values from -20 to 20
- value_vectors: bfloat16 [8192, 3072], P(('ctx', 'tp')), may hold values from -6 to 6
- out_weight: bfloat16 [3072, 5120], P('tp'), may hold values from -0.109375 to 0.109375
Outputs:
- mixed: bfloat16 [8192, 5120], P(('ctx', 'tp'))
The draws below stay inside these ranges and needn't reach their ends.
All inputs are finite; a program needn't handle non-finite values.
Results may differ from the reference program's by a relative error of at most 0.027.
Values may be sent and summed in bfloat16 or wider, within the bound.
A program may use at most 64 MiB of HBM per device.

```python
import math
import jax
import jax.numpy as jnp
from jax import lax

D = 5120
HD = 128
HEADS = 24
TOKENS = 8192
N_TP = 8


def base_field(key):
    values = jax.random.normal(key, (TOKENS, HEADS * HD), jnp.float32)
    return jnp.clip(values, -6.0, 6.0) * 1.75


def draw_query_vectors(key, part):
    values = base_field(jax.random.fold_in(key, 1))
    return values.astype(jnp.bfloat16)


def draw_key_vectors(key, part):
    values = base_field(jax.random.fold_in(key, 2))
    return values.astype(jnp.bfloat16)


def level_of(stream_key, shape, shards, low, high):
    gain = 1.0
    for position, blocks in shards:
        heights = jax.random.uniform(jax.random.fold_in(jax.random.fold_in(stream_key, 6), position), (blocks,), jnp.float32, low / len(shards), high / len(shards))
        gain = gain * jnp.repeat(jnp.exp(heights), shape[position] // blocks).reshape((-1,) + (1,) * (len(shape) - 1 - position))
    return gain


def gaussian(own_key, shape, deviation, limit, cuts=(), dtype=jnp.bfloat16):
    gain = level_of(own_key, shape, cuts, -0.22, 0.18) if cuts else 1.0
    values = jax.random.normal(own_key, shape, jnp.float32) * deviation * gain
    return jnp.minimum(jnp.maximum(values, -limit), limit).astype(dtype)


def setup_inputs(seed: int = 0) -> dict:
    seeds = jax.random.split(jax.random.key(seed), 5)
    query_vectors = draw_query_vectors(jax.random.fold_in(seeds[4], 71), 0)
    key_vectors = draw_key_vectors(jax.random.fold_in(seeds[4], 71), 0)
    value_vectors = gaussian(seeds[2], (TOKENS, HEADS * HD), 1.0, 6.0, ((0, 512),))
    out_weight = gaussian(seeds[3], (HEADS * HD, D), (HEADS * HD) ** -0.5, 0.109375, ((0, 8),))
    return dict(query_vectors=query_vectors, key_vectors=key_vectors, value_vectors=value_vectors, out_weight=out_weight)


def reference(query_vectors, key_vectors, value_vectors, out_weight):
    score_scale = 1.0 / math.sqrt(HD)
    query_heads = query_vectors.astype(jnp.float32).reshape(TOKENS, HEADS, HD)
    key_heads = key_vectors.astype(jnp.float32).reshape(TOKENS, HEADS, HD)
    value_heads = value_vectors.astype(jnp.float32).reshape(TOKENS, HEADS, HD)
    block_rows = math.gcd(TOKENS, 128)
    block_count = TOKENS // block_rows

    def attend_block(query_block):
        scores = jnp.einsum('ihd,jhd->ihj', query_block, key_heads, precision=lax.Precision.HIGHEST) * score_scale
        row_peak = lax.optimization_barrier(jnp.max(scores, axis=-1))
        weights_low = jnp.exp(scores - row_peak[..., None]).astype(jnp.bfloat16)
        weights_wide = weights_low.astype(jnp.float32)
        row_total = lax.optimization_barrier(jnp.sum(weights_wide, axis=-1))
        weighted = jnp.einsum('ihj,jhd->ihd', weights_wide, value_heads, precision=lax.Precision.HIGHEST)
        return (weighted / row_total[..., None]).astype(jnp.bfloat16).reshape(block_rows, HEADS * HD)
    attended = lax.map(attend_block, query_heads.reshape(block_count, block_rows, HEADS, HD))
    attended = attended.reshape(TOKENS, HEADS * HD)
    group_cols = HEADS // N_TP * HD
    mixed = jnp.zeros((TOKENS, D), jnp.float32)
    for group in range(N_TP):
        partial_low = jnp.dot(attended[:, group * group_cols:(group + 1) * group_cols], out_weight[group * group_cols:(group + 1) * group_cols, :], preferred_element_type=jnp.float32).astype(jnp.bfloat16)
        partial_low = lax.optimization_barrier(partial_low)
        mixed = mixed + partial_low.astype(jnp.float32)
    return mixed.astype(jnp.bfloat16)
```

```python
import math

import jax
import jax.numpy as jnp
import numpy as np
from jax import lax
from jax.sharding import Mesh
from jax.sharding import PartitionSpec as P

HD = 128
KEY_SPLIT = 8


def attend_local(query_heads, key_heads, value_heads, score_scale):
    scores = (
        jnp.einsum("hid,hjd->hij", query_heads, key_heads, preferred_element_type=jnp.float32)
        * score_scale
    )
    row_peak = jnp.max(scores, axis=-1)
    weights_low = jnp.exp(scores - row_peak[..., None]).astype(jnp.bfloat16)
    row_total = jnp.sum(weights_low.astype(jnp.float32), axis=-1)
    weighted = jnp.einsum(
        "hij,hjd->hid", weights_low, value_heads, preferred_element_type=jnp.float32
    )
    return row_peak, row_total, weighted


def local(query_vectors, key_vectors, value_vectors, out_weight):
    score_scale = 1.0 / math.sqrt(HD)
    tp_count = lax.axis_size("tp")
    own_heads = query_vectors.shape[1] // HD // tp_count

    def own_group(rows):
        return lax.all_to_all(rows, "tp", 1, 0, tiled=True)

    def heads_major(rows):
        return rows.reshape(rows.shape[0], own_heads, HD).transpose(1, 0, 2)

    block_q = own_group(query_vectors)
    block_k = own_group(key_vectors)
    block_v = own_group(value_vectors)
    block_rows = block_q.shape[0]
    query_heads = heads_major(lax.all_gather(block_q, "ca", axis=0, tiled=True))
    key_heads = heads_major(lax.all_gather(block_k, "cz", axis=0, tiled=True))
    value_heads = heads_major(lax.all_gather(block_v, "cz", axis=0, tiled=True))

    row_peak, row_total, weighted = attend_local(query_heads, key_heads, value_heads, score_scale)
    top_peak = lax.pmax(row_peak, "ca")
    factor = jnp.exp(row_peak - top_peak)
    own_totals = lax.psum_scatter(row_total * factor, "ca", scatter_dimension=1, tiled=True)
    numerator = (weighted * factor[..., None]).astype(jnp.bfloat16)
    own_numerator = lax.psum_scatter(numerator, "ca", scatter_dimension=1, tiled=True)
    attended = (own_numerator.astype(jnp.float32) / own_totals[..., None]).astype(jnp.bfloat16)
    attended = attended.transpose(1, 0, 2).reshape(block_rows, own_heads * HD)
    return lax.psum_scatter(
        jnp.dot(attended, out_weight, preferred_element_type=jnp.float32).astype(jnp.bfloat16),
        "tp",
        scatter_dimension=0,
        tiled=True,
    )


def solution(mesh):
    ctx_count, tp_count = mesh.devices.shape
    split_mesh = Mesh(
        mesh.devices.reshape(ctx_count // KEY_SPLIT, KEY_SPLIT, tp_count), ("ca", "cz", "tp")
    )
    rows = P(("ca", "cz", "tp"), None)
    return jax.shard_map(
        local,
        mesh=split_mesh,
        in_specs=(rows, rows, rows, P("tp", None)),
        out_specs=rows,
        check_vma=False,
    )
```

```python
import math

import jax
import jax.numpy as jnp
from jax import lax
from jax.sharding import Mesh
from jax.sharding import PartitionSpec as P

HD = 128
KEY_SPLIT = 8


def attend_local(query_heads, key_heads, value_heads, score_scale):
    scores = (
        jnp.einsum("hid,hjd->hij", query_heads, key_heads, preferred_element_type=jnp.float32)
        * score_scale
    )
    row_peak = jnp.max(scores, axis=-1)
    weights_low = jnp.exp(scores - row_peak[..., None]).astype(jnp.bfloat16)
    row_total = jnp.sum(weights_low.astype(jnp.float32), axis=-1)
    weighted = jnp.einsum(
        "hij,hjd->hid", weights_low, value_heads, preferred_element_type=jnp.float32
    )
    return row_peak, row_total, weighted


def gather_by_exchange(block, axis_name):
    count = lax.axis_size(axis_name)
    spread = jnp.broadcast_to(block[None], (count,) + block.shape)
    return lax.all_to_all(spread, axis_name, 0, 0, tiled=True)


def local(query_vectors, key_vectors, value_vectors, out_weight):
    score_scale = 1.0 / math.sqrt(HD)
    tp_count = lax.axis_size("tp")
    ca_count = lax.axis_size("ca")
    token_rows = query_vectors.shape[0]
    own_heads = query_vectors.shape[1] // HD // tp_count
    own_cols = own_heads * HD

    qkv = jnp.stack([query_vectors, key_vectors, value_vectors], axis=1)
    qkv = qkv.reshape(token_rows, 3, tp_count, own_cols)
    block = lax.all_to_all(qkv, "tp", 2, 0, tiled=True)
    block_rows = block.shape[0]
    block = block.reshape(block_rows, 3, own_heads, HD).transpose(1, 2, 0, 3)

    query_heads = gather_by_exchange(block[0], "ca")
    query_heads = query_heads.transpose(1, 0, 2, 3).reshape(own_heads, ca_count * block_rows, HD)
    kv = gather_by_exchange(block[1:], "cz")
    kv = kv.transpose(1, 2, 0, 3, 4).reshape(2, own_heads, -1, HD)

    row_peak, row_total, weighted = attend_local(query_heads, kv[0], kv[1], score_scale)
    stats = jnp.stack([row_peak, row_total], axis=0).reshape(2, own_heads, ca_count, block_rows)
    stats = lax.all_to_all(stats.transpose(2, 0, 1, 3), "ca", 0, 0, tiled=True)
    parts = weighted.astype(jnp.bfloat16).reshape(own_heads, ca_count, block_rows, HD)
    parts = lax.all_to_all(parts.transpose(1, 0, 2, 3), "ca", 0, 0, tiled=True)
    top_peak = jnp.max(stats[:, 0], axis=0)
    factor = jnp.exp(stats[:, 0] - top_peak[None])
    totals = jnp.sum(stats[:, 1] * factor, axis=0)
    numerator = jnp.sum(parts.astype(jnp.float32) * factor[..., None], axis=0)
    attended = (numerator / totals[..., None]).astype(jnp.bfloat16)
    attended = attended.transpose(1, 0, 2).reshape(block_rows, own_cols)

    partial = jnp.dot(attended, out_weight, preferred_element_type=jnp.float32).astype(jnp.bfloat16)
    partial = partial.reshape(tp_count, block_rows // tp_count, -1)
    partial = lax.all_to_all(partial, "tp", 0, 0, tiled=True)
    return jnp.sum(partial.astype(jnp.float32), axis=0).astype(jnp.bfloat16)


def solution(mesh):
    ctx_count, tp_count = mesh.devices.shape
    split_mesh = Mesh(
        mesh.devices.reshape(ctx_count // KEY_SPLIT, KEY_SPLIT, tp_count), ("ca", "cz", "tp")
    )
    rows = P(("ca", "cz", "tp"), None)
    return jax.shard_map(
        local,
        mesh=split_mesh,
        in_specs=(rows, rows, rows, P("tp", None)),
        out_specs=rows,
        check_vma=False,
    )
```

```python
import functools
import math

import jax
import jax.numpy as jnp
from jax import lax
from jax.sharding import Mesh
from jax.sharding import PartitionSpec as P
from jax.experimental import pallas as pl
from jax.experimental.pallas import tpu as pltpu

HD = 128
KEY_SPLIT = 8


def attend_local(query_heads, key_heads, value_heads, score_scale):
    scores = (
        jnp.einsum("hid,hjd->hij", query_heads, key_heads, preferred_element_type=jnp.float32)
        * score_scale
    )
    row_peak = jnp.max(scores, axis=-1)
    weights_low = jnp.exp(scores - row_peak[..., None]).astype(jnp.bfloat16)
    row_total = jnp.sum(weights_low.astype(jnp.float32), axis=-1)
    weighted = jnp.einsum(
        "hij,hjd->hid", weights_low, value_heads, preferred_element_type=jnp.float32
    )
    return row_peak, row_total, weighted


def gather_by_exchange(block, axis_name):
    count = lax.axis_size(axis_name)
    spread = jnp.broadcast_to(block[None], (count,) + block.shape)
    return lax.all_to_all(spread, axis_name, 0, 0, tiled=True)


def exchange_kernel(na, nz, q_ref, kv_ref, q_out, kv_out, q_send, q_recv, r_send, r_recv,
                    l_send, l_recv, own_sem):
    mesh_ids = pl.DeviceIdType.MESH
    a = lax.axis_index("ca")
    z = lax.axis_index("cz")
    t = lax.axis_index("tp")
    right = lax.rem(z + 1, nz)
    left = lax.rem(z + nz - 1, nz)

    barrier = pltpu.get_barrier_semaphore()
    for off in range(1, na):
        pl.semaphore_signal(barrier, inc=1, device_id=(lax.rem(a + off, na), z, t),
                            device_id_type=mesh_ids)
    for side in (left, right):
        pl.semaphore_signal(barrier, inc=1, device_id=(a, side, t), device_id_type=mesh_ids)
    pl.semaphore_wait(barrier, na - 1 + 2)

    own = [
        pltpu.make_async_copy(q_ref, q_out.at[a], own_sem.at[0]),
        pltpu.make_async_copy(kv_ref, kv_out.at[z], own_sem.at[1]),
    ]
    for copy in own:
        copy.start()
    q_copies = []
    for off in range(1, na):
        copy = pltpu.make_async_remote_copy(
            src_ref=q_ref, dst_ref=q_out.at[a], send_sem=q_send.at[off - 1],
            recv_sem=q_recv.at[off - 1], device_id=(lax.rem(a + off, na), z, t),
            device_id_type=mesh_ids)
        copy.start()
        q_copies.append(copy)

    n_right = nz // 2
    n_left = (nz - 1) // 2
    right_copies = []
    left_copies = []
    for step in range(max(n_right, n_left)):
        if step < n_right:
            slot = lax.rem(z - step + nz, nz)
            if step > 0:
                right_copies[step - 1].wait_recv()
            copy = pltpu.make_async_remote_copy(
                src_ref=kv_ref if step == 0 else kv_out.at[slot], dst_ref=kv_out.at[slot],
                send_sem=r_send.at[step], recv_sem=r_recv.at[step], device_id=(a, right, t),
                device_id_type=mesh_ids)
            copy.start()
            right_copies.append(copy)
        if step < n_left:
            slot = lax.rem(z + step, nz)
            if step > 0:
                left_copies[step - 1].wait_recv()
            copy = pltpu.make_async_remote_copy(
                src_ref=kv_ref if step == 0 else kv_out.at[slot], dst_ref=kv_out.at[slot],
                send_sem=l_send.at[step], recv_sem=l_recv.at[step], device_id=(a, left, t),
                device_id_type=mesh_ids)
            copy.start()
            left_copies.append(copy)
    right_copies[-1].wait_recv()
    left_copies[-1].wait_recv()
    for copy in right_copies + left_copies:
        copy.wait_send()
    for copy in q_copies:
        copy.wait()
    for copy in own:
        copy.wait()


def exchange(q_blk, kv_blk, na, nz):
    n_right = nz // 2
    n_left = (nz - 1) // 2
    return pl.pallas_call(
        functools.partial(exchange_kernel, na, nz),
        out_shape=(
            jax.ShapeDtypeStruct((na,) + q_blk.shape, q_blk.dtype),
            jax.ShapeDtypeStruct((nz,) + kv_blk.shape, kv_blk.dtype),
        ),
        in_specs=[pl.BlockSpec(memory_space=pl.ANY)] * 2,
        out_specs=(pl.BlockSpec(memory_space=pl.ANY), pl.BlockSpec(memory_space=pl.ANY)),
        scratch_shapes=[
            pltpu.SemaphoreType.DMA((na - 1,)),
            pltpu.SemaphoreType.DMA((na - 1,)),
            pltpu.SemaphoreType.DMA((n_right,)),
            pltpu.SemaphoreType.DMA((n_right,)),
            pltpu.SemaphoreType.DMA((n_left,)),
            pltpu.SemaphoreType.DMA((n_left,)),
            pltpu.SemaphoreType.DMA((2,)),
        ],
        compiler_params=pltpu.CompilerParams(collective_id=0, has_side_effects=True),
    )(q_blk, kv_blk)


def local(query_vectors, key_vectors, value_vectors, out_weight):
    score_scale = 1.0 / math.sqrt(HD)
    tp_count = lax.axis_size("tp")
    ca_count = lax.axis_size("ca")
    token_rows = query_vectors.shape[0]
    own_heads = query_vectors.shape[1] // HD // tp_count
    own_cols = own_heads * HD

    qkv = jnp.stack([query_vectors, key_vectors, value_vectors], axis=1)
    qkv = qkv.reshape(token_rows, 3, tp_count, own_cols)
    block = lax.all_to_all(qkv, "tp", 2, 0, tiled=True)
    block_rows = block.shape[0]
    block = block.reshape(block_rows, 3, own_heads, HD).transpose(1, 2, 0, 3)

    query_heads, kv = exchange(block[0], block[1:], ca_count, lax.axis_size("cz"))
    query_heads = query_heads.transpose(1, 0, 2, 3).reshape(own_heads, ca_count * block_rows, HD)
    kv = kv.transpose(1, 2, 0, 3, 4).reshape(2, own_heads, -1, HD)

    row_peak, row_total, weighted = attend_local(query_heads, kv[0], kv[1], score_scale)
    stats = jnp.stack([row_peak, row_total], axis=0).reshape(2, own_heads, ca_count, block_rows)
    stats = lax.all_to_all(stats.transpose(2, 0, 1, 3), "ca", 0, 0, tiled=True)
    parts = weighted.astype(jnp.bfloat16).reshape(own_heads, ca_count, block_rows, HD)
    parts = lax.all_to_all(parts.transpose(1, 0, 2, 3), "ca", 0, 0, tiled=True)
    top_peak = jnp.max(stats[:, 0], axis=0)
    factor = jnp.exp(stats[:, 0] - top_peak[None])
    totals = jnp.sum(stats[:, 1] * factor, axis=0)
    numerator = jnp.sum(parts.astype(jnp.float32) * factor[..., None], axis=0)
    attended = (numerator / totals[..., None]).astype(jnp.bfloat16)
    attended = attended.transpose(1, 0, 2).reshape(block_rows, own_cols)

    partial = jnp.dot(attended, out_weight, preferred_element_type=jnp.float32).astype(jnp.bfloat16)
    partial = partial.reshape(tp_count, block_rows // tp_count, -1)
    partial = lax.all_to_all(partial, "tp", 0, 0, tiled=True)
    return jnp.sum(partial.astype(jnp.float32), axis=0).astype(jnp.bfloat16)


def solution(mesh):
    ctx_count, tp_count = mesh.devices.shape
    split_mesh = Mesh(
        mesh.devices.reshape(ctx_count // KEY_SPLIT, KEY_SPLIT, tp_count), ("ca", "cz", "tp")
    )
    rows = P(("ca", "cz", "tp"), None)
    return jax.shard_map(
        local,
        mesh=split_mesh,
        in_specs=(rows, rows, rows, P("tp", None)),
        out_specs=rows,
        check_vma=False,
    )
```

```python
import functools
import math

import jax
import jax.numpy as jnp
from jax import lax
from jax.sharding import Mesh
from jax.sharding import PartitionSpec as P
from jax.experimental import pallas as pl
from jax.experimental.pallas import tpu as pltpu

HD = 128
KEY_SPLIT = 8


def attend_local(query_heads, key_heads, value_heads, score_scale):
    scores = (
        jnp.einsum("hid,hjd->hij", query_heads, key_heads, preferred_element_type=jnp.float32)
        * score_scale
    )
    row_peak = jnp.max(scores, axis=-1)
    weights_low = jnp.exp(scores - row_peak[..., None]).astype(jnp.bfloat16)
    row_total = jnp.sum(weights_low.astype(jnp.float32), axis=-1)
    weighted = jnp.einsum(
        "hij,hjd->hid", weights_low, value_heads, preferred_element_type=jnp.float32
    )
    return row_peak, row_total, weighted


def gather_by_exchange(block, axis_name):
    count = lax.axis_size(axis_name)
    spread = jnp.broadcast_to(block[None], (count,) + block.shape)
    return lax.all_to_all(spread, axis_name, 0, 0, tiled=True)


def exchange_kernel(na, nz, q_ref, kv_ref, q_out, kv_out, q_send, q_recv, r_send, r_recv,
                    l_send, l_recv, own_sem):
    mesh_ids = pl.DeviceIdType.MESH
    a = lax.axis_index("ca")
    z = lax.axis_index("cz")
    t = lax.axis_index("tp")
    right = lax.rem(z + 1, nz)
    left = lax.rem(z + nz - 1, nz)

    barrier = pltpu.get_barrier_semaphore()
    for off in range(1, na):
        pl.semaphore_signal(barrier, inc=1, device_id=(lax.rem(a + off, na), z, t),
                            device_id_type=mesh_ids)
    for side in (left, right):
        pl.semaphore_signal(barrier, inc=1, device_id=(a, side, t), device_id_type=mesh_ids)
    pl.semaphore_wait(barrier, na - 1 + 2)

    own = [
        pltpu.make_async_copy(q_ref, q_out.at[a], own_sem.at[0]),
        pltpu.make_async_copy(kv_ref, kv_out.at[z], own_sem.at[1]),
    ]
    for copy in own:
        copy.start()
    q_copies = []
    for off in range(1, na):
        copy = pltpu.make_async_remote_copy(
            src_ref=q_ref, dst_ref=q_out.at[a], send_sem=q_send.at[off - 1],
            recv_sem=q_recv.at[off - 1], device_id=(lax.rem(a + off, na), z, t),
            device_id_type=mesh_ids)
        copy.start()
        q_copies.append(copy)

    n_right = nz // 2
    n_left = (nz - 1) // 2
    right_copies = []
    left_copies = []
    for step in range(max(n_right, n_left)):
        if step < n_right:
            slot = lax.rem(z - step + nz, nz)
            if step > 0:
                right_copies[step - 1].wait_recv()
            copy = pltpu.make_async_remote_copy(
                src_ref=kv_ref if step == 0 else kv_out.at[slot], dst_ref=kv_out.at[slot],
                send_sem=r_send.at[step], recv_sem=r_recv.at[step], device_id=(a, right, t),
                device_id_type=mesh_ids)
            copy.start()
            right_copies.append(copy)
        if step < n_left:
            slot = lax.rem(z + step, nz)
            if step > 0:
                left_copies[step - 1].wait_recv()
            copy = pltpu.make_async_remote_copy(
                src_ref=kv_ref if step == 0 else kv_out.at[slot], dst_ref=kv_out.at[slot],
                send_sem=l_send.at[step], recv_sem=l_recv.at[step], device_id=(a, left, t),
                device_id_type=mesh_ids)
            copy.start()
            left_copies.append(copy)
    right_copies[-1].wait_recv()
    left_copies[-1].wait_recv()
    for copy in right_copies + left_copies:
        copy.wait_send()
    for copy in q_copies:
        copy.wait()
    for copy in own:
        copy.wait()


def exchange(q_blk, kv_blk, na, nz):
    n_right = nz // 2
    n_left = (nz - 1) // 2
    return pl.pallas_call(
        functools.partial(exchange_kernel, na, nz),
        out_shape=(
            jax.ShapeDtypeStruct((na,) + q_blk.shape, q_blk.dtype),
            jax.ShapeDtypeStruct((nz,) + kv_blk.shape, kv_blk.dtype),
        ),
        in_specs=[pl.BlockSpec(memory_space=pl.ANY)] * 2,
        out_specs=(pl.BlockSpec(memory_space=pl.ANY), pl.BlockSpec(memory_space=pl.ANY)),
        scratch_shapes=[
            pltpu.SemaphoreType.DMA((na - 1,)),
            pltpu.SemaphoreType.DMA((na - 1,)),
            pltpu.SemaphoreType.DMA((n_right,)),
            pltpu.SemaphoreType.DMA((n_right,)),
            pltpu.SemaphoreType.DMA((n_left,)),
            pltpu.SemaphoreType.DMA((n_left,)),
            pltpu.SemaphoreType.DMA((2,)),
        ],
        compiler_params=pltpu.CompilerParams(collective_id=0, has_side_effects=True),
    )(q_blk, kv_blk)


def project_kernel(n_hi, att_ref, w_ref, out_ref, send1, recv1, total, send2, recv2, sems1,
                   send_sems2, recv_sems2):
    mesh_ids = pl.DeviceIdType.MESH
    a = lax.axis_index("ca")
    z = lax.axis_index("cz")
    t = lax.axis_index("tp")
    core = lax.rem(t, 2)
    hi = t // 2
    partner = (a, z, hi * 2 + 1 - core)
    rows = send2.shape[1]

    barrier = pltpu.get_barrier_semaphore()
    pl.semaphore_signal(barrier, inc=1, device_id=partner, device_id_type=mesh_ids)
    for off in range(1, n_hi):
        pl.semaphore_signal(barrier, inc=1, device_id=(a, z, lax.rem(hi + off, n_hi) * 2 + core),
                            device_id_type=mesh_ids)
    pl.semaphore_wait(barrier, n_hi)

    send1[...] = jnp.dot(
        att_ref[1 - core], w_ref[...], preferred_element_type=jnp.float32
    ).astype(jnp.bfloat16)
    first = pltpu.make_async_remote_copy(
        src_ref=send1, dst_ref=recv1, send_sem=sems1.at[0], recv_sem=sems1.at[1],
        device_id=partner, device_id_type=mesh_ids)
    first.start()
    total[...] = jnp.dot(
        att_ref[core], w_ref[...], preferred_element_type=jnp.float32
    ).astype(jnp.bfloat16).astype(jnp.float32)
    first.wait()
    total[...] = total[...] + recv1[...].astype(jnp.float32)
    for j in range(n_hi):
        send2[j] = total[pl.ds(j * rows, rows), :].astype(jnp.bfloat16)
    second = []
    for off in range(1, n_hi):
        dest = lax.rem(hi + off, n_hi)
        copy = pltpu.make_async_remote_copy(
            src_ref=send2.at[dest], dst_ref=recv2.at[off - 1], send_sem=send_sems2.at[off - 1],
            recv_sem=recv_sems2.at[off - 1], device_id=(a, z, dest * 2 + core),
            device_id_type=mesh_ids)
        copy.start()
        second.append(copy)
    own = total[pl.ds(pl.multiple_of(hi * rows, rows), rows), :]
    for copy in second:
        copy.wait()
    for off in range(1, n_hi):
        own = own + recv2[off - 1].astype(jnp.float32)
    out_ref[...] = own.astype(out_ref.dtype)


def project(attended, out_weight, tp_count):
    n_hi = tp_count // 2
    block_rows, width = attended.shape
    rows = block_rows // tp_count
    by_core = attended.reshape(n_hi, 2, rows, width).transpose(1, 0, 2, 3)
    by_core = by_core.reshape(2, n_hi * rows, width)
    cols = out_weight.shape[1]
    vmem = pl.BlockSpec(memory_space=pltpu.VMEM)
    return pl.pallas_call(
        functools.partial(project_kernel, n_hi),
        out_shape=jax.ShapeDtypeStruct((rows, cols), jnp.bfloat16),
        in_specs=[vmem, vmem],
        out_specs=vmem,
        scratch_shapes=[
            pltpu.VMEM((n_hi * rows, cols), jnp.bfloat16),
            pltpu.VMEM((n_hi * rows, cols), jnp.bfloat16),
            pltpu.VMEM((n_hi * rows, cols), jnp.float32),
            pltpu.VMEM((n_hi, rows, cols), jnp.bfloat16),
            pltpu.VMEM((n_hi - 1, rows, cols), jnp.bfloat16),
            pltpu.SemaphoreType.DMA((2,)),
            pltpu.SemaphoreType.DMA((n_hi - 1,)),
            pltpu.SemaphoreType.DMA((n_hi - 1,)),
        ],
        compiler_params=pltpu.CompilerParams(collective_id=1, has_side_effects=True),
    )(by_core, out_weight)


def local(query_vectors, key_vectors, value_vectors, out_weight):
    score_scale = 1.0 / math.sqrt(HD)
    tp_count = lax.axis_size("tp")
    ca_count = lax.axis_size("ca")
    token_rows = query_vectors.shape[0]
    own_heads = query_vectors.shape[1] // HD // tp_count
    own_cols = own_heads * HD

    qkv = jnp.stack([query_vectors, key_vectors, value_vectors], axis=1)
    qkv = qkv.reshape(token_rows, 3, tp_count, own_cols)
    block = lax.all_to_all(qkv, "tp", 2, 0, tiled=True)
    block_rows = block.shape[0]
    block = block.reshape(block_rows, 3, own_heads, HD).transpose(1, 2, 0, 3)

    query_heads, kv = exchange(block[0], block[1:], ca_count, lax.axis_size("cz"))
    query_heads = query_heads.transpose(1, 0, 2, 3).reshape(own_heads, ca_count * block_rows, HD)
    kv = kv.transpose(1, 2, 0, 3, 4).reshape(2, own_heads, -1, HD)

    row_peak, row_total, weighted = attend_local(query_heads, kv[0], kv[1], score_scale)
    stats = jnp.stack([row_peak, row_total], axis=0).reshape(2, own_heads, ca_count, block_rows)
    stats = lax.all_to_all(stats.transpose(2, 0, 1, 3), "ca", 0, 0, tiled=True)
    parts = weighted.astype(jnp.bfloat16).reshape(own_heads, ca_count, block_rows, HD)
    parts = lax.all_to_all(parts.transpose(1, 0, 2, 3), "ca", 0, 0, tiled=True)
    top_peak = jnp.max(stats[:, 0], axis=0)
    factor = jnp.exp(stats[:, 0] - top_peak[None])
    totals = jnp.sum(stats[:, 1] * factor, axis=0)
    numerator = jnp.sum(parts.astype(jnp.float32) * factor[..., None], axis=0)
    attended = (numerator / totals[..., None]).astype(jnp.bfloat16)
    attended = attended.transpose(1, 0, 2).reshape(block_rows, own_cols)

    return project(attended, out_weight, tp_count)


def solution(mesh):
    ctx_count, tp_count = mesh.devices.shape
    split_mesh = Mesh(
        mesh.devices.reshape(ctx_count // KEY_SPLIT, KEY_SPLIT, tp_count), ("ca", "cz", "tp")
    )
    rows = P(("ca", "cz", "tp"), None)
    return jax.shard_map(
        local,
        mesh=split_mesh,
        in_specs=(rows, rows, rows, P("tp", None)),
        out_specs=rows,
        check_vma=False,
    )
```

```python
import functools
import math

import jax
import jax.numpy as jnp
from jax import lax
from jax.sharding import Mesh
from jax.sharding import PartitionSpec as P
from jax.experimental import pallas as pl
from jax.experimental.pallas import tpu as pltpu

HD = 128
KEY_SPLIT = 8


def attend_local(query_heads, key_heads, value_heads, score_scale):
    scores = (
        jnp.einsum("hid,hjd->hij", query_heads, key_heads, preferred_element_type=jnp.float32)
        * score_scale
    )
    row_peak = jnp.max(scores, axis=-1)
    weights_low = jnp.exp(scores - row_peak[..., None]).astype(jnp.bfloat16)
    row_total = jnp.sum(weights_low.astype(jnp.float32), axis=-1)
    weighted = jnp.einsum(
        "hij,hjd->hid", weights_low, value_heads, preferred_element_type=jnp.float32
    )
    return row_peak, row_total, weighted


def gather_by_exchange(block, axis_name):
    count = lax.axis_size(axis_name)
    spread = jnp.broadcast_to(block[None], (count,) + block.shape)
    return lax.all_to_all(spread, axis_name, 0, 0, tiled=True)


def exchange_kernel(na, nz, q_ref, kv_ref, q_out, kv_out, q_send, q_recv, r_send, r_recv,
                    l_send, l_recv, own_sem):
    mesh_ids = pl.DeviceIdType.MESH
    a = lax.axis_index("ca")
    z = lax.axis_index("cz")
    t = lax.axis_index("tp")
    right = lax.rem(z + 1, nz)
    left = lax.rem(z + nz - 1, nz)

    barrier = pltpu.get_barrier_semaphore()
    for off in range(1, na):
        pl.semaphore_signal(barrier, inc=1, device_id=(lax.rem(a + off, na), z, t),
                            device_id_type=mesh_ids)
    for side in (left, right):
        pl.semaphore_signal(barrier, inc=1, device_id=(a, side, t), device_id_type=mesh_ids)
    pl.semaphore_wait(barrier, na - 1 + 2)

    own = [
        pltpu.make_async_copy(q_ref, q_out.at[a], own_sem.at[0]),
        pltpu.make_async_copy(kv_ref, kv_out.at[z], own_sem.at[1]),
    ]
    for copy in own:
        copy.start()
    q_copies = []
    for off in range(1, na):
        copy = pltpu.make_async_remote_copy(
            src_ref=q_ref, dst_ref=q_out.at[a], send_sem=q_send.at[off - 1],
            recv_sem=q_recv.at[off - 1], device_id=(lax.rem(a + off, na), z, t),
            device_id_type=mesh_ids)
        copy.start()
        q_copies.append(copy)

    n_right = nz // 2
    n_left = (nz - 1) // 2
    right_copies = []
    left_copies = []
    for step in range(max(n_right, n_left)):
        if step < n_right:
            slot = lax.rem(z - step + nz, nz)
            if step > 0:
                right_copies[step - 1].wait_recv()
            copy = pltpu.make_async_remote_copy(
                src_ref=kv_ref if step == 0 else kv_out.at[slot], dst_ref=kv_out.at[slot],
                send_sem=r_send.at[step], recv_sem=r_recv.at[step], device_id=(a, right, t),
                device_id_type=mesh_ids)
            copy.start()
            right_copies.append(copy)
        if step < n_left:
            slot = lax.rem(z + step, nz)
            if step > 0:
                left_copies[step - 1].wait_recv()
            copy = pltpu.make_async_remote_copy(
                src_ref=kv_ref if step == 0 else kv_out.at[slot], dst_ref=kv_out.at[slot],
                send_sem=l_send.at[step], recv_sem=l_recv.at[step], device_id=(a, left, t),
                device_id_type=mesh_ids)
            copy.start()
            left_copies.append(copy)
    right_copies[-1].wait_recv()
    left_copies[-1].wait_recv()
    for copy in right_copies + left_copies:
        copy.wait_send()
    for copy in q_copies:
        copy.wait()
    for copy in own:
        copy.wait()


def exchange(q_blk, kv_blk, na, nz):
    n_right = nz // 2
    n_left = (nz - 1) // 2
    return pl.pallas_call(
        functools.partial(exchange_kernel, na, nz),
        out_shape=(
            jax.ShapeDtypeStruct((na,) + q_blk.shape, q_blk.dtype),
            jax.ShapeDtypeStruct((nz,) + kv_blk.shape, kv_blk.dtype),
        ),
        in_specs=[pl.BlockSpec(memory_space=pl.ANY)] * 2,
        out_specs=(pl.BlockSpec(memory_space=pl.ANY), pl.BlockSpec(memory_space=pl.ANY)),
        scratch_shapes=[
            pltpu.SemaphoreType.DMA((na - 1,)),
            pltpu.SemaphoreType.DMA((na - 1,)),
            pltpu.SemaphoreType.DMA((n_right,)),
            pltpu.SemaphoreType.DMA((n_right,)),
            pltpu.SemaphoreType.DMA((n_left,)),
            pltpu.SemaphoreType.DMA((n_left,)),
            pltpu.SemaphoreType.DMA((2,)),
        ],
        compiler_params=pltpu.CompilerParams(collective_id=0, has_side_effects=True),
    )(q_blk, kv_blk)


def project_kernel(na, n_hi, parts_ref, stats_ref, w_ref, out_ref, got_parts, got_stats, full,
                   send1, recv1, total, send2, recv2, part_sems, stat_sems, sems1, send_sems2,
                   recv_sems2):
    mesh_ids = pl.DeviceIdType.MESH
    a = lax.axis_index("ca")
    z = lax.axis_index("cz")
    t = lax.axis_index("tp")
    core = lax.rem(t, 2)
    hi = t // 2
    partner = (a, z, hi * 2 + 1 - core)
    rows = send2.shape[1]
    heads = parts_ref.shape[1]

    barrier = pltpu.get_barrier_semaphore()
    for off in range(1, na):
        pl.semaphore_signal(barrier, inc=1, device_id=(lax.rem(a + off, na), z, t),
                            device_id_type=mesh_ids)
    pl.semaphore_signal(barrier, inc=1, device_id=partner, device_id_type=mesh_ids)
    for off in range(1, n_hi):
        pl.semaphore_signal(barrier, inc=1, device_id=(a, z, lax.rem(hi + off, n_hi) * 2 + core),
                            device_id_type=mesh_ids)
    pl.semaphore_wait(barrier, na - 1 + n_hi)

    gathered = []
    for off in range(1, na):
        dest = lax.rem(a + off, na)
        for src, dst, sems in ((parts_ref, got_parts, part_sems), (stats_ref, got_stats, stat_sems)):
            copy = pltpu.make_async_remote_copy(
                src_ref=src.at[dest], dst_ref=dst.at[off - 1], send_sem=sems.at[0, off - 1],
                recv_sem=sems.at[1, off - 1], device_id=(dest, z, t), device_id_type=mesh_ids)
            copy.start()
            gathered.append(copy)
    for copy in gathered:
        copy.wait()

    peaks = [stats_ref[a, 0]] + [got_stats[off - 1, 0] for off in range(1, na)]
    sums = [stats_ref[a, 1]] + [got_stats[off - 1, 1] for off in range(1, na)]
    top = peaks[0]
    for peak in peaks[1:]:
        top = jnp.maximum(top, peak)
    factors = [jnp.exp(peak - top) for peak in peaks]
    totals = factors[0] * sums[0]
    for factor, part_sum in zip(factors[1:], sums[1:]):
        totals = totals + factor * part_sum
    for h in range(heads):
        numerator = parts_ref[a, h].astype(jnp.float32) * factors[0][h][:, None]
        for off in range(1, na):
            numerator = numerator + (
                got_parts[off - 1, h].astype(jnp.float32) * factors[off][h][:, None]
            )
        attended = (numerator / totals[h][:, None]).astype(jnp.bfloat16)
        product = jnp.dot(attended, w_ref[pl.ds(h * HD, HD), :], preferred_element_type=jnp.float32)
        if h == 0:
            full[...] = product
        else:
            full[...] = full[...] + product

    for j in range(n_hi):
        their = pl.multiple_of((j * 2 + 1 - core) * rows, rows)
        mine = pl.multiple_of((j * 2 + core) * rows, rows)
        send1[j] = full[pl.ds(their, rows), :].astype(jnp.bfloat16)
        total[j] = full[pl.ds(mine, rows), :].astype(jnp.bfloat16).astype(jnp.float32)
    first = pltpu.make_async_remote_copy(
        src_ref=send1, dst_ref=recv1, send_sem=sems1.at[0], recv_sem=sems1.at[1],
        device_id=partner, device_id_type=mesh_ids)
    first.start()
    first.wait()
    for j in range(n_hi):
        send2[j] = (total[j] + recv1[j].astype(jnp.float32)).astype(jnp.bfloat16)
    second = []
    for off in range(1, n_hi):
        dest = lax.rem(hi + off, n_hi)
        copy = pltpu.make_async_remote_copy(
            src_ref=send2.at[dest], dst_ref=recv2.at[off - 1], send_sem=send_sems2.at[off - 1],
            recv_sem=recv_sems2.at[off - 1], device_id=(a, z, dest * 2 + core),
            device_id_type=mesh_ids)
        copy.start()
        second.append(copy)
    own = total[hi] + recv1[hi].astype(jnp.float32)
    for copy in second:
        copy.wait()
    for off in range(1, n_hi):
        own = own + recv2[off - 1].astype(jnp.float32)
    out_ref[...] = own.astype(out_ref.dtype)


def project(parts, stats, out_weight, tp_count):
    na, heads, block_rows, _ = parts.shape
    n_hi = tp_count // 2
    rows = block_rows // tp_count
    cols = out_weight.shape[1]
    vmem = pl.BlockSpec(memory_space=pltpu.VMEM)
    return pl.pallas_call(
        functools.partial(project_kernel, na, n_hi),
        out_shape=jax.ShapeDtypeStruct((rows, cols), jnp.bfloat16),
        in_specs=[vmem, vmem, vmem],
        out_specs=vmem,
        scratch_shapes=[
            pltpu.VMEM((na - 1,) + parts.shape[1:], parts.dtype),
            pltpu.VMEM((na - 1,) + stats.shape[1:], stats.dtype),
            pltpu.VMEM((block_rows, cols), jnp.float32),
            pltpu.VMEM((n_hi, rows, cols), jnp.bfloat16),
            pltpu.VMEM((n_hi, rows, cols), jnp.bfloat16),
            pltpu.VMEM((n_hi, rows, cols), jnp.float32),
            pltpu.VMEM((n_hi, rows, cols), jnp.bfloat16),
            pltpu.VMEM((n_hi - 1, rows, cols), jnp.bfloat16),
            pltpu.SemaphoreType.DMA((2, na - 1)),
            pltpu.SemaphoreType.DMA((2, na - 1)),
            pltpu.SemaphoreType.DMA((2,)),
            pltpu.SemaphoreType.DMA((n_hi - 1,)),
            pltpu.SemaphoreType.DMA((n_hi - 1,)),
        ],
        compiler_params=pltpu.CompilerParams(collective_id=1, has_side_effects=True),
    )(parts, stats, out_weight)


def local(query_vectors, key_vectors, value_vectors, out_weight):
    score_scale = 1.0 / math.sqrt(HD)
    tp_count = lax.axis_size("tp")
    ca_count = lax.axis_size("ca")
    token_rows = query_vectors.shape[0]
    own_heads = query_vectors.shape[1] // HD // tp_count
    own_cols = own_heads * HD

    qkv = jnp.stack([query_vectors, key_vectors, value_vectors], axis=1)
    qkv = qkv.reshape(token_rows, 3, tp_count, own_cols)
    block = lax.all_to_all(qkv, "tp", 2, 0, tiled=True)
    block_rows = block.shape[0]
    block = block.reshape(block_rows, 3, own_heads, HD).transpose(1, 2, 0, 3)

    query_heads, kv = exchange(block[0], block[1:], ca_count, lax.axis_size("cz"))
    query_heads = query_heads.transpose(1, 0, 2, 3).reshape(own_heads, ca_count * block_rows, HD)
    kv = kv.transpose(1, 2, 0, 3, 4).reshape(2, own_heads, -1, HD)

    row_peak, row_total, weighted = attend_local(query_heads, kv[0], kv[1], score_scale)
    stats = jnp.stack([row_peak, row_total], axis=0).reshape(2, own_heads, ca_count, block_rows)
    parts = weighted.astype(jnp.bfloat16).reshape(own_heads, ca_count, block_rows, HD)
    return project(parts.transpose(1, 0, 2, 3), stats.transpose(2, 0, 1, 3), out_weight, tp_count)


def solution(mesh):
    ctx_count, tp_count = mesh.devices.shape
    split_mesh = Mesh(
        mesh.devices.reshape(ctx_count // KEY_SPLIT, KEY_SPLIT, tp_count), ("ca", "cz", "tp")
    )
    rows = P(("ca", "cz", "tp"), None)
    return jax.shard_map(
        local,
        mesh=split_mesh,
        in_specs=(rows, rows, rows, P("tp", None)),
        out_specs=rows,
        check_vma=False,
    )
```

```python
import functools
import math

import jax
import jax.numpy as jnp
from jax import lax
from jax.sharding import Mesh
from jax.sharding import PartitionSpec as P
from jax.experimental import pallas as pl
from jax.experimental.pallas import tpu as pltpu

HD = 128
KEY_SPLIT = 8


def attend_local(query_heads, key_heads, value_heads, score_scale):
    scores = (
        jnp.einsum("hid,hjd->hij", query_heads, key_heads, preferred_element_type=jnp.float32)
        * score_scale
    )
    row_peak = jnp.max(scores, axis=-1)
    weights_low = jnp.exp(scores - row_peak[..., None]).astype(jnp.bfloat16)
    row_total = jnp.sum(weights_low.astype(jnp.float32), axis=-1)
    weighted = jnp.einsum(
        "hij,hjd->hid", weights_low, value_heads, preferred_element_type=jnp.float32
    )
    return row_peak, row_total, weighted


def gather_by_exchange(block, axis_name):
    count = lax.axis_size(axis_name)
    spread = jnp.broadcast_to(block[None], (count,) + block.shape)
    return lax.all_to_all(spread, axis_name, 0, 0, tiled=True)


def exchange_kernel(na, nz, nt, staged, q_out, kv_out, tq_sems, tkv_sems, own_sems, q_sems,
                    r_sems, l_sems):
    mesh_ids = pl.DeviceIdType.MESH
    a = lax.axis_index("ca")
    z = lax.axis_index("cz")
    t = lax.axis_index("tp")
    right = lax.rem(z + 1, nz)
    left = lax.rem(z + nz - 1, nz)
    rows = staged.shape[3]

    barrier = pltpu.get_barrier_semaphore()
    for off in range(1, nt):
        pl.semaphore_signal(barrier, inc=1, device_id=(a, z, lax.rem(t + off, nt)),
                            device_id_type=mesh_ids)
    for off in range(1, na):
        pl.semaphore_signal(barrier, inc=1, device_id=(lax.rem(a + off, na), z, t),
                            device_id_type=mesh_ids)
    for side in (left, right):
        pl.semaphore_signal(barrier, inc=1, device_id=(a, side, t), device_id_type=mesh_ids)
    pl.semaphore_wait(barrier, nt - 1 + na - 1 + 2)

    mine = pl.ds(pl.multiple_of(t * rows, rows), rows)
    own = [
        pltpu.make_async_copy(staged.at[t, 0], q_out.at[a, :, mine], own_sems.at[0]),
        pltpu.make_async_copy(staged.at[t, pl.ds(1, 2)], kv_out.at[z, :, :, mine], own_sems.at[1]),
    ]
    for copy in own:
        copy.start()
    spread = []
    for off in range(1, nt):
        dest = lax.rem(t + off, nt)
        spread.append(pltpu.make_async_remote_copy(
            src_ref=staged.at[dest, 0], dst_ref=q_out.at[a, :, mine],
            send_sem=tq_sems.at[0, off - 1], recv_sem=tq_sems.at[1, off - 1],
            device_id=(a, z, dest), device_id_type=mesh_ids))
        spread.append(pltpu.make_async_remote_copy(
            src_ref=staged.at[dest, pl.ds(1, 2)], dst_ref=kv_out.at[z, :, :, mine],
            send_sem=tkv_sems.at[0, off - 1], recv_sem=tkv_sems.at[1, off - 1],
            device_id=(a, z, dest), device_id_type=mesh_ids))
    for copy in spread:
        copy.start()
    for copy in spread:
        copy.wait()
    for copy in own:
        copy.wait()

    q_copies = []
    for off in range(1, na):
        copy = pltpu.make_async_remote_copy(
            src_ref=q_out.at[a], dst_ref=q_out.at[a], send_sem=q_sems.at[0, off - 1],
            recv_sem=q_sems.at[1, off - 1], device_id=(lax.rem(a + off, na), z, t),
            device_id_type=mesh_ids)
        copy.start()
        q_copies.append(copy)

    n_right = nz // 2
    n_left = (nz - 1) // 2
    chains = ((right, n_right, r_sems, -1, []), (left, n_left, l_sems, 1, []))
    for step in range(n_right):
        for part in range(2):
            for side, count, sems, sign, copies in chains:
                if step >= count:
                    continue
                slot = lax.rem(z + sign * step + nz, nz)
                if step > 0:
                    copies[(step - 1) * 2 + part].wait_recv()
                copy = pltpu.make_async_remote_copy(
                    src_ref=kv_out.at[slot, part], dst_ref=kv_out.at[slot, part],
                    send_sem=sems.at[0, step * 2 + part], recv_sem=sems.at[1, step * 2 + part],
                    device_id=(a, side, t), device_id_type=mesh_ids)
                copy.start()
                copies.append(copy)
    for side, count, sems, sign, copies in chains:
        copies[-2].wait_recv()
        copies[-1].wait_recv()
        for copy in copies:
            copy.wait_send()
    for copy in q_copies:
        copy.wait()


def exchange(staged, na, nz):
    nt, _, heads, rows, width = staged.shape
    n_right = nz // 2
    n_left = (nz - 1) // 2
    return pl.pallas_call(
        functools.partial(exchange_kernel, na, nz, nt),
        out_shape=(
            jax.ShapeDtypeStruct((na, heads, nt * rows, width), staged.dtype),
            jax.ShapeDtypeStruct((nz, 2, heads, nt * rows, width), staged.dtype),
        ),
        in_specs=[pl.BlockSpec(memory_space=pl.ANY)],
        out_specs=(pl.BlockSpec(memory_space=pl.ANY), pl.BlockSpec(memory_space=pl.ANY)),
        scratch_shapes=[
            pltpu.SemaphoreType.DMA((2, nt - 1)),
            pltpu.SemaphoreType.DMA((2, nt - 1)),
            pltpu.SemaphoreType.DMA((2,)),
            pltpu.SemaphoreType.DMA((2, na - 1)),
            pltpu.SemaphoreType.DMA((2, 2 * n_right)),
            pltpu.SemaphoreType.DMA((2, 2 * n_left)),
        ],
        compiler_params=pltpu.CompilerParams(collective_id=0, has_side_effects=True),
    )(staged)


def project_kernel(na, n_hi, parts_ref, stats_ref, w_ref, out_ref, got_parts, got_stats, full,
                   send1, recv1, total, send2, recv2, part_sems, stat_sems, sems1, send_sems2,
                   recv_sems2):
    mesh_ids = pl.DeviceIdType.MESH
    a = lax.axis_index("ca")
    z = lax.axis_index("cz")
    t = lax.axis_index("tp")
    core = lax.rem(t, 2)
    hi = t // 2
    partner = (a, z, hi * 2 + 1 - core)
    rows = send2.shape[1]
    heads = parts_ref.shape[1]

    barrier = pltpu.get_barrier_semaphore()
    for off in range(1, na):
        pl.semaphore_signal(barrier, inc=1, device_id=(lax.rem(a + off, na), z, t),
                            device_id_type=mesh_ids)
    pl.semaphore_signal(barrier, inc=1, device_id=partner, device_id_type=mesh_ids)
    for off in range(1, n_hi):
        pl.semaphore_signal(barrier, inc=1, device_id=(a, z, lax.rem(hi + off, n_hi) * 2 + core),
                            device_id_type=mesh_ids)
    pl.semaphore_wait(barrier, na - 1 + n_hi)

    gathered = []
    for off in range(1, na):
        dest = lax.rem(a + off, na)
        for src, dst, sems in ((parts_ref, got_parts, part_sems), (stats_ref, got_stats, stat_sems)):
            copy = pltpu.make_async_remote_copy(
                src_ref=src.at[dest], dst_ref=dst.at[off - 1], send_sem=sems.at[0, off - 1],
                recv_sem=sems.at[1, off - 1], device_id=(dest, z, t), device_id_type=mesh_ids)
            copy.start()
            gathered.append(copy)
    for copy in gathered:
        copy.wait()

    peaks = [stats_ref[a, 0]] + [got_stats[off - 1, 0] for off in range(1, na)]
    sums = [stats_ref[a, 1]] + [got_stats[off - 1, 1] for off in range(1, na)]
    top = peaks[0]
    for peak in peaks[1:]:
        top = jnp.maximum(top, peak)
    factors = [jnp.exp(peak - top) for peak in peaks]
    totals = factors[0] * sums[0]
    for factor, part_sum in zip(factors[1:], sums[1:]):
        totals = totals + factor * part_sum
    for h in range(heads):
        numerator = parts_ref[a, h].astype(jnp.float32) * factors[0][h][:, None]
        for off in range(1, na):
            numerator = numerator + (
                got_parts[off - 1, h].astype(jnp.float32) * factors[off][h][:, None]
            )
        attended = (numerator / totals[h][:, None]).astype(jnp.bfloat16)
        product = jnp.dot(attended, w_ref[pl.ds(h * HD, HD), :], preferred_element_type=jnp.float32)
        if h == 0:
            full[...] = product
        else:
            full[...] = full[...] + product

    for j in range(n_hi):
        their = pl.multiple_of((j * 2 + 1 - core) * rows, rows)
        mine = pl.multiple_of((j * 2 + core) * rows, rows)
        send1[j] = full[pl.ds(their, rows), :].astype(jnp.bfloat16)
        total[j] = full[pl.ds(mine, rows), :].astype(jnp.bfloat16).astype(jnp.float32)
    first = pltpu.make_async_remote_copy(
        src_ref=send1, dst_ref=recv1, send_sem=sems1.at[0], recv_sem=sems1.at[1],
        device_id=partner, device_id_type=mesh_ids)
    first.start()
    first.wait()
    for j in range(n_hi):
        send2[j] = (total[j] + recv1[j].astype(jnp.float32)).astype(jnp.bfloat16)
    second = []
    for off in range(1, n_hi):
        dest = lax.rem(hi + off, n_hi)
        copy = pltpu.make_async_remote_copy(
            src_ref=send2.at[dest], dst_ref=recv2.at[off - 1], send_sem=send_sems2.at[off - 1],
            recv_sem=recv_sems2.at[off - 1], device_id=(a, z, dest * 2 + core),
            device_id_type=mesh_ids)
        copy.start()
        second.append(copy)
    own = total[hi] + recv1[hi].astype(jnp.float32)
    for copy in second:
        copy.wait()
    for off in range(1, n_hi):
        own = own + recv2[off - 1].astype(jnp.float32)
    out_ref[...] = own.astype(out_ref.dtype)


def project(parts, stats, out_weight, tp_count):
    na, heads, block_rows, _ = parts.shape
    n_hi = tp_count // 2
    rows = block_rows // tp_count
    cols = out_weight.shape[1]
    vmem = pl.BlockSpec(memory_space=pltpu.VMEM)
    return pl.pallas_call(
        functools.partial(project_kernel, na, n_hi),
        out_shape=jax.ShapeDtypeStruct((rows, cols), jnp.bfloat16),
        in_specs=[vmem, vmem, vmem],
        out_specs=vmem,
        scratch_shapes=[
            pltpu.VMEM((na - 1,) + parts.shape[1:], parts.dtype),
            pltpu.VMEM((na - 1,) + stats.shape[1:], stats.dtype),
            pltpu.VMEM((block_rows, cols), jnp.float32),
            pltpu.VMEM((n_hi, rows, cols), jnp.bfloat16),
            pltpu.VMEM((n_hi, rows, cols), jnp.bfloat16),
            pltpu.VMEM((n_hi, rows, cols), jnp.float32),
            pltpu.VMEM((n_hi, rows, cols), jnp.bfloat16),
            pltpu.VMEM((n_hi - 1, rows, cols), jnp.bfloat16),
            pltpu.SemaphoreType.DMA((2, na - 1)),
            pltpu.SemaphoreType.DMA((2, na - 1)),
            pltpu.SemaphoreType.DMA((2,)),
            pltpu.SemaphoreType.DMA((n_hi - 1,)),
            pltpu.SemaphoreType.DMA((n_hi - 1,)),
        ],
        compiler_params=pltpu.CompilerParams(collective_id=1, has_side_effects=True),
    )(parts, stats, out_weight)


def local(query_vectors, key_vectors, value_vectors, out_weight):
    score_scale = 1.0 / math.sqrt(HD)
    tp_count = lax.axis_size("tp")
    ca_count = lax.axis_size("ca")
    token_rows = query_vectors.shape[0]
    own_heads = query_vectors.shape[1] // HD // tp_count
    own_cols = own_heads * HD

    qkv = jnp.stack([query_vectors, key_vectors, value_vectors], axis=0)
    staged = qkv.reshape(3, token_rows, tp_count, own_heads, HD).transpose(2, 0, 3, 1, 4)
    block_rows = token_rows * tp_count
    query_heads, kv = exchange(staged, ca_count, lax.axis_size("cz"))
    query_heads = query_heads.transpose(1, 0, 2, 3).reshape(own_heads, ca_count * block_rows, HD)
    kv = kv.transpose(1, 2, 0, 3, 4).reshape(2, own_heads, -1, HD)

    row_peak, row_total, weighted = attend_local(query_heads, kv[0], kv[1], score_scale)
    stats = jnp.stack([row_peak, row_total], axis=0).reshape(2, own_heads, ca_count, block_rows)
    parts = weighted.astype(jnp.bfloat16).reshape(own_heads, ca_count, block_rows, HD)
    return project(parts.transpose(1, 0, 2, 3), stats.transpose(2, 0, 1, 3), out_weight, tp_count)


def solution(mesh):
    ctx_count, tp_count = mesh.devices.shape
    split_mesh = Mesh(
        mesh.devices.reshape(ctx_count // KEY_SPLIT, KEY_SPLIT, tp_count), ("ca", "cz", "tp")
    )
    rows = P(("ca", "cz", "tp"), None)
    return jax.shard_map(
        local,
        mesh=split_mesh,
        in_specs=(rows, rows, rows, P("tp", None)),
        out_specs=rows,
        check_vma=False,
    )
```

```python
import functools
import math

import jax
import jax.numpy as jnp
from jax import lax
from jax.sharding import Mesh
from jax.sharding import PartitionSpec as P
from jax.experimental import pallas as pl
from jax.experimental.pallas import tpu as pltpu

HD = 128
KEY_SPLIT = 8


def attend_local(query_heads, key_heads, value_heads, score_scale):
    scores = (
        jnp.einsum("hid,hjd->hij", query_heads, key_heads, preferred_element_type=jnp.float32)
        * score_scale
    )
    row_peak = jnp.max(scores, axis=-1)
    weights_low = jnp.exp(scores - row_peak[..., None]).astype(jnp.bfloat16)
    row_total = jnp.sum(weights_low.astype(jnp.float32), axis=-1)
    weighted = jnp.einsum(
        "hij,hjd->hid", weights_low, value_heads, preferred_element_type=jnp.float32
    )
    return row_peak, row_total, weighted


def gather_by_exchange(block, axis_name):
    count = lax.axis_size(axis_name)
    spread = jnp.broadcast_to(block[None], (count,) + block.shape)
    return lax.all_to_all(spread, axis_name, 0, 0, tiled=True)


def attend_kernel(na, nz, nt, score_scale, staged, parts_out, peak_out, total_out, q_buf,
                  kv_buf, acc, tq_sems, tkv_sems, own_sems, q_sems, r_sems, l_sems):
    mesh_ids = pl.DeviceIdType.MESH
    a = lax.axis_index("ca")
    z = lax.axis_index("cz")
    t = lax.axis_index("tp")
    right = lax.rem(z + 1, nz)
    left = lax.rem(z + nz - 1, nz)
    heads = staged.shape[2]
    rows = staged.shape[3]

    barrier = pltpu.get_barrier_semaphore()
    for off in range(1, nt):
        pl.semaphore_signal(barrier, inc=1, device_id=(a, z, lax.rem(t + off, nt)),
                            device_id_type=mesh_ids)
    for off in range(1, na):
        pl.semaphore_signal(barrier, inc=1, device_id=(lax.rem(a + off, na), z, t),
                            device_id_type=mesh_ids)
    for side in (left, right):
        pl.semaphore_signal(barrier, inc=1, device_id=(a, side, t), device_id_type=mesh_ids)
    pl.semaphore_wait(barrier, nt - 1 + na - 1 + 2)

    mine = pl.ds(pl.multiple_of(t * rows, rows), rows)
    own = [
        pltpu.make_async_copy(staged.at[t, 0], q_buf.at[a, :, mine], own_sems.at[0]),
        pltpu.make_async_copy(staged.at[t, pl.ds(1, 2)], kv_buf.at[z, :, :, mine], own_sems.at[1]),
    ]
    for copy in own:
        copy.start()
    spread = []
    for off in range(1, nt):
        dest = lax.rem(t + off, nt)
        spread.append(pltpu.make_async_remote_copy(
            src_ref=staged.at[dest, 0], dst_ref=q_buf.at[a, :, mine],
            send_sem=tq_sems.at[0, off - 1], recv_sem=tq_sems.at[1, off - 1],
            device_id=(a, z, dest), device_id_type=mesh_ids))
        spread.append(pltpu.make_async_remote_copy(
            src_ref=staged.at[dest, pl.ds(1, 2)], dst_ref=kv_buf.at[z, :, :, mine],
            send_sem=tkv_sems.at[0, off - 1], recv_sem=tkv_sems.at[1, off - 1],
            device_id=(a, z, dest), device_id_type=mesh_ids))
    for copy in spread:
        copy.start()
    peak_out[...] = jnp.full(peak_out.shape, -1e30, jnp.float32)
    total_out[...] = jnp.zeros(total_out.shape, jnp.float32)
    acc[...] = jnp.zeros(acc.shape, jnp.float32)
    for copy in spread:
        copy.wait()
    for copy in own:
        copy.wait()

    q_copies = []
    for off in range(1, na):
        copy = pltpu.make_async_remote_copy(
            src_ref=q_buf.at[a], dst_ref=q_buf.at[a], send_sem=q_sems.at[0, off - 1],
            recv_sem=q_sems.at[1, off - 1], device_id=(lax.rem(a + off, na), z, t),
            device_id_type=mesh_ids)
        copy.start()
        q_copies.append(copy)

    def absorb(slot):
        def body(c, carry):
            for h in range(heads):
                query = q_buf[c, h]
                scores = lax.dot_general(
                    query, kv_buf[slot, 0, h], (((1,), (1,)), ((), ())),
                    preferred_element_type=jnp.float32) * score_scale
                old_peak = peak_out[c, h]
                new_peak = jnp.maximum(old_peak, jnp.max(scores, axis=-1, keepdims=True))
                weights_low = jnp.exp(scores - new_peak).astype(jnp.bfloat16)
                shrink = jnp.exp(old_peak - new_peak)
                total_out[c, h] = total_out[c, h] * shrink + jnp.sum(
                    weights_low.astype(jnp.float32), axis=-1, keepdims=True)
                acc[c, h] = acc[c, h] * shrink + jnp.dot(
                    weights_low, kv_buf[slot, 1, h], preferred_element_type=jnp.float32)
                peak_out[c, h] = new_peak
            return carry
        lax.fori_loop(0, na, body, 0)

    n_right = nz // 2
    n_left = (nz - 1) // 2
    chains = ((right, n_right, r_sems, -1, []), (left, n_left, l_sems, 1, []))

    def ring_step(step):
        for part in range(2):
            for side, count, sems, sign, copies in chains:
                if step >= count:
                    continue
                slot = lax.rem(z + sign * step + nz, nz)
                if step > 0:
                    copies[(step - 1) * 2 + part].wait_recv()
                copy = pltpu.make_async_remote_copy(
                    src_ref=kv_buf.at[slot, part], dst_ref=kv_buf.at[slot, part],
                    send_sem=sems.at[0, step * 2 + part], recv_sem=sems.at[1, step * 2 + part],
                    device_id=(a, side, t), device_id_type=mesh_ids)
                copy.start()
                copies.append(copy)

    ring_step(0)
    for copy in q_copies:
        copy.wait()
    absorb(z)
    for step in range(1, n_right + 1):
        if step < n_right:
            ring_step(step)
        for side, count, sems, sign, copies in chains:
            if step == count:
                copies[-2].wait_recv()
                copies[-1].wait_recv()
        absorb(lax.rem(z - step + nz, nz))
        if step <= n_left:
            absorb(lax.rem(z + step, nz))
    for side, count, sems, sign, copies in chains:
        for copy in copies:
            copy.wait_send()
    parts_out[...] = acc[...].astype(parts_out.dtype)


def attend(staged, na, nz, score_scale):
    nt, _, heads, rows, width = staged.shape
    n_right = nz // 2
    n_left = (nz - 1) // 2
    block = nt * rows
    vmem = pl.BlockSpec(memory_space=pltpu.VMEM)
    return pl.pallas_call(
        functools.partial(attend_kernel, na, nz, nt, score_scale),
        out_shape=(
            jax.ShapeDtypeStruct((na, heads, block, width), staged.dtype),
            jax.ShapeDtypeStruct((na, heads, block, 1), jnp.float32),
            jax.ShapeDtypeStruct((na, heads, block, 1), jnp.float32),
        ),
        in_specs=[pl.BlockSpec(memory_space=pl.ANY)],
        out_specs=(vmem, vmem, vmem),
        scratch_shapes=[
            pltpu.VMEM((na, heads, block, width), staged.dtype),
            pltpu.VMEM((nz, 2, heads, block, width), staged.dtype),
            pltpu.VMEM((na, heads, block, width), jnp.float32),
            pltpu.SemaphoreType.DMA((2, nt - 1)),
            pltpu.SemaphoreType.DMA((2, nt - 1)),
            pltpu.SemaphoreType.DMA((2,)),
            pltpu.SemaphoreType.DMA((2, na - 1)),
            pltpu.SemaphoreType.DMA((2, 2 * n_right)),
            pltpu.SemaphoreType.DMA((2, 2 * n_left)),
        ],
        compiler_params=pltpu.CompilerParams(collective_id=0, has_side_effects=True),
    )(staged)


def project_kernel(na, n_hi, parts_ref, stats_ref, w_ref, out_ref, got_parts, got_stats, full,
                   send1, recv1, total, send2, recv2, part_sems, stat_sems, sems1, send_sems2,
                   recv_sems2):
    mesh_ids = pl.DeviceIdType.MESH
    a = lax.axis_index("ca")
    z = lax.axis_index("cz")
    t = lax.axis_index("tp")
    core = lax.rem(t, 2)
    hi = t // 2
    partner = (a, z, hi * 2 + 1 - core)
    rows = send2.shape[1]
    heads = parts_ref.shape[1]

    barrier = pltpu.get_barrier_semaphore()
    for off in range(1, na):
        pl.semaphore_signal(barrier, inc=1, device_id=(lax.rem(a + off, na), z, t),
                            device_id_type=mesh_ids)
    pl.semaphore_signal(barrier, inc=1, device_id=partner, device_id_type=mesh_ids)
    for off in range(1, n_hi):
        pl.semaphore_signal(barrier, inc=1, device_id=(a, z, lax.rem(hi + off, n_hi) * 2 + core),
                            device_id_type=mesh_ids)
    pl.semaphore_wait(barrier, na - 1 + n_hi)

    gathered = []
    for off in range(1, na):
        dest = lax.rem(a + off, na)
        for src, dst, sems in ((parts_ref, got_parts, part_sems), (stats_ref, got_stats, stat_sems)):
            copy = pltpu.make_async_remote_copy(
                src_ref=src.at[dest], dst_ref=dst.at[off - 1], send_sem=sems.at[0, off - 1],
                recv_sem=sems.at[1, off - 1], device_id=(dest, z, t), device_id_type=mesh_ids)
            copy.start()
            gathered.append(copy)
    for copy in gathered:
        copy.wait()

    peaks = [stats_ref[a, 0]] + [got_stats[off - 1, 0] for off in range(1, na)]
    sums = [stats_ref[a, 1]] + [got_stats[off - 1, 1] for off in range(1, na)]
    top = peaks[0]
    for peak in peaks[1:]:
        top = jnp.maximum(top, peak)
    factors = [jnp.exp(peak - top) for peak in peaks]
    totals = factors[0] * sums[0]
    for factor, part_sum in zip(factors[1:], sums[1:]):
        totals = totals + factor * part_sum
    for h in range(heads):
        numerator = parts_ref[a, h].astype(jnp.float32) * factors[0][h][:, None]
        for off in range(1, na):
            numerator = numerator + (
                got_parts[off - 1, h].astype(jnp.float32) * factors[off][h][:, None]
            )
        attended = (numerator / totals[h][:, None]).astype(jnp.bfloat16)
        product = jnp.dot(attended, w_ref[pl.ds(h * HD, HD), :], preferred_element_type=jnp.float32)
        if h == 0:
            full[...] = product
        else:
            full[...] = full[...] + product

    for j in range(n_hi):
        their = pl.multiple_of((j * 2 + 1 - core) * rows, rows)
        mine = pl.multiple_of((j * 2 + core) * rows, rows)
        send1[j] = full[pl.ds(their, rows), :].astype(jnp.bfloat16)
        total[j] = full[pl.ds(mine, rows), :].astype(jnp.bfloat16).astype(jnp.float32)
    first = pltpu.make_async_remote_copy(
        src_ref=send1, dst_ref=recv1, send_sem=sems1.at[0], recv_sem=sems1.at[1],
        device_id=partner, device_id_type=mesh_ids)
    first.start()
    first.wait()
    for j in range(n_hi):
        send2[j] = (total[j] + recv1[j].astype(jnp.float32)).astype(jnp.bfloat16)
    second = []
    for off in range(1, n_hi):
        dest = lax.rem(hi + off, n_hi)
        copy = pltpu.make_async_remote_copy(
            src_ref=send2.at[dest], dst_ref=recv2.at[off - 1], send_sem=send_sems2.at[off - 1],
            recv_sem=recv_sems2.at[off - 1], device_id=(a, z, dest * 2 + core),
            device_id_type=mesh_ids)
        copy.start()
        second.append(copy)
    own = total[hi] + recv1[hi].astype(jnp.float32)
    for copy in second:
        copy.wait()
    for off in range(1, n_hi):
        own = own + recv2[off - 1].astype(jnp.float32)
    out_ref[...] = own.astype(out_ref.dtype)


def project(parts, stats, out_weight, tp_count):
    na, heads, block_rows, _ = parts.shape
    n_hi = tp_count // 2
    rows = block_rows // tp_count
    cols = out_weight.shape[1]
    vmem = pl.BlockSpec(memory_space=pltpu.VMEM)
    return pl.pallas_call(
        functools.partial(project_kernel, na, n_hi),
        out_shape=jax.ShapeDtypeStruct((rows, cols), jnp.bfloat16),
        in_specs=[vmem, vmem, vmem],
        out_specs=vmem,
        scratch_shapes=[
            pltpu.VMEM((na - 1,) + parts.shape[1:], parts.dtype),
            pltpu.VMEM((na - 1,) + stats.shape[1:], stats.dtype),
            pltpu.VMEM((block_rows, cols), jnp.float32),
            pltpu.VMEM((n_hi, rows, cols), jnp.bfloat16),
            pltpu.VMEM((n_hi, rows, cols), jnp.bfloat16),
            pltpu.VMEM((n_hi, rows, cols), jnp.float32),
            pltpu.VMEM((n_hi, rows, cols), jnp.bfloat16),
            pltpu.VMEM((n_hi - 1, rows, cols), jnp.bfloat16),
            pltpu.SemaphoreType.DMA((2, na - 1)),
            pltpu.SemaphoreType.DMA((2, na - 1)),
            pltpu.SemaphoreType.DMA((2,)),
            pltpu.SemaphoreType.DMA((n_hi - 1,)),
            pltpu.SemaphoreType.DMA((n_hi - 1,)),
        ],
        compiler_params=pltpu.CompilerParams(collective_id=1, has_side_effects=True),
    )(parts, stats, out_weight)


def local(query_vectors, key_vectors, value_vectors, out_weight):
    score_scale = 1.0 / math.sqrt(HD)
    tp_count = lax.axis_size("tp")
    ca_count = lax.axis_size("ca")
    token_rows = query_vectors.shape[0]
    own_heads = query_vectors.shape[1] // HD // tp_count
    own_cols = own_heads * HD

    qkv = jnp.stack([query_vectors, key_vectors, value_vectors], axis=0)
    staged = qkv.reshape(3, token_rows, tp_count, own_heads, HD).transpose(2, 0, 3, 1, 4)
    block_rows = token_rows * tp_count
    parts, peak, total = attend(staged, ca_count, lax.axis_size("cz"), score_scale)
    stats = jnp.stack([peak[..., 0], total[..., 0]], axis=1)
    return project(parts, stats, out_weight, tp_count)


def solution(mesh):
    ctx_count, tp_count = mesh.devices.shape
    split_mesh = Mesh(
        mesh.devices.reshape(ctx_count // KEY_SPLIT, KEY_SPLIT, tp_count), ("ca", "cz", "tp")
    )
    rows = P(("ca", "cz", "tp"), None)
    return jax.shard_map(
        local,
        mesh=split_mesh,
        in_specs=(rows, rows, rows, P("tp", None)),
        out_specs=rows,
        check_vma=False,
    )
```

```python
import functools
import math

import jax
import jax.numpy as jnp
from jax import lax
from jax.sharding import Mesh
from jax.sharding import PartitionSpec as P
from jax.experimental import pallas as pl
from jax.experimental.pallas import tpu as pltpu

HD = 128
KEY_SPLIT = 8


def attend_local(query_heads, key_heads, value_heads, score_scale):
    scores = (
        jnp.einsum("hid,hjd->hij", query_heads, key_heads, preferred_element_type=jnp.float32)
        * score_scale
    )
    row_peak = jnp.max(scores, axis=-1)
    weights_low = jnp.exp(scores - row_peak[..., None]).astype(jnp.bfloat16)
    row_total = jnp.sum(weights_low.astype(jnp.float32), axis=-1)
    weighted = jnp.einsum(
        "hij,hjd->hid", weights_low, value_heads, preferred_element_type=jnp.float32
    )
    return row_peak, row_total, weighted


def gather_by_exchange(block, axis_name):
    count = lax.axis_size(axis_name)
    spread = jnp.broadcast_to(block[None], (count,) + block.shape)
    return lax.all_to_all(spread, axis_name, 0, 0, tiled=True)


def exchange_kernel(na, nz, nt, q_ref, k_ref, v_ref, q_out, kv_out, spread_sems, own_sems,
                    q_sems, r_sems, l_sems):
    mesh_ids = pl.DeviceIdType.MESH
    a = lax.axis_index("ca")
    z = lax.axis_index("cz")
    t = lax.axis_index("tp")
    right = lax.rem(z + 1, nz)
    left = lax.rem(z + nz - 1, nz)
    rows = q_ref.shape[0]
    cols = q_out.shape[2]

    barrier = pltpu.get_barrier_semaphore()
    for off in range(1, nt):
        pl.semaphore_signal(barrier, inc=1, device_id=(a, z, lax.rem(t + off, nt)),
                            device_id_type=mesh_ids)
    for off in range(1, na):
        pl.semaphore_signal(barrier, inc=1, device_id=(lax.rem(a + off, na), z, t),
                            device_id_type=mesh_ids)
    for side in (left, right):
        pl.semaphore_signal(barrier, inc=1, device_id=(a, side, t), device_id_type=mesh_ids)
    pl.semaphore_wait(barrier, nt - 1 + na - 1 + 2)

    mine = pl.ds(pl.multiple_of(t * rows, rows), rows)
    targets = (q_out.at[a, mine], kv_out.at[z, 0, mine], kv_out.at[z, 1, mine])
    sources = (q_ref, k_ref, v_ref)

    def columns(dest):
        return pl.ds(pl.multiple_of(dest * cols, cols), cols)

    own = []
    for i in range(3):
        copy = pltpu.make_async_copy(sources[i].at[:, columns(t)], targets[i], own_sems.at[i])
        copy.start()
        own.append(copy)
    spread = []
    for off in range(1, nt):
        dest = lax.rem(t + off, nt)
        for i in range(3):
            spread.append(pltpu.make_async_remote_copy(
                src_ref=sources[i].at[:, columns(dest)], dst_ref=targets[i],
                send_sem=spread_sems.at[0, i, off - 1], recv_sem=spread_sems.at[1, i, off - 1],
                device_id=(a, z, dest), device_id_type=mesh_ids))
    for copy in spread:
        copy.start()
    for copy in spread:
        copy.wait()
    for copy in own:
        copy.wait()

    q_copies = []
    for off in range(1, na):
        copy = pltpu.make_async_remote_copy(
            src_ref=q_out.at[a], dst_ref=q_out.at[a], send_sem=q_sems.at[0, off - 1],
            recv_sem=q_sems.at[1, off - 1], device_id=(lax.rem(a + off, na), z, t),
            device_id_type=mesh_ids)
        copy.start()
        q_copies.append(copy)

    n_right = nz // 2
    n_left = (nz - 1) // 2
    chains = ((right, n_right, r_sems, -1, []), (left, n_left, l_sems, 1, []))
    for step in range(n_right):
        for part in range(2):
            for side, count, sems, sign, copies in chains:
                if step >= count:
                    continue
                slot = lax.rem(z + sign * step + nz, nz)
                if step > 0:
                    copies[(step - 1) * 2 + part].wait_recv()
                copy = pltpu.make_async_remote_copy(
                    src_ref=kv_out.at[slot, part], dst_ref=kv_out.at[slot, part],
                    send_sem=sems.at[0, step * 2 + part], recv_sem=sems.at[1, step * 2 + part],
                    device_id=(a, side, t), device_id_type=mesh_ids)
                copy.start()
                copies.append(copy)
    for side, count, sems, sign, copies in chains:
        copies[-2].wait_recv()
        copies[-1].wait_recv()
        for copy in copies:
            copy.wait_send()
    for copy in q_copies:
        copy.wait()


def exchange(query_vectors, key_vectors, value_vectors, na, nz, nt):
    rows, width = query_vectors.shape
    cols = width // nt
    n_right = nz // 2
    n_left = (nz - 1) // 2
    dtype = query_vectors.dtype
    return pl.pallas_call(
        functools.partial(exchange_kernel, na, nz, nt),
        out_shape=(
            jax.ShapeDtypeStruct((na, nt * rows, cols), dtype),
            jax.ShapeDtypeStruct((nz, 2, nt * rows, cols), dtype),
        ),
        in_specs=[pl.BlockSpec(memory_space=pl.ANY)] * 3,
        out_specs=(pl.BlockSpec(memory_space=pl.ANY), pl.BlockSpec(memory_space=pl.ANY)),
        scratch_shapes=[
            pltpu.SemaphoreType.DMA((2, 3, nt - 1)),
            pltpu.SemaphoreType.DMA((3,)),
            pltpu.SemaphoreType.DMA((2, na - 1)),
            pltpu.SemaphoreType.DMA((2, 2 * n_right)),
            pltpu.SemaphoreType.DMA((2, 2 * n_left)),
        ],
        compiler_params=pltpu.CompilerParams(collective_id=0, has_side_effects=True),
    )(query_vectors, key_vectors, value_vectors)


def project_kernel(na, n_hi, parts_ref, stats_ref, w_ref, out_ref, got_parts, got_stats, full,
                   send1, recv1, total, send2, recv2, part_sems, stat_sems, sems1, send_sems2,
                   recv_sems2):
    mesh_ids = pl.DeviceIdType.MESH
    a = lax.axis_index("ca")
    z = lax.axis_index("cz")
    t = lax.axis_index("tp")
    core = lax.rem(t, 2)
    hi = t // 2
    partner = (a, z, hi * 2 + 1 - core)
    rows = send2.shape[1]
    heads = parts_ref.shape[1]

    barrier = pltpu.get_barrier_semaphore()
    for off in range(1, na):
        pl.semaphore_signal(barrier, inc=1, device_id=(lax.rem(a + off, na), z, t),
                            device_id_type=mesh_ids)
    pl.semaphore_signal(barrier, inc=1, device_id=partner, device_id_type=mesh_ids)
    for off in range(1, n_hi):
        pl.semaphore_signal(barrier, inc=1, device_id=(a, z, lax.rem(hi + off, n_hi) * 2 + core),
                            device_id_type=mesh_ids)
    pl.semaphore_wait(barrier, na - 1 + n_hi)

    gathered = []
    for off in range(1, na):
        dest = lax.rem(a + off, na)
        for src, dst, sems in ((parts_ref, got_parts, part_sems), (stats_ref, got_stats, stat_sems)):
            copy = pltpu.make_async_remote_copy(
                src_ref=src.at[dest], dst_ref=dst.at[off - 1], send_sem=sems.at[0, off - 1],
                recv_sem=sems.at[1, off - 1], device_id=(dest, z, t), device_id_type=mesh_ids)
            copy.start()
            gathered.append(copy)
    for copy in gathered:
        copy.wait()

    peaks = [stats_ref[a, 0]] + [got_stats[off - 1, 0] for off in range(1, na)]
    sums = [stats_ref[a, 1]] + [got_stats[off - 1, 1] for off in range(1, na)]
    top = peaks[0]
    for peak in peaks[1:]:
        top = jnp.maximum(top, peak)
    factors = [jnp.exp(peak - top) for peak in peaks]
    totals = factors[0] * sums[0]
    for factor, part_sum in zip(factors[1:], sums[1:]):
        totals = totals + factor * part_sum
    for h in range(heads):
        numerator = parts_ref[a, h].astype(jnp.float32) * factors[0][h][:, None]
        for off in range(1, na):
            numerator = numerator + (
                got_parts[off - 1, h].astype(jnp.float32) * factors[off][h][:, None]
            )
        attended = (numerator / totals[h][:, None]).astype(jnp.bfloat16)
        product = jnp.dot(attended, w_ref[pl.ds(h * HD, HD), :], preferred_element_type=jnp.float32)
        if h == 0:
            full[...] = product
        else:
            full[...] = full[...] + product

    for j in range(n_hi):
        their = pl.multiple_of((j * 2 + 1 - core) * rows, rows)
        mine = pl.multiple_of((j * 2 + core) * rows, rows)
        send1[j] = full[pl.ds(their, rows), :].astype(jnp.bfloat16)
        total[j] = full[pl.ds(mine, rows), :].astype(jnp.bfloat16).astype(jnp.float32)
    first = pltpu.make_async_remote_copy(
        src_ref=send1, dst_ref=recv1, send_sem=sems1.at[0], recv_sem=sems1.at[1],
        device_id=partner, device_id_type=mesh_ids)
    first.start()
    first.wait()
    for j in range(n_hi):
        send2[j] = (total[j] + recv1[j].astype(jnp.float32)).astype(jnp.bfloat16)
    second = []
    for off in range(1, n_hi):
        dest = lax.rem(hi + off, n_hi)
        copy = pltpu.make_async_remote_copy(
            src_ref=send2.at[dest], dst_ref=recv2.at[off - 1], send_sem=send_sems2.at[off - 1],
            recv_sem=recv_sems2.at[off - 1], device_id=(a, z, dest * 2 + core),
            device_id_type=mesh_ids)
        copy.start()
        second.append(copy)
    own = total[hi] + recv1[hi].astype(jnp.float32)
    for copy in second:
        copy.wait()
    for off in range(1, n_hi):
        own = own + recv2[off - 1].astype(jnp.float32)
    out_ref[...] = own.astype(out_ref.dtype)


def project(parts, stats, out_weight, tp_count):
    na, heads, block_rows, _ = parts.shape
    n_hi = tp_count // 2
    rows = block_rows // tp_count
    cols = out_weight.shape[1]
    vmem = pl.BlockSpec(memory_space=pltpu.VMEM)
    return pl.pallas_call(
        functools.partial(project_kernel, na, n_hi),
        out_shape=jax.ShapeDtypeStruct((rows, cols), jnp.bfloat16),
        in_specs=[vmem, vmem, vmem],
        out_specs=vmem,
        scratch_shapes=[
            pltpu.VMEM((na - 1,) + parts.shape[1:], parts.dtype),
            pltpu.VMEM((na - 1,) + stats.shape[1:], stats.dtype),
            pltpu.VMEM((block_rows, cols), jnp.float32),
            pltpu.VMEM((n_hi, rows, cols), jnp.bfloat16),
            pltpu.VMEM((n_hi, rows, cols), jnp.bfloat16),
            pltpu.VMEM((n_hi, rows, cols), jnp.float32),
            pltpu.VMEM((n_hi, rows, cols), jnp.bfloat16),
            pltpu.VMEM((n_hi - 1, rows, cols), jnp.bfloat16),
            pltpu.SemaphoreType.DMA((2, na - 1)),
            pltpu.SemaphoreType.DMA((2, na - 1)),
            pltpu.SemaphoreType.DMA((2,)),
            pltpu.SemaphoreType.DMA((n_hi - 1,)),
            pltpu.SemaphoreType.DMA((n_hi - 1,)),
        ],
        compiler_params=pltpu.CompilerParams(collective_id=1, has_side_effects=True),
    )(parts, stats, out_weight)


def local(query_vectors, key_vectors, value_vectors, out_weight):
    score_scale = 1.0 / math.sqrt(HD)
    tp_count = lax.axis_size("tp")
    ca_count = lax.axis_size("ca")
    token_rows = query_vectors.shape[0]
    own_heads = query_vectors.shape[1] // HD // tp_count
    own_cols = own_heads * HD

    block_rows = token_rows * tp_count
    query_rows, kv = exchange(
        query_vectors, key_vectors, value_vectors, ca_count, lax.axis_size("cz"), tp_count)
    query_heads = query_rows.reshape(-1, own_heads, HD).transpose(1, 0, 2)
    kv = kv.transpose(1, 0, 2, 3).reshape(2, -1, own_heads, HD).transpose(0, 2, 1, 3)

    row_peak, row_total, weighted = attend_local(query_heads, kv[0], kv[1], score_scale)
    stats = jnp.stack([row_peak, row_total], axis=0).reshape(2, own_heads, ca_count, block_rows)
    parts = weighted.astype(jnp.bfloat16).reshape(own_heads, ca_count, block_rows, HD)
    return project(parts.transpose(1, 0, 2, 3), stats.transpose(2, 0, 1, 3), out_weight, tp_count)


def solution(mesh):
    ctx_count, tp_count = mesh.devices.shape
    split_mesh = Mesh(
        mesh.devices.reshape(ctx_count // KEY_SPLIT, KEY_SPLIT, tp_count), ("ca", "cz", "tp")
    )
    rows = P(("ca", "cz", "tp"), None)
    return jax.shard_map(
        local,
        mesh=split_mesh,
        in_specs=(rows, rows, rows, P("tp", None)),
        out_specs=rows,
        check_vma=False,
    )
```

```python
import functools
import math

import jax
import jax.numpy as jnp
from jax import lax
from jax.sharding import Mesh
from jax.sharding import PartitionSpec as P
from jax.experimental import pallas as pl
from jax.experimental.pallas import tpu as pltpu

HD = 128
KEY_SPLIT = 8


def attend_local(query_heads, key_heads, value_heads, score_scale):
    scores = (
        jnp.einsum("hid,hjd->hij", query_heads, key_heads, preferred_element_type=jnp.float32)
        * score_scale
    )
    row_peak = jnp.max(scores, axis=-1)
    weights_low = jnp.exp(scores - row_peak[..., None]).astype(jnp.bfloat16)
    row_total = jnp.sum(weights_low.astype(jnp.float32), axis=-1)
    weighted = jnp.einsum(
        "hij,hjd->hid", weights_low, value_heads, preferred_element_type=jnp.float32
    )
    return row_peak, row_total, weighted


def gather_by_exchange(block, axis_name):
    count = lax.axis_size(axis_name)
    spread = jnp.broadcast_to(block[None], (count,) + block.shape)
    return lax.all_to_all(spread, axis_name, 0, 0, tiled=True)


def exchange_kernel(na, nz, nt, q_ref, k_ref, v_ref, q_out, kv_out, spread_sems, own_sems,
                    q_sems, r_sems, l_sems):
    mesh_ids = pl.DeviceIdType.MESH
    a = lax.axis_index("ca")
    z = lax.axis_index("cz")
    t = lax.axis_index("tp")
    right = lax.rem(z + 1, nz)
    left = lax.rem(z + nz - 1, nz)
    rows = q_ref.shape[0]
    heads = q_out.shape[0]

    barrier = pltpu.get_barrier_semaphore()
    for off in range(1, nt):
        pl.semaphore_signal(barrier, inc=1, device_id=(a, z, lax.rem(t + off, nt)),
                            device_id_type=mesh_ids)
    for off in range(1, na):
        pl.semaphore_signal(barrier, inc=1, device_id=(lax.rem(a + off, na), z, t),
                            device_id_type=mesh_ids)
    for side in (left, right):
        pl.semaphore_signal(barrier, inc=1, device_id=(a, side, t), device_id_type=mesh_ids)
    pl.semaphore_wait(barrier, nt - 1 + na - 1 + 2)

    mine = pl.ds(pl.multiple_of(t * rows, rows), rows)
    sources = (q_ref, k_ref, v_ref)

    def target(i, h):
        if i == 0:
            return q_out.at[h, a, mine]
        return kv_out.at[i - 1, h, z, mine]

    def columns(dest, h):
        return pl.ds(pl.multiple_of((dest * heads + h) * HD, HD), HD)

    own = []
    for i in range(3):
        for h in range(heads):
            copy = pltpu.make_async_copy(
                sources[i].at[:, columns(t, h)], target(i, h), own_sems.at[i, h])
            copy.start()
            own.append(copy)
    spread = []
    for off in range(1, nt):
        dest = lax.rem(t + off, nt)
        for i in range(3):
            for h in range(heads):
                spread.append(pltpu.make_async_remote_copy(
                    src_ref=sources[i].at[:, columns(dest, h)], dst_ref=target(i, h),
                    send_sem=spread_sems.at[0, i, h, off - 1],
                    recv_sem=spread_sems.at[1, i, h, off - 1],
                    device_id=(a, z, dest), device_id_type=mesh_ids))
    for copy in spread:
        copy.start()
    for copy in spread:
        copy.wait()
    for copy in own:
        copy.wait()

    q_copies = []
    for off in range(1, na):
        copy = pltpu.make_async_remote_copy(
            src_ref=q_out.at[:, a], dst_ref=q_out.at[:, a], send_sem=q_sems.at[0, off - 1],
            recv_sem=q_sems.at[1, off - 1], device_id=(lax.rem(a + off, na), z, t),
            device_id_type=mesh_ids)
        copy.start()
        q_copies.append(copy)

    n_right = nz // 2
    n_left = (nz - 1) // 2
    chains = ((right, n_right, r_sems, -1, []), (left, n_left, l_sems, 1, []))
    for step in range(n_right):
        for part in range(2):
            for side, count, sems, sign, copies in chains:
                if step >= count:
                    continue
                slot = lax.rem(z + sign * step + nz, nz)
                if step > 0:
                    copies[(step - 1) * 2 + part].wait_recv()
                copy = pltpu.make_async_remote_copy(
                    src_ref=kv_out.at[part, :, slot], dst_ref=kv_out.at[part, :, slot],
                    send_sem=sems.at[0, step * 2 + part], recv_sem=sems.at[1, step * 2 + part],
                    device_id=(a, side, t), device_id_type=mesh_ids)
                copy.start()
                copies.append(copy)
    for side, count, sems, sign, copies in chains:
        copies[-2].wait_recv()
        copies[-1].wait_recv()
        for copy in copies:
            copy.wait_send()
    for copy in q_copies:
        copy.wait()


def exchange(query_vectors, key_vectors, value_vectors, na, nz, nt):
    rows, width = query_vectors.shape
    heads = width // nt // HD
    n_right = nz // 2
    n_left = (nz - 1) // 2
    dtype = query_vectors.dtype
    return pl.pallas_call(
        functools.partial(exchange_kernel, na, nz, nt),
        out_shape=(
            jax.ShapeDtypeStruct((heads, na, nt * rows, HD), dtype),
            jax.ShapeDtypeStruct((2, heads, nz, nt * rows, HD), dtype),
        ),
        in_specs=[pl.BlockSpec(memory_space=pl.ANY)] * 3,
        out_specs=(pl.BlockSpec(memory_space=pl.ANY), pl.BlockSpec(memory_space=pl.ANY)),
        scratch_shapes=[
            pltpu.SemaphoreType.DMA((2, 3, heads, nt - 1)),
            pltpu.SemaphoreType.DMA((3, heads)),
            pltpu.SemaphoreType.DMA((2, na - 1)),
            pltpu.SemaphoreType.DMA((2, 2 * n_right)),
            pltpu.SemaphoreType.DMA((2, 2 * n_left)),
        ],
        compiler_params=pltpu.CompilerParams(collective_id=0, has_side_effects=True),
    )(query_vectors, key_vectors, value_vectors)


def project_kernel(na, n_hi, parts_ref, stats_ref, w_ref, out_ref, got_parts, got_stats, full,
                   send1, recv1, total, send2, recv2, part_sems, stat_sems, sems1, send_sems2,
                   recv_sems2, own_stat_sem):
    mesh_ids = pl.DeviceIdType.MESH
    a = lax.axis_index("ca")
    z = lax.axis_index("cz")
    t = lax.axis_index("tp")
    core = lax.rem(t, 2)
    hi = t // 2
    partner = (a, z, hi * 2 + 1 - core)
    rows = send2.shape[1]
    heads = parts_ref.shape[0]

    barrier = pltpu.get_barrier_semaphore()
    for off in range(1, na):
        pl.semaphore_signal(barrier, inc=1, device_id=(lax.rem(a + off, na), z, t),
                            device_id_type=mesh_ids)
    pl.semaphore_signal(barrier, inc=1, device_id=partner, device_id_type=mesh_ids)
    for off in range(1, n_hi):
        pl.semaphore_signal(barrier, inc=1, device_id=(a, z, lax.rem(hi + off, n_hi) * 2 + core),
                            device_id_type=mesh_ids)
    pl.semaphore_wait(barrier, na - 1 + n_hi)

    own_stats = pltpu.make_async_copy(stats_ref.at[:, :, a], got_stats.at[na - 1], own_stat_sem)
    own_stats.start()
    gathered = []
    for off in range(1, na):
        dest = lax.rem(a + off, na)
        for src, dst, sems in ((parts_ref.at[:, dest], got_parts, part_sems),
                               (stats_ref.at[:, :, dest], got_stats, stat_sems)):
            copy = pltpu.make_async_remote_copy(
                src_ref=src, dst_ref=dst.at[off - 1], send_sem=sems.at[0, off - 1],
                recv_sem=sems.at[1, off - 1], device_id=(dest, z, t), device_id_type=mesh_ids)
            copy.start()
            gathered.append(copy)
    for copy in gathered:
        copy.wait()
    own_stats.wait()

    peaks = [got_stats[na - 1, 0]] + [got_stats[off - 1, 0] for off in range(1, na)]
    sums = [got_stats[na - 1, 1]] + [got_stats[off - 1, 1] for off in range(1, na)]
    top = peaks[0]
    for peak in peaks[1:]:
        top = jnp.maximum(top, peak)
    factors = [jnp.exp(peak - top) for peak in peaks]
    totals = factors[0] * sums[0]
    for factor, part_sum in zip(factors[1:], sums[1:]):
        totals = totals + factor * part_sum
    for h in range(heads):
        numerator = parts_ref[h, a].astype(jnp.float32) * factors[0][h][:, None]
        for off in range(1, na):
            numerator = numerator + (
                got_parts[off - 1, h].astype(jnp.float32) * factors[off][h][:, None]
            )
        attended = (numerator / totals[h][:, None]).astype(jnp.bfloat16)
        product = jnp.dot(attended, w_ref[pl.ds(h * HD, HD), :], preferred_element_type=jnp.float32)
        if h == 0:
            full[...] = product
        else:
            full[...] = full[...] + product

    for j in range(n_hi):
        their = pl.multiple_of((j * 2 + 1 - core) * rows, rows)
        mine = pl.multiple_of((j * 2 + core) * rows, rows)
        send1[j] = full[pl.ds(their, rows), :].astype(jnp.bfloat16)
        total[j] = full[pl.ds(mine, rows), :].astype(jnp.bfloat16).astype(jnp.float32)
    first = pltpu.make_async_remote_copy(
        src_ref=send1, dst_ref=recv1, send_sem=sems1.at[0], recv_sem=sems1.at[1],
        device_id=partner, device_id_type=mesh_ids)
    first.start()
    first.wait()
    for j in range(n_hi):
        send2[j] = (total[j] + recv1[j].astype(jnp.float32)).astype(jnp.bfloat16)
    second = []
    for off in range(1, n_hi):
        dest = lax.rem(hi + off, n_hi)
        copy = pltpu.make_async_remote_copy(
            src_ref=send2.at[dest], dst_ref=recv2.at[off - 1], send_sem=send_sems2.at[off - 1],
            recv_sem=recv_sems2.at[off - 1], device_id=(a, z, dest * 2 + core),
            device_id_type=mesh_ids)
        copy.start()
        second.append(copy)
    own = total[hi] + recv1[hi].astype(jnp.float32)
    for copy in second:
        copy.wait()
    for off in range(1, n_hi):
        own = own + recv2[off - 1].astype(jnp.float32)
    out_ref[...] = own.astype(out_ref.dtype)


def project(parts, stats, out_weight, tp_count):
    heads, na, block_rows, _ = parts.shape
    n_hi = tp_count // 2
    rows = block_rows // tp_count
    cols = out_weight.shape[1]
    vmem = pl.BlockSpec(memory_space=pltpu.VMEM)
    return pl.pallas_call(
        functools.partial(project_kernel, na, n_hi),
        out_shape=jax.ShapeDtypeStruct((rows, cols), jnp.bfloat16),
        in_specs=[vmem, vmem, vmem],
        out_specs=vmem,
        scratch_shapes=[
            pltpu.VMEM((na - 1, heads, block_rows, HD), parts.dtype),
            pltpu.VMEM((na, 2, heads, block_rows), stats.dtype),
            pltpu.VMEM((block_rows, cols), jnp.float32),
            pltpu.VMEM((n_hi, rows, cols), jnp.bfloat16),
            pltpu.VMEM((n_hi, rows, cols), jnp.bfloat16),
            pltpu.VMEM((n_hi, rows, cols), jnp.float32),
            pltpu.VMEM((n_hi, rows, cols), jnp.bfloat16),
            pltpu.VMEM((n_hi - 1, rows, cols), jnp.bfloat16),
            pltpu.SemaphoreType.DMA((2, na - 1)),
            pltpu.SemaphoreType.DMA((2, na - 1)),
            pltpu.SemaphoreType.DMA((2,)),
            pltpu.SemaphoreType.DMA((n_hi - 1,)),
            pltpu.SemaphoreType.DMA((n_hi - 1,)),
            pltpu.SemaphoreType.DMA(()),
        ],
        compiler_params=pltpu.CompilerParams(collective_id=1, has_side_effects=True),
    )(parts, stats, out_weight)


def local(query_vectors, key_vectors, value_vectors, out_weight):
    score_scale = 1.0 / math.sqrt(HD)
    tp_count = lax.axis_size("tp")
    ca_count = lax.axis_size("ca")
    token_rows = query_vectors.shape[0]
    own_heads = query_vectors.shape[1] // HD // tp_count
    own_cols = own_heads * HD

    block_rows = token_rows * tp_count
    query_heads, kv = exchange(
        query_vectors, key_vectors, value_vectors, ca_count, lax.axis_size("cz"), tp_count)
    query_heads = query_heads.reshape(own_heads, -1, HD)
    kv = kv.reshape(2, own_heads, -1, HD)

    row_peak, row_total, weighted = attend_local(query_heads, kv[0], kv[1], score_scale)
    stats = jnp.stack([row_peak, row_total], axis=0).reshape(2, own_heads, ca_count, block_rows)
    parts = weighted.astype(jnp.bfloat16).reshape(own_heads, ca_count, block_rows, HD)
    return project(parts, stats, out_weight, tp_count)


def solution(mesh):
    ctx_count, tp_count = mesh.devices.shape
    split_mesh = Mesh(
        mesh.devices.reshape(ctx_count // KEY_SPLIT, KEY_SPLIT, tp_count), ("ca", "cz", "tp")
    )
    rows = P(("ca", "cz", "tp"), None)
    return jax.shard_map(
        local,
        mesh=split_mesh,
        in_specs=(rows, rows, rows, P("tp", None)),
        out_specs=rows,
        check_vma=False,
    )
```

```python
import functools
import math

import jax
import jax.numpy as jnp
from jax import lax
from jax.sharding import Mesh
from jax.sharding import PartitionSpec as P
from jax.experimental import pallas as pl
from jax.experimental.pallas import tpu as pltpu

HD = 128
KEY_SPLIT = 8


def attend_local(query_heads, key_heads, value_heads, score_scale):
    scores = (
        jnp.einsum("hid,hjd->hij", query_heads, key_heads, preferred_element_type=jnp.float32)
        * score_scale
    )
    row_peak = jnp.max(scores, axis=-1)
    weights_low = jnp.exp(scores - row_peak[..., None]).astype(jnp.bfloat16)
    row_total = jnp.sum(weights_low.astype(jnp.float32), axis=-1)
    weighted = jnp.einsum(
        "hij,hjd->hid", weights_low, value_heads, preferred_element_type=jnp.float32
    )
    return row_peak, row_total, weighted


def gather_by_exchange(block, axis_name):
    count = lax.axis_size(axis_name)
    spread = jnp.broadcast_to(block[None], (count,) + block.shape)
    return lax.all_to_all(spread, axis_name, 0, 0, tiled=True)


def exchange_kernel(na, nz, nt, q_ref, k_ref, v_ref, q_out, kv_out, spread_sems, own_sems,
                    q_sems, r_sems, l_sems):
    mesh_ids = pl.DeviceIdType.MESH
    a = lax.axis_index("ca")
    z = lax.axis_index("cz")
    t = lax.axis_index("tp")
    right = lax.rem(z + 1, nz)
    left = lax.rem(z + nz - 1, nz)
    rows = q_ref.shape[0]
    heads = q_out.shape[0]

    barrier = pltpu.get_barrier_semaphore()
    for off in range(1, nt):
        pl.semaphore_signal(barrier, inc=1, device_id=(a, z, lax.rem(t + off, nt)),
                            device_id_type=mesh_ids)
    for off in range(1, na):
        pl.semaphore_signal(barrier, inc=1, device_id=(lax.rem(a + off, na), z, t),
                            device_id_type=mesh_ids)
    for side in (left, right):
        pl.semaphore_signal(barrier, inc=1, device_id=(a, side, t), device_id_type=mesh_ids)
    pl.semaphore_wait(barrier, nt - 1 + na - 1 + 2)

    mine = pl.ds(pl.multiple_of(t * rows, rows), rows)
    sources = (q_ref, k_ref, v_ref)

    def target(i, h):
        if i == 0:
            return q_out.at[h, a, mine]
        return kv_out.at[i - 1, h, z, mine]

    def columns(dest, h):
        return pl.ds(pl.multiple_of((dest * heads + h) * HD, HD), HD)

    own = []
    for i in range(3):
        for h in range(heads):
            copy = pltpu.make_async_copy(
                sources[i].at[:, columns(t, h)], target(i, h), own_sems.at[i, h])
            copy.start()
            own.append(copy)
    spread = []
    for off in range(1, nt):
        dest = lax.rem(t + off, nt)
        for i in range(3):
            for h in range(heads):
                spread.append(pltpu.make_async_remote_copy(
                    src_ref=sources[i].at[:, columns(dest, h)], dst_ref=target(i, h),
                    send_sem=spread_sems.at[0, i, h, off - 1],
                    recv_sem=spread_sems.at[1, i, h, off - 1],
                    device_id=(a, z, dest), device_id_type=mesh_ids))
    for copy in spread:
        copy.start()
    for copy in spread:
        copy.wait()
    for copy in own:
        copy.wait()

    q_copies = []
    for off in range(1, na):
        copy = pltpu.make_async_remote_copy(
            src_ref=q_out.at[:, a], dst_ref=q_out.at[:, a], send_sem=q_sems.at[0, off - 1],
            recv_sem=q_sems.at[1, off - 1], device_id=(lax.rem(a + off, na), z, t),
            device_id_type=mesh_ids)
        copy.start()
        q_copies.append(copy)

    n_right = nz // 2
    n_left = (nz - 1) // 2
    chains = ((right, n_right, r_sems, -1, []), (left, n_left, l_sems, 1, []))
    for step in range(n_right):
        for part in range(2):
            for side, count, sems, sign, copies in chains:
                if step >= count:
                    continue
                slot = lax.rem(z + sign * step + nz, nz)
                if step > 0:
                    copies[(step - 1) * 2 + part].wait_recv()
                copy = pltpu.make_async_remote_copy(
                    src_ref=kv_out.at[part, :, slot], dst_ref=kv_out.at[part, :, slot],
                    send_sem=sems.at[0, step * 2 + part], recv_sem=sems.at[1, step * 2 + part],
                    device_id=(a, side, t), device_id_type=mesh_ids)
                copy.start()
                copies.append(copy)
    for side, count, sems, sign, copies in chains:
        copies[-2].wait_recv()
        copies[-1].wait_recv()
        for copy in copies:
            copy.wait_send()
    for copy in q_copies:
        copy.wait()


def exchange(query_vectors, key_vectors, value_vectors, na, nz, nt):
    rows, width = query_vectors.shape
    heads = width // nt // HD
    n_right = nz // 2
    n_left = (nz - 1) // 2
    dtype = query_vectors.dtype
    return pl.pallas_call(
        functools.partial(exchange_kernel, na, nz, nt),
        out_shape=(
            jax.ShapeDtypeStruct((heads, na, nt * rows, HD), dtype),
            jax.ShapeDtypeStruct((2, heads, nz, nt * rows, HD), dtype),
        ),
        in_specs=[pl.BlockSpec(memory_space=pl.ANY)] * 3,
        out_specs=(pl.BlockSpec(memory_space=pl.ANY), pl.BlockSpec(memory_space=pl.ANY)),
        scratch_shapes=[
            pltpu.SemaphoreType.DMA((2, 3, heads, nt - 1)),
            pltpu.SemaphoreType.DMA((3, heads)),
            pltpu.SemaphoreType.DMA((2, na - 1)),
            pltpu.SemaphoreType.DMA((2, 2 * n_right)),
            pltpu.SemaphoreType.DMA((2, 2 * n_left)),
        ],
        compiler_params=pltpu.CompilerParams(collective_id=0, has_side_effects=True),
    )(query_vectors, key_vectors, value_vectors)


def project_kernel(na, n_hi, parts_ref, stats_ref, w_ref, out_ref, got_parts, got_stats, att_buf,
                   pick, send1, recv1, total, send2, recv2, part_sems, stat_sems, sems1, send_sems2,
                   recv_sems2, own_stat_sem):
    mesh_ids = pl.DeviceIdType.MESH
    a = lax.axis_index("ca")
    z = lax.axis_index("cz")
    t = lax.axis_index("tp")
    core = lax.rem(t, 2)
    hi = t // 2
    partner = (a, z, hi * 2 + 1 - core)
    rows = send2.shape[1]
    heads = parts_ref.shape[0]

    barrier = pltpu.get_barrier_semaphore()
    for off in range(1, na):
        pl.semaphore_signal(barrier, inc=1, device_id=(lax.rem(a + off, na), z, t),
                            device_id_type=mesh_ids)
    pl.semaphore_signal(barrier, inc=1, device_id=partner, device_id_type=mesh_ids)
    for off in range(1, n_hi):
        pl.semaphore_signal(barrier, inc=1, device_id=(a, z, lax.rem(hi + off, n_hi) * 2 + core),
                            device_id_type=mesh_ids)
    pl.semaphore_wait(barrier, na - 1 + n_hi)

    own_stats = pltpu.make_async_copy(stats_ref.at[:, :, a], got_stats.at[na - 1], own_stat_sem)
    own_stats.start()
    gathered = []
    for off in range(1, na):
        dest = lax.rem(a + off, na)
        for src, dst, sems in ((parts_ref.at[:, dest], got_parts, part_sems),
                               (stats_ref.at[:, :, dest], got_stats, stat_sems)):
            copy = pltpu.make_async_remote_copy(
                src_ref=src, dst_ref=dst.at[off - 1], send_sem=sems.at[0, off - 1],
                recv_sem=sems.at[1, off - 1], device_id=(dest, z, t), device_id_type=mesh_ids)
            copy.start()
            gathered.append(copy)
    for copy in gathered:
        copy.wait()
    own_stats.wait()

    peaks = [got_stats[na - 1, 0]] + [got_stats[off - 1, 0] for off in range(1, na)]
    sums = [got_stats[na - 1, 1]] + [got_stats[off - 1, 1] for off in range(1, na)]
    top = peaks[0]
    for peak in peaks[1:]:
        top = jnp.maximum(top, peak)
    factors = [jnp.exp(peak - top) for peak in peaks]
    totals = factors[0] * sums[0]
    for factor, part_sum in zip(factors[1:], sums[1:]):
        totals = totals + factor * part_sum
    for h in range(heads):
        numerator = parts_ref[h, a].astype(jnp.float32) * factors[0][h][:, None]
        for off in range(1, na):
            numerator = numerator + (
                got_parts[off - 1, h].astype(jnp.float32) * factors[off][h][:, None]
            )
        att_buf[:, pl.ds(h * HD, HD)] = (numerator / totals[h][:, None]).astype(jnp.bfloat16)

    for j in range(n_hi):
        their = pl.multiple_of((j * 2 + 1 - core) * rows, rows)
        mine = pl.multiple_of((j * 2 + core) * rows, rows)
        pick[0, pl.ds(j * rows, rows), :] = att_buf[pl.ds(their, rows), :]
        pick[1, pl.ds(j * rows, rows), :] = att_buf[pl.ds(mine, rows), :]
    send1[...] = jnp.dot(pick[0], w_ref[...], preferred_element_type=jnp.float32).astype(
        jnp.bfloat16)
    first = pltpu.make_async_remote_copy(
        src_ref=send1, dst_ref=recv1, send_sem=sems1.at[0], recv_sem=sems1.at[1],
        device_id=partner, device_id_type=mesh_ids)
    first.start()
    total[...] = jnp.dot(pick[1], w_ref[...], preferred_element_type=jnp.float32).astype(
        jnp.bfloat16).astype(jnp.float32)
    first.wait()
    for j in range(n_hi):
        block = pl.ds(j * rows, rows)
        send2[j] = (total[block, :] + recv1[block, :].astype(jnp.float32)).astype(jnp.bfloat16)
    second = []
    for off in range(1, n_hi):
        dest = lax.rem(hi + off, n_hi)
        copy = pltpu.make_async_remote_copy(
            src_ref=send2.at[dest], dst_ref=recv2.at[off - 1], send_sem=send_sems2.at[off - 1],
            recv_sem=recv_sems2.at[off - 1], device_id=(a, z, dest * 2 + core),
            device_id_type=mesh_ids)
        copy.start()
        second.append(copy)
    own_rows = pl.ds(pl.multiple_of(hi * rows, rows), rows)
    own = total[own_rows, :] + recv1[own_rows, :].astype(jnp.float32)
    for copy in second:
        copy.wait()
    for off in range(1, n_hi):
        own = own + recv2[off - 1].astype(jnp.float32)
    out_ref[...] = own.astype(out_ref.dtype)


def project(parts, stats, out_weight, tp_count):
    heads, na, block_rows, _ = parts.shape
    n_hi = tp_count // 2
    rows = block_rows // tp_count
    cols = out_weight.shape[1]
    vmem = pl.BlockSpec(memory_space=pltpu.VMEM)
    return pl.pallas_call(
        functools.partial(project_kernel, na, n_hi),
        out_shape=jax.ShapeDtypeStruct((rows, cols), jnp.bfloat16),
        in_specs=[vmem, vmem, vmem],
        out_specs=vmem,
        scratch_shapes=[
            pltpu.VMEM((na - 1, heads, block_rows, HD), parts.dtype),
            pltpu.VMEM((na, 2, heads, block_rows), stats.dtype),
            pltpu.VMEM((block_rows, heads * HD), jnp.bfloat16),
            pltpu.VMEM((2, n_hi * rows, heads * HD), jnp.bfloat16),
            pltpu.VMEM((n_hi * rows, cols), jnp.bfloat16),
            pltpu.VMEM((n_hi * rows, cols), jnp.bfloat16),
            pltpu.VMEM((n_hi * rows, cols), jnp.float32),
            pltpu.VMEM((n_hi, rows, cols), jnp.bfloat16),
            pltpu.VMEM((n_hi - 1, rows, cols), jnp.bfloat16),
            pltpu.SemaphoreType.DMA((2, na - 1)),
            pltpu.SemaphoreType.DMA((2, na - 1)),
            pltpu.SemaphoreType.DMA((2,)),
            pltpu.SemaphoreType.DMA((n_hi - 1,)),
            pltpu.SemaphoreType.DMA((n_hi - 1,)),
            pltpu.SemaphoreType.DMA(()),
        ],
        compiler_params=pltpu.CompilerParams(collective_id=1, has_side_effects=True),
    )(parts, stats, out_weight)


def local(query_vectors, key_vectors, value_vectors, out_weight):
    score_scale = 1.0 / math.sqrt(HD)
    tp_count = lax.axis_size("tp")
    ca_count = lax.axis_size("ca")
    token_rows = query_vectors.shape[0]
    own_heads = query_vectors.shape[1] // HD // tp_count
    own_cols = own_heads * HD

    block_rows = token_rows * tp_count
    query_heads, kv = exchange(
        query_vectors, key_vectors, value_vectors, ca_count, lax.axis_size("cz"), tp_count)
    query_heads = query_heads.reshape(own_heads, -1, HD)
    kv = kv.reshape(2, own_heads, -1, HD)

    row_peak, row_total, weighted = attend_local(query_heads, kv[0], kv[1], score_scale)
    stats = jnp.stack([row_peak, row_total], axis=0).reshape(2, own_heads, ca_count, block_rows)
    parts = weighted.astype(jnp.bfloat16).reshape(own_heads, ca_count, block_rows, HD)
    return project(parts, stats, out_weight, tp_count)


def solution(mesh):
    ctx_count, tp_count = mesh.devices.shape
    split_mesh = Mesh(
        mesh.devices.reshape(ctx_count // KEY_SPLIT, KEY_SPLIT, tp_count), ("ca", "cz", "tp")
    )
    rows = P(("ca", "cz", "tp"), None)
    return jax.shard_map(
        local,
        mesh=split_mesh,
        in_specs=(rows, rows, rows, P("tp", None)),
        out_specs=rows,
        check_vma=False,
    )
```

```python
import functools
import math

import jax
import jax.numpy as jnp
from jax import lax
from jax.sharding import Mesh
from jax.sharding import PartitionSpec as P
from jax.experimental import pallas as pl
from jax.experimental.pallas import tpu as pltpu

HD = 128
KEY_SPLIT = 8


def attend_local(query_heads, key_heads, value_heads, score_scale):
    scores = (
        jnp.einsum("hid,hjd->hij", query_heads, key_heads, preferred_element_type=jnp.float32)
        * score_scale
    )
    row_peak = jnp.max(scores, axis=-1)
    weights_low = jnp.exp(scores - row_peak[..., None]).astype(jnp.bfloat16)
    row_total = jnp.sum(weights_low.astype(jnp.float32), axis=-1)
    weighted = jnp.einsum(
        "hij,hjd->hid", weights_low, value_heads, preferred_element_type=jnp.float32
    )
    return row_peak, row_total, weighted


def gather_by_exchange(block, axis_name):
    count = lax.axis_size(axis_name)
    spread = jnp.broadcast_to(block[None], (count,) + block.shape)
    return lax.all_to_all(spread, axis_name, 0, 0, tiled=True)


def exchange_kernel(na, nz, nt, q_ref, k_ref, v_ref, q_out, kv_out, spread_sems, own_sems,
                    q_sems, r_sems, l_sems):
    mesh_ids = pl.DeviceIdType.MESH
    a = lax.axis_index("ca")
    z = lax.axis_index("cz")
    t = lax.axis_index("tp")
    right = lax.rem(z + 1, nz)
    left = lax.rem(z + nz - 1, nz)
    rows = q_ref.shape[0]
    heads = q_out.shape[0]

    barrier = pltpu.get_barrier_semaphore()
    for off in range(1, nt):
        pl.semaphore_signal(barrier, inc=1, device_id=(a, z, lax.rem(t + off, nt)),
                            device_id_type=mesh_ids)
    for off in range(1, na):
        pl.semaphore_signal(barrier, inc=1, device_id=(lax.rem(a + off, na), z, t),
                            device_id_type=mesh_ids)
    for side in (left, right):
        pl.semaphore_signal(barrier, inc=1, device_id=(a, side, t), device_id_type=mesh_ids)
    pl.semaphore_wait(barrier, nt - 1 + na - 1 + 2)

    mine = pl.ds(pl.multiple_of(t * rows, rows), rows)
    sources = (q_ref, k_ref, v_ref)

    def target(i, h):
        if i == 0:
            return q_out.at[h, a, mine]
        return kv_out.at[i - 1, h, z, mine]

    def columns(dest, h):
        return pl.ds(pl.multiple_of((dest * heads + h) * HD, HD), HD)

    own = []
    for i in range(3):
        for h in range(heads):
            copy = pltpu.make_async_copy(
                sources[i].at[:, columns(t, h)], target(i, h), own_sems.at[i, h])
            copy.start()
            own.append(copy)
    spread = []
    for off in range(1, nt):
        dest = lax.rem(t + off, nt)
        for i in range(3):
            for h in range(heads):
                spread.append(pltpu.make_async_remote_copy(
                    src_ref=sources[i].at[:, columns(dest, h)], dst_ref=target(i, h),
                    send_sem=spread_sems.at[0, i, h, off - 1],
                    recv_sem=spread_sems.at[1, i, h, off - 1],
                    device_id=(a, z, dest), device_id_type=mesh_ids))
    for copy in spread:
        copy.start()
    for copy in spread:
        copy.wait()
    for copy in own:
        copy.wait()

    q_copies = []
    for off in range(1, na):
        copy = pltpu.make_async_remote_copy(
            src_ref=q_out.at[:, a], dst_ref=q_out.at[:, a], send_sem=q_sems.at[0, off - 1],
            recv_sem=q_sems.at[1, off - 1], device_id=(lax.rem(a + off, na), z, t),
            device_id_type=mesh_ids)
        copy.start()
        q_copies.append(copy)

    n_right = nz // 2
    n_left = (nz - 1) // 2
    chains = ((right, n_right, r_sems, -1, []), (left, n_left, l_sems, 1, []))
    for step in range(n_right):
        for part in range(2):
            for side, count, sems, sign, copies in chains:
                if step >= count:
                    continue
                slot = lax.rem(z + sign * step + nz, nz)
                if step > 0:
                    copies[(step - 1) * 2 + part].wait_recv()
                copy = pltpu.make_async_remote_copy(
                    src_ref=kv_out.at[part, :, slot], dst_ref=kv_out.at[part, :, slot],
                    send_sem=sems.at[0, step * 2 + part], recv_sem=sems.at[1, step * 2 + part],
                    device_id=(a, side, t), device_id_type=mesh_ids)
                copy.start()
                copies.append(copy)
    for side, count, sems, sign, copies in chains:
        copies[-2].wait_recv()
        copies[-1].wait_recv()
        for copy in copies:
            copy.wait_send()
    for copy in q_copies:
        copy.wait()


def exchange(query_vectors, key_vectors, value_vectors, na, nz, nt):
    rows, width = query_vectors.shape
    heads = width // nt // HD
    n_right = nz // 2
    n_left = (nz - 1) // 2
    dtype = query_vectors.dtype
    return pl.pallas_call(
        functools.partial(exchange_kernel, na, nz, nt),
        out_shape=(
            jax.ShapeDtypeStruct((heads, na, nt * rows, HD), dtype),
            jax.ShapeDtypeStruct((2, heads, nz, nt * rows, HD), dtype),
        ),
        in_specs=[pl.BlockSpec(memory_space=pl.ANY)] * 3,
        out_specs=(pl.BlockSpec(memory_space=pl.ANY), pl.BlockSpec(memory_space=pl.ANY)),
        scratch_shapes=[
            pltpu.SemaphoreType.DMA((2, 3, heads, nt - 1)),
            pltpu.SemaphoreType.DMA((3, heads)),
            pltpu.SemaphoreType.DMA((2, na - 1)),
            pltpu.SemaphoreType.DMA((2, 2 * n_right)),
            pltpu.SemaphoreType.DMA((2, 2 * n_left)),
        ],
        compiler_params=pltpu.CompilerParams(collective_id=0, has_side_effects=True),
    )(query_vectors, key_vectors, value_vectors)


def project_kernel(na, n_hi, parts_ref, stats_ref, w_ref, out_ref, got_parts, got_stats, att_buf,
                   pick, send1, recv1, total, send2, recv2, relay_in, far_in, part_sems, stat_sems,
                   sems1, direct_sems, relay_sems, onward_sems, own_stat_sem):
    mesh_ids = pl.DeviceIdType.MESH
    a = lax.axis_index("ca")
    z = lax.axis_index("cz")
    t = lax.axis_index("tp")
    core = lax.rem(t, 2)
    hi = t // 2
    partner = (a, z, hi * 2 + 1 - core)
    rows = send2.shape[1]
    heads = parts_ref.shape[0]

    barrier = pltpu.get_barrier_semaphore()
    for off in range(1, na):
        pl.semaphore_signal(barrier, inc=1, device_id=(lax.rem(a + off, na), z, t),
                            device_id_type=mesh_ids)
    pl.semaphore_signal(barrier, inc=1, device_id=partner, device_id_type=mesh_ids)
    for off in range(1, n_hi):
        pl.semaphore_signal(barrier, inc=1, device_id=(a, z, lax.rem(hi + off, n_hi) * 2 + core),
                            device_id_type=mesh_ids)
    pl.semaphore_wait(barrier, na - 1 + n_hi)

    own_stats = pltpu.make_async_copy(stats_ref.at[:, :, a], got_stats.at[na - 1], own_stat_sem)
    own_stats.start()
    gathered = []
    for off in range(1, na):
        dest = lax.rem(a + off, na)
        for src, dst, sems in ((parts_ref.at[:, dest], got_parts, part_sems),
                               (stats_ref.at[:, :, dest], got_stats, stat_sems)):
            copy = pltpu.make_async_remote_copy(
                src_ref=src, dst_ref=dst.at[off - 1], send_sem=sems.at[0, off - 1],
                recv_sem=sems.at[1, off - 1], device_id=(dest, z, t), device_id_type=mesh_ids)
            copy.start()
            gathered.append(copy)
    for copy in gathered:
        copy.wait()
    own_stats.wait()

    peaks = [got_stats[na - 1, 0]] + [got_stats[off - 1, 0] for off in range(1, na)]
    sums = [got_stats[na - 1, 1]] + [got_stats[off - 1, 1] for off in range(1, na)]
    top = peaks[0]
    for peak in peaks[1:]:
        top = jnp.maximum(top, peak)
    factors = [jnp.exp(peak - top) for peak in peaks]
    totals = factors[0] * sums[0]
    for factor, part_sum in zip(factors[1:], sums[1:]):
        totals = totals + factor * part_sum
    for h in range(heads):
        numerator = parts_ref[h, a].astype(jnp.float32) * factors[0][h][:, None]
        for off in range(1, na):
            numerator = numerator + (
                got_parts[off - 1, h].astype(jnp.float32) * factors[off][h][:, None]
            )
        att_buf[:, pl.ds(h * HD, HD)] = (numerator / totals[h][:, None]).astype(jnp.bfloat16)

    for j in range(n_hi):
        their = pl.multiple_of((j * 2 + 1 - core) * rows, rows)
        mine = pl.multiple_of((j * 2 + core) * rows, rows)
        pick[0, pl.ds(j * rows, rows), :] = att_buf[pl.ds(their, rows), :]
        pick[1, pl.ds(j * rows, rows), :] = att_buf[pl.ds(mine, rows), :]
    send1[...] = jnp.dot(pick[0], w_ref[...], preferred_element_type=jnp.float32).astype(
        jnp.bfloat16)
    first = pltpu.make_async_remote_copy(
        src_ref=send1, dst_ref=recv1, send_sem=sems1.at[0], recv_sem=sems1.at[1],
        device_id=partner, device_id_type=mesh_ids)
    first.start()
    total[...] = jnp.dot(pick[1], w_ref[...], preferred_element_type=jnp.float32).astype(
        jnp.bfloat16).astype(jnp.float32)
    first.wait()
    for j in range(n_hi):
        block = pl.ds(j * rows, rows)
        send2[j] = (total[block, :] + recv1[block, :].astype(jnp.float32)).astype(jnp.bfloat16)
    half = send2.shape[2] // 2
    up = lax.rem(hi + 1, n_hi)
    down = lax.rem(hi + n_hi - 1, n_hi)
    far = lax.rem(hi + 2, n_hi)

    def to(dest):
        return (a, z, dest * 2 + core)

    def remote(src_ref, dst_ref, sems, slot, dest):
        copy = pltpu.make_async_remote_copy(
            src_ref=src_ref, dst_ref=dst_ref, send_sem=sems.at[0, slot],
            recv_sem=sems.at[1, slot], device_id=to(dest), device_id_type=mesh_ids)
        copy.start()
        return copy

    direct = [
        remote(send2.at[up], recv2.at[0], direct_sems, 0, up),
        remote(send2.at[down], recv2.at[1], direct_sems, 1, down),
    ]
    relay = [
        remote(send2.at[far, :, pl.ds(0, half)], relay_in.at[0], relay_sems, 0, up),
        remote(send2.at[far, :, pl.ds(half, half)], relay_in.at[1], relay_sems, 1, down),
    ]
    relay[0].wait_recv()
    onward = [remote(relay_in.at[0], far_in.at[0], onward_sems, 0, up)]
    relay[1].wait_recv()
    onward.append(remote(relay_in.at[1], far_in.at[1], onward_sems, 1, down))
    own_rows = pl.ds(pl.multiple_of(hi * rows, rows), rows)
    own = total[own_rows, :] + recv1[own_rows, :].astype(jnp.float32)
    for copy in direct + onward:
        copy.wait()
    for copy in relay:
        copy.wait_send()
    own = own + recv2[0].astype(jnp.float32) + recv2[1].astype(jnp.float32)
    own = own + jnp.concatenate([far_in[0], far_in[1]], axis=1).astype(jnp.float32)
    out_ref[...] = own.astype(out_ref.dtype)


def project(parts, stats, out_weight, tp_count):
    heads, na, block_rows, _ = parts.shape
    n_hi = tp_count // 2
    rows = block_rows // tp_count
    cols = out_weight.shape[1]
    vmem = pl.BlockSpec(memory_space=pltpu.VMEM)
    return pl.pallas_call(
        functools.partial(project_kernel, na, n_hi),
        out_shape=jax.ShapeDtypeStruct((rows, cols), jnp.bfloat16),
        in_specs=[vmem, vmem, vmem],
        out_specs=vmem,
        scratch_shapes=[
            pltpu.VMEM((na - 1, heads, block_rows, HD), parts.dtype),
            pltpu.VMEM((na, 2, heads, block_rows), stats.dtype),
            pltpu.VMEM((block_rows, heads * HD), jnp.bfloat16),
            pltpu.VMEM((2, n_hi * rows, heads * HD), jnp.bfloat16),
            pltpu.VMEM((n_hi * rows, cols), jnp.bfloat16),
            pltpu.VMEM((n_hi * rows, cols), jnp.bfloat16),
            pltpu.VMEM((n_hi * rows, cols), jnp.float32),
            pltpu.VMEM((n_hi, rows, cols), jnp.bfloat16),
            pltpu.VMEM((2, rows, cols), jnp.bfloat16),
            pltpu.VMEM((2, rows, cols // 2), jnp.bfloat16),
            pltpu.VMEM((2, rows, cols // 2), jnp.bfloat16),
            pltpu.SemaphoreType.DMA((2, na - 1)),
            pltpu.SemaphoreType.DMA((2, na - 1)),
            pltpu.SemaphoreType.DMA((2,)),
            pltpu.SemaphoreType.DMA((2, 2)),
            pltpu.SemaphoreType.DMA((2, 2)),
            pltpu.SemaphoreType.DMA((2, 2)),
            pltpu.SemaphoreType.DMA(()),
        ],
        compiler_params=pltpu.CompilerParams(collective_id=1, has_side_effects=True),
    )(parts, stats, out_weight)


def local(query_vectors, key_vectors, value_vectors, out_weight):
    score_scale = 1.0 / math.sqrt(HD)
    tp_count = lax.axis_size("tp")
    ca_count = lax.axis_size("ca")
    token_rows = query_vectors.shape[0]
    own_heads = query_vectors.shape[1] // HD // tp_count
    own_cols = own_heads * HD

    block_rows = token_rows * tp_count
    query_heads, kv = exchange(
        query_vectors, key_vectors, value_vectors, ca_count, lax.axis_size("cz"), tp_count)
    query_heads = query_heads.reshape(own_heads, -1, HD)
    kv = kv.reshape(2, own_heads, -1, HD)

    row_peak, row_total, weighted = attend_local(query_heads, kv[0], kv[1], score_scale)
    stats = jnp.stack([row_peak, row_total], axis=0).reshape(2, own_heads, ca_count, block_rows)
    parts = weighted.astype(jnp.bfloat16).reshape(own_heads, ca_count, block_rows, HD)
    return project(parts, stats, out_weight, tp_count)


def solution(mesh):
    ctx_count, tp_count = mesh.devices.shape
    split_mesh = Mesh(
        mesh.devices.reshape(ctx_count // KEY_SPLIT, KEY_SPLIT, tp_count), ("ca", "cz", "tp")
    )
    rows = P(("ca", "cz", "tp"), None)
    return jax.shard_map(
        local,
        mesh=split_mesh,
        in_specs=(rows, rows, rows, P("tp", None)),
        out_specs=rows,
        check_vma=False,
    )
```

```python
import functools
import math

import jax
import jax.numpy as jnp
from jax import lax
from jax.sharding import Mesh
from jax.sharding import PartitionSpec as P
from jax.experimental import pallas as pl
from jax.experimental.pallas import tpu as pltpu

HD = 128
KEY_SPLIT = 8


def attend_local(query_heads, key_heads, value_heads, score_scale):
    scores = (
        jnp.einsum("hid,hjd->hij", query_heads, key_heads, preferred_element_type=jnp.float32)
        * score_scale
    )
    row_peak = jnp.max(scores, axis=-1)
    weights_low = jnp.exp(scores - row_peak[..., None]).astype(jnp.bfloat16)
    row_total = jnp.sum(weights_low.astype(jnp.float32), axis=-1)
    weighted = jnp.einsum(
        "hij,hjd->hid", weights_low, value_heads, preferred_element_type=jnp.float32
    )
    return row_peak, row_total, weighted


def gather_by_exchange(block, axis_name):
    count = lax.axis_size(axis_name)
    spread = jnp.broadcast_to(block[None], (count,) + block.shape)
    return lax.all_to_all(spread, axis_name, 0, 0, tiled=True)


def exchange_kernel(na, nz, nt, q_ref, k_ref, v_ref, q_out, kv_out, spread_sems, own_sems,
                    q_sems, r_sems, l_sems):
    mesh_ids = pl.DeviceIdType.MESH
    a = lax.axis_index("ca")
    z = lax.axis_index("cz")
    t = lax.axis_index("tp")
    right = lax.rem(z + 1, nz)
    left = lax.rem(z + nz - 1, nz)
    rows = q_ref.shape[0]
    heads = q_out.shape[0]

    barrier = pltpu.get_barrier_semaphore()
    for off in range(1, nt):
        pl.semaphore_signal(barrier, inc=1, device_id=(a, z, lax.rem(t + off, nt)),
                            device_id_type=mesh_ids)
    for off in range(1, na):
        pl.semaphore_signal(barrier, inc=1, device_id=(lax.rem(a + off, na), z, t),
                            device_id_type=mesh_ids)
    for side in (left, right):
        pl.semaphore_signal(barrier, inc=1, device_id=(a, side, t), device_id_type=mesh_ids)
    pl.semaphore_wait(barrier, nt - 1 + na - 1 + 2)

    mine = pl.ds(pl.multiple_of(t * rows, rows), rows)
    sources = (q_ref, k_ref, v_ref)

    def target(i, h):
        if i == 0:
            return q_out.at[h, a, mine]
        return kv_out.at[i - 1, h, z, mine]

    def columns(dest, h):
        return pl.ds(pl.multiple_of((dest * heads + h) * HD, HD), HD)

    own = []
    for i in range(3):
        for h in range(heads):
            copy = pltpu.make_async_copy(
                sources[i].at[:, columns(t, h)], target(i, h), own_sems.at[i, h])
            copy.start()
            own.append(copy)
    spread = []
    for off in range(1, nt):
        dest = lax.rem(t + off, nt)
        for i in range(3):
            for h in range(heads):
                spread.append(pltpu.make_async_remote_copy(
                    src_ref=sources[i].at[:, columns(dest, h)], dst_ref=target(i, h),
                    send_sem=spread_sems.at[0, i, h, off - 1],
                    recv_sem=spread_sems.at[1, i, h, off - 1],
                    device_id=(a, z, dest), device_id_type=mesh_ids))
    for copy in spread:
        copy.start()
    for copy in spread:
        copy.wait()
    for copy in own:
        copy.wait()

    q_copies = []
    for off in range(1, na):
        copy = pltpu.make_async_remote_copy(
            src_ref=q_out.at[:, a], dst_ref=q_out.at[:, a], send_sem=q_sems.at[0, off - 1],
            recv_sem=q_sems.at[1, off - 1], device_id=(lax.rem(a + off, na), z, t),
            device_id_type=mesh_ids)
        copy.start()
        q_copies.append(copy)

    n_right = nz // 2
    n_left = (nz - 1) // 2
    chains = ((right, n_right, r_sems, -1, []), (left, n_left, l_sems, 1, []))
    pieces = 2 * heads
    for step in range(n_right):
        for part in range(2):
            for h in range(heads):
                piece = part * heads + h
                for side, count, sems, sign, copies in chains:
                    if step >= count:
                        continue
                    slot = lax.rem(z + sign * step + nz, nz)
                    if step > 0:
                        copies[(step - 1) * pieces + piece].wait_recv()
                    copy = pltpu.make_async_remote_copy(
                        src_ref=kv_out.at[part, h, slot], dst_ref=kv_out.at[part, h, slot],
                        send_sem=sems.at[0, step * pieces + piece],
                        recv_sem=sems.at[1, step * pieces + piece],
                        device_id=(a, side, t), device_id_type=mesh_ids)
                    copy.start()
                    copies.append(copy)
    for side, count, sems, sign, copies in chains:
        for copy in copies[-pieces:]:
            copy.wait_recv()
        for copy in copies:
            copy.wait_send()
    for copy in q_copies:
        copy.wait()


def exchange(query_vectors, key_vectors, value_vectors, na, nz, nt):
    rows, width = query_vectors.shape
    heads = width // nt // HD
    n_right = nz // 2
    n_left = (nz - 1) // 2
    dtype = query_vectors.dtype
    return pl.pallas_call(
        functools.partial(exchange_kernel, na, nz, nt),
        out_shape=(
            jax.ShapeDtypeStruct((heads, na, nt * rows, HD), dtype),
            jax.ShapeDtypeStruct((2, heads, nz, nt * rows, HD), dtype),
        ),
        in_specs=[pl.BlockSpec(memory_space=pl.ANY)] * 3,
        out_specs=(pl.BlockSpec(memory_space=pl.ANY), pl.BlockSpec(memory_space=pl.ANY)),
        scratch_shapes=[
            pltpu.SemaphoreType.DMA((2, 3, heads, nt - 1)),
            pltpu.SemaphoreType.DMA((3, heads)),
            pltpu.SemaphoreType.DMA((2, na - 1)),
            pltpu.SemaphoreType.DMA((2, 2 * heads * n_right)),
            pltpu.SemaphoreType.DMA((2, 2 * heads * n_left)),
        ],
        compiler_params=pltpu.CompilerParams(collective_id=0, has_side_effects=True),
    )(query_vectors, key_vectors, value_vectors)


def project_kernel(na, n_hi, parts_ref, stats_ref, w_ref, out_ref, got_parts, got_stats, att_buf,
                   pick, send1, recv1, total, send2, recv2, part_sems, stat_sems, sems1, send_sems2,
                   recv_sems2, own_stat_sem):
    mesh_ids = pl.DeviceIdType.MESH
    a = lax.axis_index("ca")
    z = lax.axis_index("cz")
    t = lax.axis_index("tp")
    core = lax.rem(t, 2)
    hi = t // 2
    partner = (a, z, hi * 2 + 1 - core)
    rows = send2.shape[1]
    heads = parts_ref.shape[0]

    barrier = pltpu.get_barrier_semaphore()
    for off in range(1, na):
        pl.semaphore_signal(barrier, inc=1, device_id=(lax.rem(a + off, na), z, t),
                            device_id_type=mesh_ids)
    pl.semaphore_signal(barrier, inc=1, device_id=partner, device_id_type=mesh_ids)
    for off in range(1, n_hi):
        pl.semaphore_signal(barrier, inc=1, device_id=(a, z, lax.rem(hi + off, n_hi) * 2 + core),
                            device_id_type=mesh_ids)
    pl.semaphore_wait(barrier, na - 1 + n_hi)

    own_stats = pltpu.make_async_copy(stats_ref.at[:, :, a], got_stats.at[na - 1], own_stat_sem)
    own_stats.start()
    gathered = []
    for off in range(1, na):
        dest = lax.rem(a + off, na)
        for src, dst, sems in ((parts_ref.at[:, dest], got_parts, part_sems),
                               (stats_ref.at[:, :, dest], got_stats, stat_sems)):
            copy = pltpu.make_async_remote_copy(
                src_ref=src, dst_ref=dst.at[off - 1], send_sem=sems.at[0, off - 1],
                recv_sem=sems.at[1, off - 1], device_id=(dest, z, t), device_id_type=mesh_ids)
            copy.start()
            gathered.append(copy)
    for copy in gathered:
        copy.wait()
    own_stats.wait()

    peaks = [got_stats[na - 1, 0]] + [got_stats[off - 1, 0] for off in range(1, na)]
    sums = [got_stats[na - 1, 1]] + [got_stats[off - 1, 1] for off in range(1, na)]
    top = peaks[0]
    for peak in peaks[1:]:
        top = jnp.maximum(top, peak)
    factors = [jnp.exp(peak - top) for peak in peaks]
    totals = factors[0] * sums[0]
    for factor, part_sum in zip(factors[1:], sums[1:]):
        totals = totals + factor * part_sum
    for h in range(heads):
        numerator = parts_ref[h, a].astype(jnp.float32) * factors[0][h][:, None]
        for off in range(1, na):
            numerator = numerator + (
                got_parts[off - 1, h].astype(jnp.float32) * factors[off][h][:, None]
            )
        att_buf[:, pl.ds(h * HD, HD)] = (numerator / totals[h][:, None]).astype(jnp.bfloat16)

    for j in range(n_hi):
        their = pl.multiple_of((j * 2 + 1 - core) * rows, rows)
        mine = pl.multiple_of((j * 2 + core) * rows, rows)
        pick[0, pl.ds(j * rows, rows), :] = att_buf[pl.ds(their, rows), :]
        pick[1, pl.ds(j * rows, rows), :] = att_buf[pl.ds(mine, rows), :]
    send1[...] = jnp.dot(pick[0], w_ref[...], preferred_element_type=jnp.float32).astype(
        jnp.bfloat16)
    first = pltpu.make_async_remote_copy(
        src_ref=send1, dst_ref=recv1, send_sem=sems1.at[0], recv_sem=sems1.at[1],
        device_id=partner, device_id_type=mesh_ids)
    first.start()
    total[...] = jnp.dot(pick[1], w_ref[...], preferred_element_type=jnp.float32).astype(
        jnp.bfloat16).astype(jnp.float32)
    first.wait()
    for j in range(n_hi):
        block = pl.ds(j * rows, rows)
        send2[j] = (total[block, :] + recv1[block, :].astype(jnp.float32)).astype(jnp.bfloat16)
    second = []
    for off in range(1, n_hi):
        dest = lax.rem(hi + off, n_hi)
        copy = pltpu.make_async_remote_copy(
            src_ref=send2.at[dest], dst_ref=recv2.at[off - 1], send_sem=send_sems2.at[off - 1],
            recv_sem=recv_sems2.at[off - 1], device_id=(a, z, dest * 2 + core),
            device_id_type=mesh_ids)
        copy.start()
        second.append(copy)
    own_rows = pl.ds(pl.multiple_of(hi * rows, rows), rows)
    own = total[own_rows, :] + recv1[own_rows, :].astype(jnp.float32)
    for copy in second:
        copy.wait()
    for off in range(1, n_hi):
        own = own + recv2[off - 1].astype(jnp.float32)
    out_ref[...] = own.astype(out_ref.dtype)


def project(parts, stats, out_weight, tp_count):
    heads, na, block_rows, _ = parts.shape
    n_hi = tp_count // 2
    rows = block_rows // tp_count
    cols = out_weight.shape[1]
    vmem = pl.BlockSpec(memory_space=pltpu.VMEM)
    return pl.pallas_call(
        functools.partial(project_kernel, na, n_hi),
        out_shape=jax.ShapeDtypeStruct((rows, cols), jnp.bfloat16),
        in_specs=[vmem, vmem, vmem],
        out_specs=vmem,
        scratch_shapes=[
            pltpu.VMEM((na - 1, heads, block_rows, HD), parts.dtype),
            pltpu.VMEM((na, 2, heads, block_rows), stats.dtype),
            pltpu.VMEM((block_rows, heads * HD), jnp.bfloat16),
            pltpu.VMEM((2, n_hi * rows, heads * HD), jnp.bfloat16),
            pltpu.VMEM((n_hi * rows, cols), jnp.bfloat16),
            pltpu.VMEM((n_hi * rows, cols), jnp.bfloat16),
            pltpu.VMEM((n_hi * rows, cols), jnp.float32),
            pltpu.VMEM((n_hi, rows, cols), jnp.bfloat16),
            pltpu.VMEM((n_hi - 1, rows, cols), jnp.bfloat16),
            pltpu.SemaphoreType.DMA((2, na - 1)),
            pltpu.SemaphoreType.DMA((2, na - 1)),
            pltpu.SemaphoreType.DMA((2,)),
            pltpu.SemaphoreType.DMA((n_hi - 1,)),
            pltpu.SemaphoreType.DMA((n_hi - 1,)),
            pltpu.SemaphoreType.DMA(()),
        ],
        compiler_params=pltpu.CompilerParams(collective_id=1, has_side_effects=True),
    )(parts, stats, out_weight)


def local(query_vectors, key_vectors, value_vectors, out_weight):
    score_scale = 1.0 / math.sqrt(HD)
    tp_count = lax.axis_size("tp")
    ca_count = lax.axis_size("ca")
    token_rows = query_vectors.shape[0]
    own_heads = query_vectors.shape[1] // HD // tp_count
    own_cols = own_heads * HD

    block_rows = token_rows * tp_count
    query_heads, kv = exchange(
        query_vectors, key_vectors, value_vectors, ca_count, lax.axis_size("cz"), tp_count)
    query_heads = query_heads.reshape(own_heads, -1, HD)
    kv = kv.reshape(2, own_heads, -1, HD)

    row_peak, row_total, weighted = attend_local(query_heads, kv[0], kv[1], score_scale)
    stats = jnp.stack([row_peak, row_total], axis=0).reshape(2, own_heads, ca_count, block_rows)
    parts = weighted.astype(jnp.bfloat16).reshape(own_heads, ca_count, block_rows, HD)
    return project(parts, stats, out_weight, tp_count)


def solution(mesh):
    ctx_count, tp_count = mesh.devices.shape
    split_mesh = Mesh(
        mesh.devices.reshape(ctx_count // KEY_SPLIT, KEY_SPLIT, tp_count), ("ca", "cz", "tp")
    )
    rows = P(("ca", "cz", "tp"), None)
    return jax.shard_map(
        local,
        mesh=split_mesh,
        in_specs=(rows, rows, rows, P("tp", None)),
        out_specs=rows,
        check_vma=False,
    )
```

```python
import functools
import math

import jax
import jax.numpy as jnp
from jax import lax
from jax.sharding import Mesh
from jax.sharding import PartitionSpec as P
from jax.experimental import pallas as pl
from jax.experimental.pallas import tpu as pltpu

HD = 128
KEY_SPLIT = 8


def attend_local(query_heads, key_heads, value_heads, score_scale):
    scores = (
        jnp.einsum("hid,hjd->hij", query_heads, key_heads, preferred_element_type=jnp.float32)
        * score_scale
    )
    row_peak = jnp.max(scores, axis=-1)
    weights_low = jnp.exp(scores - row_peak[..., None]).astype(jnp.bfloat16)
    row_total = jnp.sum(weights_low.astype(jnp.float32), axis=-1)
    weighted = jnp.einsum(
        "hij,hjd->hid", weights_low, value_heads, preferred_element_type=jnp.float32
    )
    return row_peak, row_total, weighted


def gather_by_exchange(block, axis_name):
    count = lax.axis_size(axis_name)
    spread = jnp.broadcast_to(block[None], (count,) + block.shape)
    return lax.all_to_all(spread, axis_name, 0, 0, tiled=True)


def exchange_kernel(na, nz, nt, q_ref, k_ref, v_ref, q_out, k_out, v_out, spread_sems,
                    own_sems, q_sems, r_sems, l_sems):
    mesh_ids = pl.DeviceIdType.MESH
    a = lax.axis_index("ca")
    z = lax.axis_index("cz")
    t = lax.axis_index("tp")
    right = lax.rem(z + 1, nz)
    left = lax.rem(z + nz - 1, nz)
    rows = q_ref.shape[0]
    heads = q_out.shape[0]

    barrier = pltpu.get_barrier_semaphore()
    for off in range(1, nt):
        pl.semaphore_signal(barrier, inc=1, device_id=(a, z, lax.rem(t + off, nt)),
                            device_id_type=mesh_ids)
    for off in range(1, na):
        pl.semaphore_signal(barrier, inc=1, device_id=(lax.rem(a + off, na), z, t),
                            device_id_type=mesh_ids)
    for side in (left, right):
        pl.semaphore_signal(barrier, inc=1, device_id=(a, side, t), device_id_type=mesh_ids)
    pl.semaphore_wait(barrier, nt - 1 + na - 1 + 2)

    mine = pl.ds(pl.multiple_of(t * rows, rows), rows)
    sources = (q_ref, k_ref, v_ref)

    def target(i, h):
        if i == 0:
            return q_out.at[h, a, mine]
        return (k_out, v_out)[i - 1].at[h, z, mine]

    def columns(dest, h):
        return pl.ds(pl.multiple_of((dest * heads + h) * HD, HD), HD)

    own = []
    for i in range(3):
        for h in range(heads):
            copy = pltpu.make_async_copy(
                sources[i].at[:, columns(t, h)], target(i, h), own_sems.at[i, h])
            copy.start()
            own.append(copy)
    spread = []
    for off in range(1, nt):
        dest = lax.rem(t + off, nt)
        for i in range(3):
            for h in range(heads):
                spread.append(pltpu.make_async_remote_copy(
                    src_ref=sources[i].at[:, columns(dest, h)], dst_ref=target(i, h),
                    send_sem=spread_sems.at[0, i, h, off - 1],
                    recv_sem=spread_sems.at[1, i, h, off - 1],
                    device_id=(a, z, dest), device_id_type=mesh_ids))
    for copy in spread:
        copy.start()
    for copy in spread:
        copy.wait()
    for copy in own:
        copy.wait()

    q_copies = []
    for off in range(1, na):
        copy = pltpu.make_async_remote_copy(
            src_ref=q_out.at[:, a], dst_ref=q_out.at[:, a], send_sem=q_sems.at[0, off - 1],
            recv_sem=q_sems.at[1, off - 1], device_id=(lax.rem(a + off, na), z, t),
            device_id_type=mesh_ids)
        copy.start()
        q_copies.append(copy)

    n_right = nz // 2
    n_left = (nz - 1) // 2
    chains = ((right, n_right, r_sems, -1, []), (left, n_left, l_sems, 1, []))
    for step in range(n_right):
        for part in range(2):
            for side, count, sems, sign, copies in chains:
                if step >= count:
                    continue
                slot = lax.rem(z + sign * step + nz, nz)
                if step > 0:
                    copies[(step - 1) * 2 + part].wait_recv()
                copy = pltpu.make_async_remote_copy(
                    src_ref=(k_out, v_out)[part].at[:, slot], dst_ref=(k_out, v_out)[part].at[:, slot],
                    send_sem=sems.at[0, step * 2 + part], recv_sem=sems.at[1, step * 2 + part],
                    device_id=(a, side, t), device_id_type=mesh_ids)
                copy.start()
                copies.append(copy)
    for side, count, sems, sign, copies in chains:
        copies[-2].wait_recv()
        copies[-1].wait_recv()
        for copy in copies:
            copy.wait_send()
    for copy in q_copies:
        copy.wait()


def exchange(query_vectors, key_vectors, value_vectors, na, nz, nt):
    rows, width = query_vectors.shape
    heads = width // nt // HD
    n_right = nz // 2
    n_left = (nz - 1) // 2
    dtype = query_vectors.dtype
    return pl.pallas_call(
        functools.partial(exchange_kernel, na, nz, nt),
        out_shape=(
            jax.ShapeDtypeStruct((heads, na, nt * rows, HD), dtype),
            jax.ShapeDtypeStruct((heads, nz, nt * rows, HD), dtype),
            jax.ShapeDtypeStruct((heads, nz, nt * rows, HD), dtype),
        ),
        in_specs=[pl.BlockSpec(memory_space=pl.ANY)] * 3,
        out_specs=tuple(pl.BlockSpec(memory_space=pl.ANY) for _ in range(3)),
        scratch_shapes=[
            pltpu.SemaphoreType.DMA((2, 3, heads, nt - 1)),
            pltpu.SemaphoreType.DMA((3, heads)),
            pltpu.SemaphoreType.DMA((2, na - 1)),
            pltpu.SemaphoreType.DMA((2, 2 * n_right)),
            pltpu.SemaphoreType.DMA((2, 2 * n_left)),
        ],
        compiler_params=pltpu.CompilerParams(collective_id=0, has_side_effects=True),
    )(query_vectors, key_vectors, value_vectors)


def project_kernel(na, n_hi, parts_ref, stats_ref, w_ref, out_ref, got_parts, got_stats, att_buf,
                   pick, send1, recv1, total, send2, recv2, part_sems, stat_sems, sems1, send_sems2,
                   recv_sems2, own_stat_sem):
    mesh_ids = pl.DeviceIdType.MESH
    a = lax.axis_index("ca")
    z = lax.axis_index("cz")
    t = lax.axis_index("tp")
    core = lax.rem(t, 2)
    hi = t // 2
    partner = (a, z, hi * 2 + 1 - core)
    rows = send2.shape[1]
    heads = parts_ref.shape[0]

    barrier = pltpu.get_barrier_semaphore()
    for off in range(1, na):
        pl.semaphore_signal(barrier, inc=1, device_id=(lax.rem(a + off, na), z, t),
                            device_id_type=mesh_ids)
    pl.semaphore_signal(barrier, inc=1, device_id=partner, device_id_type=mesh_ids)
    for off in range(1, n_hi):
        pl.semaphore_signal(barrier, inc=1, device_id=(a, z, lax.rem(hi + off, n_hi) * 2 + core),
                            device_id_type=mesh_ids)
    pl.semaphore_wait(barrier, na - 1 + n_hi)

    own_stats = pltpu.make_async_copy(stats_ref.at[:, :, a], got_stats.at[na - 1], own_stat_sem)
    own_stats.start()
    gathered = []
    for off in range(1, na):
        dest = lax.rem(a + off, na)
        for src, dst, sems in ((parts_ref.at[:, dest], got_parts, part_sems),
                               (stats_ref.at[:, :, dest], got_stats, stat_sems)):
            copy = pltpu.make_async_remote_copy(
                src_ref=src, dst_ref=dst.at[off - 1], send_sem=sems.at[0, off - 1],
                recv_sem=sems.at[1, off - 1], device_id=(dest, z, t), device_id_type=mesh_ids)
            copy.start()
            gathered.append(copy)
    for copy in gathered:
        copy.wait()
    own_stats.wait()

    peaks = [got_stats[na - 1, 0]] + [got_stats[off - 1, 0] for off in range(1, na)]
    sums = [got_stats[na - 1, 1]] + [got_stats[off - 1, 1] for off in range(1, na)]
    top = peaks[0]
    for peak in peaks[1:]:
        top = jnp.maximum(top, peak)
    factors = [jnp.exp(peak - top) for peak in peaks]
    totals = factors[0] * sums[0]
    for factor, part_sum in zip(factors[1:], sums[1:]):
        totals = totals + factor * part_sum
    for h in range(heads):
        numerator = parts_ref[h, a].astype(jnp.float32) * factors[0][h][:, None]
        for off in range(1, na):
            numerator = numerator + (
                got_parts[off - 1, h].astype(jnp.float32) * factors[off][h][:, None]
            )
        att_buf[:, pl.ds(h * HD, HD)] = (numerator / totals[h][:, None]).astype(jnp.bfloat16)

    for j in range(n_hi):
        their = pl.multiple_of((j * 2 + 1 - core) * rows, rows)
        mine = pl.multiple_of((j * 2 + core) * rows, rows)
        pick[0, pl.ds(j * rows, rows), :] = att_buf[pl.ds(their, rows), :]
        pick[1, pl.ds(j * rows, rows), :] = att_buf[pl.ds(mine, rows), :]
    send1[...] = jnp.dot(pick[0], w_ref[...], preferred_element_type=jnp.float32).astype(
        jnp.bfloat16)
    first = pltpu.make_async_remote_copy(
        src_ref=send1, dst_ref=recv1, send_sem=sems1.at[0], recv_sem=sems1.at[1],
        device_id=partner, device_id_type=mesh_ids)
    first.start()
    total[...] = jnp.dot(pick[1], w_ref[...], preferred_element_type=jnp.float32).astype(
        jnp.bfloat16).astype(jnp.float32)
    first.wait()
    for j in range(n_hi):
        block = pl.ds(j * rows, rows)
        send2[j] = (total[block, :] + recv1[block, :].astype(jnp.float32)).astype(jnp.bfloat16)
    second = []
    for off in range(1, n_hi):
        dest = lax.rem(hi + off, n_hi)
        copy = pltpu.make_async_remote_copy(
            src_ref=send2.at[dest], dst_ref=recv2.at[off - 1], send_sem=send_sems2.at[off - 1],
            recv_sem=recv_sems2.at[off - 1], device_id=(a, z, dest * 2 + core),
            device_id_type=mesh_ids)
        copy.start()
        second.append(copy)
    own_rows = pl.ds(pl.multiple_of(hi * rows, rows), rows)
    own = total[own_rows, :] + recv1[own_rows, :].astype(jnp.float32)
    for copy in second:
        copy.wait()
    for off in range(1, n_hi):
        own = own + recv2[off - 1].astype(jnp.float32)
    out_ref[...] = own.astype(out_ref.dtype)


def project(parts, stats, out_weight, tp_count):
    heads, na, block_rows, _ = parts.shape
    n_hi = tp_count // 2
    rows = block_rows // tp_count
    cols = out_weight.shape[1]
    vmem = pl.BlockSpec(memory_space=pltpu.VMEM)
    return pl.pallas_call(
        functools.partial(project_kernel, na, n_hi),
        out_shape=jax.ShapeDtypeStruct((rows, cols), jnp.bfloat16),
        in_specs=[vmem, vmem, vmem],
        out_specs=vmem,
        scratch_shapes=[
            pltpu.VMEM((na - 1, heads, block_rows, HD), parts.dtype),
            pltpu.VMEM((na, 2, heads, block_rows), stats.dtype),
            pltpu.VMEM((block_rows, heads * HD), jnp.bfloat16),
            pltpu.VMEM((2, n_hi * rows, heads * HD), jnp.bfloat16),
            pltpu.VMEM((n_hi * rows, cols), jnp.bfloat16),
            pltpu.VMEM((n_hi * rows, cols), jnp.bfloat16),
            pltpu.VMEM((n_hi * rows, cols), jnp.float32),
            pltpu.VMEM((n_hi, rows, cols), jnp.bfloat16),
            pltpu.VMEM((n_hi - 1, rows, cols), jnp.bfloat16),
            pltpu.SemaphoreType.DMA((2, na - 1)),
            pltpu.SemaphoreType.DMA((2, na - 1)),
            pltpu.SemaphoreType.DMA((2,)),
            pltpu.SemaphoreType.DMA((n_hi - 1,)),
            pltpu.SemaphoreType.DMA((n_hi - 1,)),
            pltpu.SemaphoreType.DMA(()),
        ],
        compiler_params=pltpu.CompilerParams(collective_id=1, has_side_effects=True),
    )(parts, stats, out_weight)


def local(query_vectors, key_vectors, value_vectors, out_weight):
    score_scale = 1.0 / math.sqrt(HD)
    tp_count = lax.axis_size("tp")
    ca_count = lax.axis_size("ca")
    token_rows = query_vectors.shape[0]
    own_heads = query_vectors.shape[1] // HD // tp_count
    own_cols = own_heads * HD

    block_rows = token_rows * tp_count
    query_heads, key_heads, value_heads = exchange(
        query_vectors, key_vectors, value_vectors, ca_count, lax.axis_size("cz"), tp_count)
    row_peak, row_total, weighted = attend_local(
        query_heads.reshape(own_heads, -1, HD), key_heads.reshape(own_heads, -1, HD),
        value_heads.reshape(own_heads, -1, HD), score_scale)
    stats = jnp.stack([row_peak, row_total], axis=0).reshape(2, own_heads, ca_count, block_rows)
    parts = weighted.astype(jnp.bfloat16).reshape(own_heads, ca_count, block_rows, HD)
    return project(parts, stats, out_weight, tp_count)


def solution(mesh):
    ctx_count, tp_count = mesh.devices.shape
    split_mesh = Mesh(
        mesh.devices.reshape(ctx_count // KEY_SPLIT, KEY_SPLIT, tp_count), ("ca", "cz", "tp")
    )
    rows = P(("ca", "cz", "tp"), None)
    return jax.shard_map(
        local,
        mesh=split_mesh,
        in_specs=(rows, rows, rows, P("tp", None)),
        out_specs=rows,
        check_vma=False,
    )
```

```python
import functools
import math

import jax
import jax.numpy as jnp
from jax import lax
from jax.sharding import Mesh
from jax.sharding import PartitionSpec as P
from jax.experimental import pallas as pl
from jax.experimental.pallas import tpu as pltpu

HD = 128
KEY_SPLIT = 8


def attend_local(query_heads, key_heads, value_heads, score_scale):
    scores = (
        jnp.einsum("hid,hjd->hij", query_heads, key_heads, preferred_element_type=jnp.float32)
        * score_scale
    )
    row_peak = jnp.max(scores, axis=-1)
    weights_low = jnp.exp(scores - row_peak[..., None]).astype(jnp.bfloat16)
    row_total = jnp.sum(weights_low.astype(jnp.float32), axis=-1)
    weighted = jnp.einsum(
        "hij,hjd->hid", weights_low, value_heads, preferred_element_type=jnp.float32
    )
    return row_peak, row_total, weighted


def gather_by_exchange(block, axis_name):
    count = lax.axis_size(axis_name)
    spread = jnp.broadcast_to(block[None], (count,) + block.shape)
    return lax.all_to_all(spread, axis_name, 0, 0, tiled=True)


def exchange_kernel(na, nz, nt, q_ref, k_ref, v_ref, q_out, k_out, v_out, spread_sems,
                    own_sems, q_sems, r_sems, l_sems):
    mesh_ids = pl.DeviceIdType.MESH
    a = lax.axis_index("ca")
    z = lax.axis_index("cz")
    t = lax.axis_index("tp")
    right = lax.rem(z + 1, nz)
    left = lax.rem(z + nz - 1, nz)
    rows = q_ref.shape[0]
    heads = q_out.shape[0]

    barrier = pltpu.get_barrier_semaphore()
    for off in range(1, nt):
        pl.semaphore_signal(barrier, inc=1, device_id=(a, z, lax.rem(t + off, nt)),
                            device_id_type=mesh_ids)
    for off in range(1, na):
        pl.semaphore_signal(barrier, inc=1, device_id=(lax.rem(a + off, na), z, t),
                            device_id_type=mesh_ids)
    for side in (left, right):
        pl.semaphore_signal(barrier, inc=1, device_id=(a, side, t), device_id_type=mesh_ids)
    pl.semaphore_wait(barrier, nt - 1 + na - 1 + 2)

    mine = pl.ds(pl.multiple_of(t * rows, rows), rows)
    sources = (q_ref, k_ref, v_ref)

    def target(i, h):
        if i == 0:
            return q_out.at[h, a, mine]
        return (k_out, v_out)[i - 1].at[h, z, mine]

    def columns(dest, h):
        return pl.ds(pl.multiple_of((dest * heads + h) * HD, HD), HD)

    own = []
    for i in range(3):
        for h in range(heads):
            copy = pltpu.make_async_copy(
                sources[i].at[:, columns(t, h)], target(i, h), own_sems.at[i, h])
            copy.start()
            own.append(copy)
    spread = []
    for off in range(1, nt):
        dest = lax.rem(t + off, nt)
        for i in range(3):
            for h in range(heads):
                spread.append(pltpu.make_async_remote_copy(
                    src_ref=sources[i].at[:, columns(dest, h)], dst_ref=target(i, h),
                    send_sem=spread_sems.at[0, i, h, off - 1],
                    recv_sem=spread_sems.at[1, i, h, off - 1],
                    device_id=(a, z, dest), device_id_type=mesh_ids))
    for copy in spread:
        copy.start()
    for copy in spread:
        copy.wait()
    for copy in own:
        copy.wait()

    q_copies = []
    for off in range(1, na):
        copy = pltpu.make_async_remote_copy(
            src_ref=q_out.at[:, a], dst_ref=q_out.at[:, a], send_sem=q_sems.at[0, off - 1],
            recv_sem=q_sems.at[1, off - 1], device_id=(lax.rem(a + off, na), z, t),
            device_id_type=mesh_ids)
        copy.start()
        q_copies.append(copy)

    n_steps = nz // 2
    chains = ((right, r_sems, -1, {}), (left, l_sems, 1, {}))

    def parts_of(chain, step):
        if nz % 2 == 0 and step == n_steps - 1:
            return (chain,)
        return (0, 1)

    sent = []
    for step in range(n_steps):
        for part in range(2):
            for chain, (side, sems, sign, copies) in enumerate(chains):
                if part not in parts_of(chain, step):
                    continue
                slot = lax.rem(z + sign * step + nz, nz)
                if step > 0:
                    copies.pop((step - 1, part)).wait_recv()
                buf = (k_out, v_out)[part]
                copy = pltpu.make_async_remote_copy(
                    src_ref=buf.at[:, slot], dst_ref=buf.at[:, slot],
                    send_sem=sems.at[0, step * 2 + part], recv_sem=sems.at[1, step * 2 + part],
                    device_id=(a, side, t), device_id_type=mesh_ids)
                copy.start()
                copies[(step, part)] = copy
                sent.append(copy)
    for side, sems, sign, copies in chains:
        for copy in copies.values():
            copy.wait_recv()
    for copy in sent:
        copy.wait_send()
    for copy in q_copies:
        copy.wait()


def exchange(query_vectors, key_vectors, value_vectors, na, nz, nt):
    rows, width = query_vectors.shape
    heads = width // nt // HD
    n_right = nz // 2
    n_left = (nz - 1) // 2
    dtype = query_vectors.dtype
    return pl.pallas_call(
        functools.partial(exchange_kernel, na, nz, nt),
        out_shape=(
            jax.ShapeDtypeStruct((heads, na, nt * rows, HD), dtype),
            jax.ShapeDtypeStruct((heads, nz, nt * rows, HD), dtype),
            jax.ShapeDtypeStruct((heads, nz, nt * rows, HD), dtype),
        ),
        in_specs=[pl.BlockSpec(memory_space=pl.ANY)] * 3,
        out_specs=tuple(pl.BlockSpec(memory_space=pl.ANY) for _ in range(3)),
        scratch_shapes=[
            pltpu.SemaphoreType.DMA((2, 3, heads, nt - 1)),
            pltpu.SemaphoreType.DMA((3, heads)),
            pltpu.SemaphoreType.DMA((2, na - 1)),
            pltpu.SemaphoreType.DMA((2, 2 * (nz // 2))),
            pltpu.SemaphoreType.DMA((2, 2 * (nz // 2))),
        ],
        compiler_params=pltpu.CompilerParams(collective_id=0, has_side_effects=True),
    )(query_vectors, key_vectors, value_vectors)


def project_kernel(na, n_hi, parts_ref, stats_ref, w_ref, out_ref, got_parts, got_stats, att_buf,
                   pick, send1, recv1, total, send2, recv2, part_sems, stat_sems, sems1, send_sems2,
                   recv_sems2, own_stat_sem):
    mesh_ids = pl.DeviceIdType.MESH
    a = lax.axis_index("ca")
    z = lax.axis_index("cz")
    t = lax.axis_index("tp")
    core = lax.rem(t, 2)
    hi = t // 2
    partner = (a, z, hi * 2 + 1 - core)
    rows = send2.shape[1]
    heads = parts_ref.shape[0]

    barrier = pltpu.get_barrier_semaphore()
    for off in range(1, na):
        pl.semaphore_signal(barrier, inc=1, device_id=(lax.rem(a + off, na), z, t),
                            device_id_type=mesh_ids)
    pl.semaphore_signal(barrier, inc=1, device_id=partner, device_id_type=mesh_ids)
    for off in range(1, n_hi):
        pl.semaphore_signal(barrier, inc=1, device_id=(a, z, lax.rem(hi + off, n_hi) * 2 + core),
                            device_id_type=mesh_ids)
    pl.semaphore_wait(barrier, na - 1 + n_hi)

    own_stats = pltpu.make_async_copy(stats_ref.at[:, :, a], got_stats.at[na - 1], own_stat_sem)
    own_stats.start()
    gathered = []
    for off in range(1, na):
        dest = lax.rem(a + off, na)
        for src, dst, sems in ((parts_ref.at[:, dest], got_parts, part_sems),
                               (stats_ref.at[:, :, dest], got_stats, stat_sems)):
            copy = pltpu.make_async_remote_copy(
                src_ref=src, dst_ref=dst.at[off - 1], send_sem=sems.at[0, off - 1],
                recv_sem=sems.at[1, off - 1], device_id=(dest, z, t), device_id_type=mesh_ids)
            copy.start()
            gathered.append(copy)
    for copy in gathered:
        copy.wait()
    own_stats.wait()

    peaks = [got_stats[na - 1, 0]] + [got_stats[off - 1, 0] for off in range(1, na)]
    sums = [got_stats[na - 1, 1]] + [got_stats[off - 1, 1] for off in range(1, na)]
    top = peaks[0]
    for peak in peaks[1:]:
        top = jnp.maximum(top, peak)
    factors = [jnp.exp(peak - top) for peak in peaks]
    totals = factors[0] * sums[0]
    for factor, part_sum in zip(factors[1:], sums[1:]):
        totals = totals + factor * part_sum
    for h in range(heads):
        numerator = parts_ref[h, a].astype(jnp.float32) * factors[0][h][:, None]
        for off in range(1, na):
            numerator = numerator + (
                got_parts[off - 1, h].astype(jnp.float32) * factors[off][h][:, None]
            )
        att_buf[:, pl.ds(h * HD, HD)] = (numerator / totals[h][:, None]).astype(jnp.bfloat16)

    for j in range(n_hi):
        their = pl.multiple_of((j * 2 + 1 - core) * rows, rows)
        mine = pl.multiple_of((j * 2 + core) * rows, rows)
        pick[0, pl.ds(j * rows, rows), :] = att_buf[pl.ds(their, rows), :]
        pick[1, pl.ds(j * rows, rows), :] = att_buf[pl.ds(mine, rows), :]
    send1[...] = jnp.dot(pick[0], w_ref[...], preferred_element_type=jnp.float32).astype(
        jnp.bfloat16)
    first = pltpu.make_async_remote_copy(
        src_ref=send1, dst_ref=recv1, send_sem=sems1.at[0], recv_sem=sems1.at[1],
        device_id=partner, device_id_type=mesh_ids)
    first.start()
    total[...] = jnp.dot(pick[1], w_ref[...], preferred_element_type=jnp.float32).astype(
        jnp.bfloat16).astype(jnp.float32)
    first.wait()
    for j in range(n_hi):
        block = pl.ds(j * rows, rows)
        send2[j] = (total[block, :] + recv1[block, :].astype(jnp.float32)).astype(jnp.bfloat16)
    second = []
    for off in range(1, n_hi):
        dest = lax.rem(hi + off, n_hi)
        copy = pltpu.make_async_remote_copy(
            src_ref=send2.at[dest], dst_ref=recv2.at[off - 1], send_sem=send_sems2.at[off - 1],
            recv_sem=recv_sems2.at[off - 1], device_id=(a, z, dest * 2 + core),
            device_id_type=mesh_ids)
        copy.start()
        second.append(copy)
    own_rows = pl.ds(pl.multiple_of(hi * rows, rows), rows)
    own = total[own_rows, :] + recv1[own_rows, :].astype(jnp.float32)
    for copy in second:
        copy.wait()
    for off in range(1, n_hi):
        own = own + recv2[off - 1].astype(jnp.float32)
    out_ref[...] = own.astype(out_ref.dtype)


def project(parts, stats, out_weight, tp_count):
    heads, na, block_rows, _ = parts.shape
    n_hi = tp_count // 2
    rows = block_rows // tp_count
    cols = out_weight.shape[1]
    vmem = pl.BlockSpec(memory_space=pltpu.VMEM)
    return pl.pallas_call(
        functools.partial(project_kernel, na, n_hi),
        out_shape=jax.ShapeDtypeStruct((rows, cols), jnp.bfloat16),
        in_specs=[vmem, vmem, vmem],
        out_specs=vmem,
        scratch_shapes=[
            pltpu.VMEM((na - 1, heads, block_rows, HD), parts.dtype),
            pltpu.VMEM((na, 2, heads, block_rows), stats.dtype),
            pltpu.VMEM((block_rows, heads * HD), jnp.bfloat16),
            pltpu.VMEM((2, n_hi * rows, heads * HD), jnp.bfloat16),
            pltpu.VMEM((n_hi * rows, cols), jnp.bfloat16),
            pltpu.VMEM((n_hi * rows, cols), jnp.bfloat16),
            pltpu.VMEM((n_hi * rows, cols), jnp.float32),
            pltpu.VMEM((n_hi, rows, cols), jnp.bfloat16),
            pltpu.VMEM((n_hi - 1, rows, cols), jnp.bfloat16),
            pltpu.SemaphoreType.DMA((2, na - 1)),
            pltpu.SemaphoreType.DMA((2, na - 1)),
            pltpu.SemaphoreType.DMA((2,)),
            pltpu.SemaphoreType.DMA((n_hi - 1,)),
            pltpu.SemaphoreType.DMA((n_hi - 1,)),
            pltpu.SemaphoreType.DMA(()),
        ],
        compiler_params=pltpu.CompilerParams(collective_id=1, has_side_effects=True),
    )(parts, stats, out_weight)


def local(query_vectors, key_vectors, value_vectors, out_weight):
    score_scale = 1.0 / math.sqrt(HD)
    tp_count = lax.axis_size("tp")
    ca_count = lax.axis_size("ca")
    token_rows = query_vectors.shape[0]
    own_heads = query_vectors.shape[1] // HD // tp_count
    own_cols = own_heads * HD

    block_rows = token_rows * tp_count
    query_heads, key_heads, value_heads = exchange(
        query_vectors, key_vectors, value_vectors, ca_count, lax.axis_size("cz"), tp_count)
    row_peak, row_total, weighted = attend_local(
        query_heads.reshape(own_heads, -1, HD), key_heads.reshape(own_heads, -1, HD),
        value_heads.reshape(own_heads, -1, HD), score_scale)
    stats = jnp.stack([row_peak, row_total], axis=0).reshape(2, own_heads, ca_count, block_rows)
    parts = weighted.astype(jnp.bfloat16).reshape(own_heads, ca_count, block_rows, HD)
    return project(parts, stats, out_weight, tp_count)


def solution(mesh):
    ctx_count, tp_count = mesh.devices.shape
    split_mesh = Mesh(
        mesh.devices.reshape(ctx_count // KEY_SPLIT, KEY_SPLIT, tp_count), ("ca", "cz", "tp")
    )
    rows = P(("ca", "cz", "tp"), None)
    return jax.shard_map(
        local,
        mesh=split_mesh,
        in_specs=(rows, rows, rows, P("tp", None)),
        out_specs=rows,
        check_vma=False,
    )
```

```python
import functools
import math

import jax
import jax.numpy as jnp
from jax import lax
from jax.sharding import Mesh
from jax.sharding import PartitionSpec as P
from jax.experimental import pallas as pl
from jax.experimental.pallas import tpu as pltpu

HD = 128
KEY_SPLIT = 8


def attend_local(query_heads, key_heads, value_heads, score_scale):
    scores = (
        jnp.einsum("hid,hjd->hij", query_heads, key_heads, preferred_element_type=jnp.float32)
        * score_scale
    )
    row_peak = jnp.max(scores, axis=-1)
    weights_low = jnp.exp(scores - row_peak[..., None]).astype(jnp.bfloat16)
    row_total = jnp.sum(weights_low.astype(jnp.float32), axis=-1)
    weighted = jnp.einsum(
        "hij,hjd->hid", weights_low, value_heads, preferred_element_type=jnp.float32
    )
    return row_peak, row_total, weighted


def gather_by_exchange(block, axis_name):
    count = lax.axis_size(axis_name)
    spread = jnp.broadcast_to(block[None], (count,) + block.shape)
    return lax.all_to_all(spread, axis_name, 0, 0, tiled=True)


def exchange_kernel(na, nz, nt, q_ref, k_ref, v_ref, q_out, k_out, v_out, spread_sems,
                    own_sems, q_sems, r_sems, l_sems):
    mesh_ids = pl.DeviceIdType.MESH
    a = lax.axis_index("ca")
    z = lax.axis_index("cz")
    t = lax.axis_index("tp")
    right = lax.rem(z + 1, nz)
    left = lax.rem(z + nz - 1, nz)
    rows = q_ref.shape[0]
    heads = q_out.shape[0]

    barrier = pltpu.get_barrier_semaphore()
    for off in range(1, nt):
        pl.semaphore_signal(barrier, inc=1, device_id=(a, z, lax.rem(t + off, nt)),
                            device_id_type=mesh_ids)
    for off in range(1, na):
        pl.semaphore_signal(barrier, inc=1, device_id=(lax.rem(a + off, na), z, t),
                            device_id_type=mesh_ids)
    for side in (left, right):
        pl.semaphore_signal(barrier, inc=1, device_id=(a, side, t), device_id_type=mesh_ids)
    pl.semaphore_wait(barrier, nt - 1 + na - 1 + 2)

    mine = pl.ds(pl.multiple_of(t * rows, rows), rows)
    sources = (q_ref, k_ref, v_ref)

    def target(i, h):
        if i == 0:
            return q_out.at[h, a, mine]
        return (k_out, v_out)[i - 1].at[h, z, mine]

    def columns(dest, h):
        return pl.ds(pl.multiple_of((dest * heads + h) * HD, HD), HD)

    own = []
    for i in range(3):
        for h in range(heads):
            copy = pltpu.make_async_copy(
                sources[i].at[:, columns(t, h)], target(i, h), own_sems.at[i, h])
            copy.start()
            own.append(copy)
    spread = []
    for off in range(1, nt):
        dest = lax.rem(t + off, nt)
        for i in range(3):
            for h in range(heads):
                spread.append(pltpu.make_async_remote_copy(
                    src_ref=sources[i].at[:, columns(dest, h)], dst_ref=target(i, h),
                    send_sem=spread_sems.at[0, i, h, off - 1],
                    recv_sem=spread_sems.at[1, i, h, off - 1],
                    device_id=(a, z, dest), device_id_type=mesh_ids))
    for copy in spread:
        copy.start()
    for copy in spread:
        copy.wait()
    for copy in own:
        copy.wait()

    q_copies = []
    for off in range(1, na):
        copy = pltpu.make_async_remote_copy(
            src_ref=q_out.at[:, a], dst_ref=q_out.at[:, a], send_sem=q_sems.at[0, off - 1],
            recv_sem=q_sems.at[1, off - 1], device_id=(lax.rem(a + off, na), z, t),
            device_id_type=mesh_ids)
        copy.start()
        q_copies.append(copy)

    n_steps = nz // 2
    chains = ((right, r_sems, -1, {}), (left, l_sems, 1, {}))

    def parts_of(chain, step):
        if nz % 2 == 0 and step == n_steps - 1:
            return (chain,)
        return (0, 1)

    sent = []
    for step in range(n_steps):
        for part in range(2):
            for chain, (side, sems, sign, copies) in enumerate(chains):
                if part not in parts_of(chain, step):
                    continue
                slot = lax.rem(z + sign * step + nz, nz)
                if step > 0:
                    copies.pop((step - 1, part)).wait_recv()
                buf = (k_out, v_out)[part]
                copy = pltpu.make_async_remote_copy(
                    src_ref=buf.at[:, slot], dst_ref=buf.at[:, slot],
                    send_sem=sems.at[0, step * 2 + part], recv_sem=sems.at[1, step * 2 + part],
                    device_id=(a, side, t), device_id_type=mesh_ids)
                copy.start()
                copies[(step, part)] = copy
                sent.append(copy)
    for side, sems, sign, copies in chains:
        for copy in copies.values():
            copy.wait_recv()
    for copy in sent:
        copy.wait_send()
    for copy in q_copies:
        copy.wait()


def exchange(query_vectors, key_vectors, value_vectors, na, nz, nt):
    rows, width = query_vectors.shape
    heads = width // nt // HD
    n_right = nz // 2
    n_left = (nz - 1) // 2
    dtype = query_vectors.dtype
    return pl.pallas_call(
        functools.partial(exchange_kernel, na, nz, nt),
        out_shape=(
            jax.ShapeDtypeStruct((heads, na, nt * rows, HD), dtype),
            jax.ShapeDtypeStruct((heads, nz, nt * rows, HD), dtype),
            jax.ShapeDtypeStruct((heads, nz, nt * rows, HD), dtype),
        ),
        in_specs=[pl.BlockSpec(memory_space=pl.ANY)] * 3,
        out_specs=tuple(pl.BlockSpec(memory_space=pl.ANY) for _ in range(3)),
        scratch_shapes=[
            pltpu.SemaphoreType.DMA((2, 3, heads, nt - 1)),
            pltpu.SemaphoreType.DMA((3, heads)),
            pltpu.SemaphoreType.DMA((2, na - 1)),
            pltpu.SemaphoreType.DMA((2, 2 * (nz // 2))),
            pltpu.SemaphoreType.DMA((2, 2 * (nz // 2))),
        ],
        compiler_params=pltpu.CompilerParams(collective_id=0, has_side_effects=True),
    )(query_vectors, key_vectors, value_vectors)


def project_kernel(na, n_hi, parts_ref, stats_ref, w_ref, out_ref, got_parts, got_stats, att_buf,
                   pick, send1, recv1, total, send2, recv2, part_sems, stat_sems, sems1, send_sems2,
                   recv_sems2, own_stat_sem):
    mesh_ids = pl.DeviceIdType.MESH
    a = lax.axis_index("ca")
    z = lax.axis_index("cz")
    t = lax.axis_index("tp")
    core = lax.rem(t, 2)
    hi = t // 2
    partner = (a, z, hi * 2 + 1 - core)
    rows = send2.shape[1]
    heads = parts_ref.shape[0]

    barrier = pltpu.get_barrier_semaphore()
    for off in range(1, na):
        pl.semaphore_signal(barrier, inc=1, device_id=(lax.rem(a + off, na), z, t),
                            device_id_type=mesh_ids)
    pl.semaphore_signal(barrier, inc=1, device_id=partner, device_id_type=mesh_ids)
    for off in range(1, n_hi):
        pl.semaphore_signal(barrier, inc=1, device_id=(a, z, lax.rem(hi + off, n_hi) * 2 + core),
                            device_id_type=mesh_ids)
    pl.semaphore_wait(barrier, na - 1 + n_hi)

    own_stats = pltpu.make_async_copy(stats_ref.at[:, :, a], got_stats.at[na - 1], own_stat_sem)
    own_stats.start()
    gathered = []
    for off in range(1, na):
        dest = lax.rem(a + off, na)
        for src, dst, sems in ((parts_ref.at[:, dest], got_parts, part_sems),
                               (stats_ref.at[:, :, dest], got_stats, stat_sems)):
            copy = pltpu.make_async_remote_copy(
                src_ref=src, dst_ref=dst.at[off - 1], send_sem=sems.at[0, off - 1],
                recv_sem=sems.at[1, off - 1], device_id=(dest, z, t), device_id_type=mesh_ids)
            copy.start()
            gathered.append(copy)
    for copy in gathered:
        copy.wait()
    own_stats.wait()

    peaks = [got_stats[na - 1, 0]] + [got_stats[off - 1, 0] for off in range(1, na)]
    sums = [got_stats[na - 1, 1]] + [got_stats[off - 1, 1] for off in range(1, na)]
    top = peaks[0]
    for peak in peaks[1:]:
        top = jnp.maximum(top, peak)
    factors = [jnp.exp(peak - top) for peak in peaks]
    totals = factors[0] * sums[0]
    for factor, part_sum in zip(factors[1:], sums[1:]):
        totals = totals + factor * part_sum
    for h in range(heads):
        numerator = parts_ref[h, a].astype(jnp.float32) * factors[0][h][:, None]
        for off in range(1, na):
            numerator = numerator + (
                got_parts[off - 1, h].astype(jnp.float32) * factors[off][h][:, None]
            )
        att_buf[:, pl.ds(h * HD, HD)] = (numerator / totals[h][:, None]).astype(jnp.bfloat16)

    for j in range(n_hi):
        their = pl.multiple_of((j * 2 + 1 - core) * rows, rows)
        mine = pl.multiple_of((j * 2 + core) * rows, rows)
        pick[0, pl.ds(j * rows, rows), :] = att_buf[pl.ds(their, rows), :]
        pick[1, pl.ds(j * rows, rows), :] = att_buf[pl.ds(mine, rows), :]
    send1[...] = jnp.dot(pick[0], w_ref[...], preferred_element_type=jnp.float32).astype(
        jnp.bfloat16)
    first = pltpu.make_async_remote_copy(
        src_ref=send1, dst_ref=recv1, send_sem=sems1.at[0], recv_sem=sems1.at[1],
        device_id=partner, device_id_type=mesh_ids)
    first.start()
    total[...] = jnp.dot(pick[1], w_ref[...], preferred_element_type=jnp.float32).astype(
        jnp.bfloat16).astype(jnp.float32)
    first.wait()
    for j in range(n_hi):
        block = pl.ds(j * rows, rows)
        send2[j] = (total[block, :] + recv1[block, :].astype(jnp.float32)).astype(jnp.bfloat16)
    second = []
    for off in range(1, n_hi):
        dest = lax.rem(hi + off, n_hi)
        copy = pltpu.make_async_remote_copy(
            src_ref=send2.at[dest], dst_ref=recv2.at[off - 1], send_sem=send_sems2.at[off - 1],
            recv_sem=recv_sems2.at[off - 1], device_id=(a, z, dest * 2 + core),
            device_id_type=mesh_ids)
        copy.start()
        second.append(copy)
    own_rows = pl.ds(pl.multiple_of(hi * rows, rows), rows)
    own = total[own_rows, :] + recv1[own_rows, :].astype(jnp.float32)
    for copy in second:
        copy.wait()
    for off in range(1, n_hi):
        own = own + recv2[off - 1].astype(jnp.float32)
    out_ref[...] = own.astype(out_ref.dtype)


def project(parts, stats, out_weight, tp_count):
    heads, na, block_rows, _ = parts.shape
    n_hi = tp_count // 2
    rows = block_rows // tp_count
    cols = out_weight.shape[1]
    vmem = pl.BlockSpec(memory_space=pltpu.VMEM)
    return pl.pallas_call(
        functools.partial(project_kernel, na, n_hi),
        out_shape=jax.ShapeDtypeStruct((rows, cols), jnp.float32),
        in_specs=[vmem, vmem, vmem],
        out_specs=vmem,
        scratch_shapes=[
            pltpu.VMEM((na - 1, heads, block_rows, HD), parts.dtype),
            pltpu.VMEM((na, 2, heads, block_rows), stats.dtype),
            pltpu.VMEM((block_rows, heads * HD), jnp.bfloat16),
            pltpu.VMEM((2, n_hi * rows, heads * HD), jnp.bfloat16),
            pltpu.VMEM((n_hi * rows, cols), jnp.bfloat16),
            pltpu.VMEM((n_hi * rows, cols), jnp.bfloat16),
            pltpu.VMEM((n_hi * rows, cols), jnp.float32),
            pltpu.VMEM((n_hi, rows, cols), jnp.bfloat16),
            pltpu.VMEM((n_hi - 1, rows, cols), jnp.bfloat16),
            pltpu.SemaphoreType.DMA((2, na - 1)),
            pltpu.SemaphoreType.DMA((2, na - 1)),
            pltpu.SemaphoreType.DMA((2,)),
            pltpu.SemaphoreType.DMA((n_hi - 1,)),
            pltpu.SemaphoreType.DMA((n_hi - 1,)),
            pltpu.SemaphoreType.DMA(()),
        ],
        compiler_params=pltpu.CompilerParams(collective_id=1, has_side_effects=True),
    )(parts, stats, out_weight)


def local(query_vectors, key_vectors, value_vectors, out_weight):
    score_scale = 1.0 / math.sqrt(HD)
    tp_count = lax.axis_size("tp")
    ca_count = lax.axis_size("ca")
    token_rows = query_vectors.shape[0]
    own_heads = query_vectors.shape[1] // HD // tp_count
    own_cols = own_heads * HD

    block_rows = token_rows * tp_count
    query_heads, key_heads, value_heads = exchange(
        query_vectors, key_vectors, value_vectors, ca_count, lax.axis_size("cz"), tp_count)
    row_peak, row_total, weighted = attend_local(
        query_heads.reshape(own_heads, -1, HD), key_heads.reshape(own_heads, -1, HD),
        value_heads.reshape(own_heads, -1, HD), score_scale)
    stats = jnp.stack([row_peak, row_total], axis=0).reshape(2, own_heads, ca_count, block_rows)
    parts = weighted.astype(jnp.bfloat16).reshape(own_heads, ca_count, block_rows, HD)
    return project(parts, stats, out_weight, tp_count).astype(jnp.bfloat16)


def solution(mesh):
    ctx_count, tp_count = mesh.devices.shape
    split_mesh = Mesh(
        mesh.devices.reshape(ctx_count // KEY_SPLIT, KEY_SPLIT, tp_count), ("ca", "cz", "tp")
    )
    rows = P(("ca", "cz", "tp"), None)
    return jax.shard_map(
        local,
        mesh=split_mesh,
        in_specs=(rows, rows, rows, P("tp", None)),
        out_specs=rows,
        check_vma=False,
    )
```

```python
import functools
import math

import jax
import jax.numpy as jnp
from jax import lax
from jax.sharding import Mesh
from jax.sharding import PartitionSpec as P
from jax.experimental import pallas as pl
from jax.experimental.pallas import tpu as pltpu

HD = 128
KEY_SPLIT = 8


def attend_local(query_heads, key_heads, value_heads, score_scale):
    scores = (
        jnp.einsum("hid,hjd->hij", query_heads, key_heads, preferred_element_type=jnp.float32)
        * score_scale
    )
    row_peak = jnp.max(scores, axis=-1)
    weights_low = jnp.exp(scores - row_peak[..., None]).astype(jnp.bfloat16)
    row_total = jnp.sum(weights_low.astype(jnp.float32), axis=-1)
    weighted = jnp.einsum(
        "hij,hjd->hid", weights_low, value_heads, preferred_element_type=jnp.float32
    )
    return row_peak, row_total, weighted


def gather_by_exchange(block, axis_name):
    count = lax.axis_size(axis_name)
    spread = jnp.broadcast_to(block[None], (count,) + block.shape)
    return lax.all_to_all(spread, axis_name, 0, 0, tiled=True)


def exchange_kernel(na, nz, nt, q_ref, k_ref, v_ref, q_out, k_out, v_out, spread_sems,
                    own_sems, q_sems, r_sems, l_sems):
    mesh_ids = pl.DeviceIdType.MESH
    a = lax.axis_index("ca")
    z = lax.axis_index("cz")
    t = lax.axis_index("tp")
    right = lax.rem(z + 1, nz)
    left = lax.rem(z + nz - 1, nz)
    rows = q_ref.shape[0]
    heads = q_out.shape[0]

    barrier = pltpu.get_barrier_semaphore()
    for off in range(1, nt):
        pl.semaphore_signal(barrier, inc=1, device_id=(a, z, lax.rem(t + off, nt)),
                            device_id_type=mesh_ids)
    for off in range(1, na):
        pl.semaphore_signal(barrier, inc=1, device_id=(lax.rem(a + off, na), z, t),
                            device_id_type=mesh_ids)
    for side in (left, right):
        pl.semaphore_signal(barrier, inc=1, device_id=(a, side, t), device_id_type=mesh_ids)
    pl.semaphore_wait(barrier, nt - 1 + na - 1 + 2)

    mine = pl.ds(pl.multiple_of(t * rows, rows), rows)
    sources = (q_ref, k_ref, v_ref)

    def target(i, h):
        if i == 0:
            return q_out.at[h, a, mine]
        return (k_out, v_out)[i - 1].at[h, z, mine]

    def columns(dest, h):
        return pl.ds(pl.multiple_of((dest * heads + h) * HD, HD), HD)

    own = []
    for i in range(3):
        for h in range(heads):
            copy = pltpu.make_async_copy(
                sources[i].at[:, columns(t, h)], target(i, h), own_sems.at[i, h])
            copy.start()
            own.append(copy)
    spread = [[], [], []]
    for off in range(1, nt):
        dest = lax.rem(t + off, nt)
        for i in range(3):
            for h in range(heads):
                spread[i].append(pltpu.make_async_remote_copy(
                    src_ref=sources[i].at[:, columns(dest, h)], dst_ref=target(i, h),
                    send_sem=spread_sems.at[0, i, h, off - 1],
                    recv_sem=spread_sems.at[1, i, h, off - 1],
                    device_id=(a, z, dest), device_id_type=mesh_ids))
    for group in spread:
        for copy in group:
            copy.start()
    for copy in spread[0] + own[:heads]:
        copy.wait()

    q_copies = []
    for off in range(1, na):
        copy = pltpu.make_async_remote_copy(
            src_ref=q_out.at[:, a], dst_ref=q_out.at[:, a], send_sem=q_sems.at[0, off - 1],
            recv_sem=q_sems.at[1, off - 1], device_id=(lax.rem(a + off, na), z, t),
            device_id_type=mesh_ids)
        copy.start()
        q_copies.append(copy)

    n_steps = nz // 2
    chains = ((right, r_sems, -1, {}), (left, l_sems, 1, {}))

    def parts_of(chain, step):
        if nz % 2 == 0 and step == n_steps - 1:
            return (chain,)
        return (0, 1)

    for copy in spread[1] + own[heads:2 * heads]:
        copy.wait()
    sent = []
    for step in range(n_steps):
        for part in range(2):
            for chain, (side, sems, sign, copies) in enumerate(chains):
                if part not in parts_of(chain, step):
                    continue
                slot = lax.rem(z + sign * step + nz, nz)
                if step > 0:
                    copies.pop((step - 1, part)).wait_recv()
                elif part == 1 and chain == 0:
                    for copy in spread[2] + own[2 * heads:]:
                        copy.wait()
                buf = (k_out, v_out)[part]
                copy = pltpu.make_async_remote_copy(
                    src_ref=buf.at[:, slot], dst_ref=buf.at[:, slot],
                    send_sem=sems.at[0, step * 2 + part], recv_sem=sems.at[1, step * 2 + part],
                    device_id=(a, side, t), device_id_type=mesh_ids)
                copy.start()
                copies[(step, part)] = copy
                sent.append(copy)
    for side, sems, sign, copies in chains:
        for copy in copies.values():
            copy.wait_recv()
    for copy in sent:
        copy.wait_send()
    for copy in q_copies:
        copy.wait()


def exchange(query_vectors, key_vectors, value_vectors, na, nz, nt):
    rows, width = query_vectors.shape
    heads = width // nt // HD
    n_right = nz // 2
    n_left = (nz - 1) // 2
    dtype = query_vectors.dtype
    return pl.pallas_call(
        functools.partial(exchange_kernel, na, nz, nt),
        out_shape=(
            jax.ShapeDtypeStruct((heads, na, nt * rows, HD), dtype),
            jax.ShapeDtypeStruct((heads, nz, nt * rows, HD), dtype),
            jax.ShapeDtypeStruct((heads, nz, nt * rows, HD), dtype),
        ),
        in_specs=[pl.BlockSpec(memory_space=pl.ANY)] * 3,
        out_specs=tuple(pl.BlockSpec(memory_space=pl.ANY) for _ in range(3)),
        scratch_shapes=[
            pltpu.SemaphoreType.DMA((2, 3, heads, nt - 1)),
            pltpu.SemaphoreType.DMA((3, heads)),
            pltpu.SemaphoreType.DMA((2, na - 1)),
            pltpu.SemaphoreType.DMA((2, 2 * (nz // 2))),
            pltpu.SemaphoreType.DMA((2, 2 * (nz // 2))),
        ],
        compiler_params=pltpu.CompilerParams(collective_id=0, has_side_effects=True),
    )(query_vectors, key_vectors, value_vectors)


def project_kernel(na, n_hi, parts_ref, stats_ref, w_ref, out_ref, got_parts, got_stats, att_buf,
                   pick, send1, recv1, total, send2, recv2, part_sems, stat_sems, sems1, send_sems2,
                   recv_sems2, own_stat_sem):
    mesh_ids = pl.DeviceIdType.MESH
    a = lax.axis_index("ca")
    z = lax.axis_index("cz")
    t = lax.axis_index("tp")
    core = lax.rem(t, 2)
    hi = t // 2
    partner = (a, z, hi * 2 + 1 - core)
    rows = send2.shape[1]
    heads = parts_ref.shape[0]

    barrier = pltpu.get_barrier_semaphore()
    for off in range(1, na):
        pl.semaphore_signal(barrier, inc=1, device_id=(lax.rem(a + off, na), z, t),
                            device_id_type=mesh_ids)
    pl.semaphore_signal(barrier, inc=1, device_id=partner, device_id_type=mesh_ids)
    for off in range(1, n_hi):
        pl.semaphore_signal(barrier, inc=1, device_id=(a, z, lax.rem(hi + off, n_hi) * 2 + core),
                            device_id_type=mesh_ids)
    pl.semaphore_wait(barrier, na - 1 + n_hi)

    own_stats = pltpu.make_async_copy(stats_ref.at[:, :, a], got_stats.at[na - 1], own_stat_sem)
    own_stats.start()
    gathered = []
    for off in range(1, na):
        dest = lax.rem(a + off, na)
        for src, dst, sems in ((parts_ref.at[:, dest], got_parts, part_sems),
                               (stats_ref.at[:, :, dest], got_stats, stat_sems)):
            copy = pltpu.make_async_remote_copy(
                src_ref=src, dst_ref=dst.at[off - 1], send_sem=sems.at[0, off - 1],
                recv_sem=sems.at[1, off - 1], device_id=(dest, z, t), device_id_type=mesh_ids)
            copy.start()
            gathered.append(copy)
    for copy in gathered:
        copy.wait()
    own_stats.wait()

    peaks = [got_stats[na - 1, 0]] + [got_stats[off - 1, 0] for off in range(1, na)]
    sums = [got_stats[na - 1, 1]] + [got_stats[off - 1, 1] for off in range(1, na)]
    top = peaks[0]
    for peak in peaks[1:]:
        top = jnp.maximum(top, peak)
    factors = [jnp.exp(peak - top) for peak in peaks]
    totals = factors[0] * sums[0]
    for factor, part_sum in zip(factors[1:], sums[1:]):
        totals = totals + factor * part_sum
    for h in range(heads):
        numerator = parts_ref[h, a].astype(jnp.float32) * factors[0][h][:, None]
        for off in range(1, na):
            numerator = numerator + (
                got_parts[off - 1, h].astype(jnp.float32) * factors[off][h][:, None]
            )
        att_buf[:, pl.ds(h * HD, HD)] = (numerator / totals[h][:, None]).astype(jnp.bfloat16)

    for j in range(n_hi):
        their = pl.multiple_of((j * 2 + 1 - core) * rows, rows)
        mine = pl.multiple_of((j * 2 + core) * rows, rows)
        pick[0, pl.ds(j * rows, rows), :] = att_buf[pl.ds(their, rows), :]
        pick[1, pl.ds(j * rows, rows), :] = att_buf[pl.ds(mine, rows), :]
    cols = send1.shape[1]
    half = cols // 2
    firsts = []
    for k in range(2):
        window = pl.ds(k * half, half)
        send1[:, window] = jnp.dot(
            pick[0], w_ref[:, window], preferred_element_type=jnp.float32).astype(jnp.bfloat16)
        copy = pltpu.make_async_remote_copy(
            src_ref=send1.at[:, window], dst_ref=recv1.at[:, window], send_sem=sems1.at[0, k],
            recv_sem=sems1.at[1, k], device_id=partner, device_id_type=mesh_ids)
        copy.start()
        firsts.append(copy)
    total[...] = jnp.dot(pick[1], w_ref[...], preferred_element_type=jnp.float32).astype(
        jnp.bfloat16).astype(jnp.float32)
    second = []
    for k in range(2):
        window = pl.ds(k * half, half)
        firsts[k].wait()
        for j in range(n_hi):
            block = pl.ds(j * rows, rows)
            send2[j, :, window] = (
                total[block, window] + recv1[block, window].astype(jnp.float32)
            ).astype(jnp.bfloat16)
        for off in range(1, n_hi):
            dest = lax.rem(hi + off, n_hi)
            copy = pltpu.make_async_remote_copy(
                src_ref=send2.at[dest, :, window], dst_ref=recv2.at[off - 1, :, window],
                send_sem=send_sems2.at[0, k, off - 1], recv_sem=send_sems2.at[1, k, off - 1],
                device_id=(a, z, dest * 2 + core), device_id_type=mesh_ids)
            copy.start()
            second.append(copy)
    own_rows = pl.ds(pl.multiple_of(hi * rows, rows), rows)
    own = total[own_rows, :] + recv1[own_rows, :].astype(jnp.float32)
    for copy in second:
        copy.wait()
    for off in range(1, n_hi):
        own = own + recv2[off - 1].astype(jnp.float32)
    out_ref[...] = own.astype(out_ref.dtype)


def project(parts, stats, out_weight, tp_count):
    heads, na, block_rows, _ = parts.shape
    n_hi = tp_count // 2
    rows = block_rows // tp_count
    cols = out_weight.shape[1]
    vmem = pl.BlockSpec(memory_space=pltpu.VMEM)
    return pl.pallas_call(
        functools.partial(project_kernel, na, n_hi),
        out_shape=jax.ShapeDtypeStruct((rows, cols), jnp.bfloat16),
        in_specs=[vmem, vmem, vmem],
        out_specs=vmem,
        scratch_shapes=[
            pltpu.VMEM((na - 1, heads, block_rows, HD), parts.dtype),
            pltpu.VMEM((na, 2, heads, block_rows), stats.dtype),
            pltpu.VMEM((block_rows, heads * HD), jnp.bfloat16),
            pltpu.VMEM((2, n_hi * rows, heads * HD), jnp.bfloat16),
            pltpu.VMEM((n_hi * rows, cols), jnp.bfloat16),
            pltpu.VMEM((n_hi * rows, cols), jnp.bfloat16),
            pltpu.VMEM((n_hi * rows, cols), jnp.float32),
            pltpu.VMEM((n_hi, rows, cols), jnp.bfloat16),
            pltpu.VMEM((n_hi - 1, rows, cols), jnp.bfloat16),
            pltpu.SemaphoreType.DMA((2, na - 1)),
            pltpu.SemaphoreType.DMA((2, na - 1)),
            pltpu.SemaphoreType.DMA((2, 2)),
            pltpu.SemaphoreType.DMA((2, 2, n_hi - 1)),
            pltpu.SemaphoreType.DMA((1,)),
            pltpu.SemaphoreType.DMA(()),
        ],
        compiler_params=pltpu.CompilerParams(collective_id=1, has_side_effects=True),
    )(parts, stats, out_weight)


def local(query_vectors, key_vectors, value_vectors, out_weight):
    score_scale = 1.0 / math.sqrt(HD)
    tp_count = lax.axis_size("tp")
    ca_count = lax.axis_size("ca")
    token_rows = query_vectors.shape[0]
    own_heads = query_vectors.shape[1] // HD // tp_count
    own_cols = own_heads * HD

    block_rows = token_rows * tp_count
    query_heads, key_heads, value_heads = exchange(
        query_vectors, key_vectors, value_vectors, ca_count, lax.axis_size("cz"), tp_count)
    row_peak, row_total, weighted = attend_local(
        query_heads.reshape(own_heads, -1, HD), key_heads.reshape(own_heads, -1, HD),
        value_heads.reshape(own_heads, -1, HD), score_scale)
    stats = jnp.stack([row_peak, row_total], axis=0).reshape(2, own_heads, ca_count, block_rows)
    parts = weighted.astype(jnp.bfloat16).reshape(own_heads, ca_count, block_rows, HD)
    return project(parts, stats, out_weight, tp_count)


def solution(mesh):
    ctx_count, tp_count = mesh.devices.shape
    split_mesh = Mesh(
        mesh.devices.reshape(ctx_count // KEY_SPLIT, KEY_SPLIT, tp_count), ("ca", "cz", "tp")
    )
    rows = P(("ca", "cz", "tp"), None)
    return jax.shard_map(
        local,
        mesh=split_mesh,
        in_specs=(rows, rows, rows, P("tp", None)),
        out_specs=rows,
        check_vma=False,
    )
```

```python
import functools
import math

import jax
import jax.numpy as jnp
from jax import lax
from jax.sharding import Mesh
from jax.sharding import PartitionSpec as P
from jax.experimental import pallas as pl
from jax.experimental.pallas import tpu as pltpu

HD = 128
KEY_SPLIT = 8
STAGE_CHUNKS = 4


def attend_local(query_heads, key_heads, value_heads, score_scale):
    scores = (
        jnp.einsum("hid,hjd->hij", query_heads, key_heads, preferred_element_type=jnp.float32)
        * score_scale
    )
    row_peak = jnp.max(scores, axis=-1)
    weights_low = jnp.exp(scores - row_peak[..., None]).astype(jnp.bfloat16)
    row_total = jnp.sum(weights_low.astype(jnp.float32), axis=-1)
    weighted = jnp.einsum(
        "hij,hjd->hid", weights_low, value_heads, preferred_element_type=jnp.float32
    )
    return row_peak, row_total, weighted


def gather_by_exchange(block, axis_name):
    count = lax.axis_size(axis_name)
    spread = jnp.broadcast_to(block[None], (count,) + block.shape)
    return lax.all_to_all(spread, axis_name, 0, 0, tiled=True)


def exchange_kernel(na, nz, nt, q_ref, k_ref, v_ref, q_out, k_out, v_out, spread_sems,
                    own_sems, q_sems, r_sems, l_sems):
    mesh_ids = pl.DeviceIdType.MESH
    a = lax.axis_index("ca")
    z = lax.axis_index("cz")
    t = lax.axis_index("tp")
    right = lax.rem(z + 1, nz)
    left = lax.rem(z + nz - 1, nz)
    rows = q_ref.shape[0]
    heads = q_out.shape[0]

    barrier = pltpu.get_barrier_semaphore()
    for off in range(1, nt):
        pl.semaphore_signal(barrier, inc=1, device_id=(a, z, lax.rem(t + off, nt)),
                            device_id_type=mesh_ids)
    for off in range(1, na):
        pl.semaphore_signal(barrier, inc=1, device_id=(lax.rem(a + off, na), z, t),
                            device_id_type=mesh_ids)
    for side in (left, right):
        pl.semaphore_signal(barrier, inc=1, device_id=(a, side, t), device_id_type=mesh_ids)
    pl.semaphore_wait(barrier, nt - 1 + na - 1 + 2)

    mine = pl.ds(pl.multiple_of(t * rows, rows), rows)
    sources = (q_ref, k_ref, v_ref)

    def target(i, h):
        if i == 0:
            return q_out.at[h, a, mine]
        return (k_out, v_out)[i - 1].at[h, z, mine]

    def columns(dest, h):
        return pl.ds(pl.multiple_of((dest * heads + h) * HD, HD), HD)

    own = []
    for i in range(3):
        for h in range(heads):
            copy = pltpu.make_async_copy(
                sources[i].at[:, columns(t, h)], target(i, h), own_sems.at[i, h])
            copy.start()
            own.append(copy)
    spread = [[], [], []]
    for off in range(1, nt):
        dest = lax.rem(t + off, nt)
        for i in range(3):
            for h in range(heads):
                spread[i].append(pltpu.make_async_remote_copy(
                    src_ref=sources[i].at[:, columns(dest, h)], dst_ref=target(i, h),
                    send_sem=spread_sems.at[0, i, h, off - 1],
                    recv_sem=spread_sems.at[1, i, h, off - 1],
                    device_id=(a, z, dest), device_id_type=mesh_ids))
    for group in spread:
        for copy in group:
            copy.start()
    for copy in spread[0] + own[:heads]:
        copy.wait()

    q_copies = []
    for off in range(1, na):
        copy = pltpu.make_async_remote_copy(
            src_ref=q_out.at[:, a], dst_ref=q_out.at[:, a], send_sem=q_sems.at[0, off - 1],
            recv_sem=q_sems.at[1, off - 1], device_id=(lax.rem(a + off, na), z, t),
            device_id_type=mesh_ids)
        copy.start()
        q_copies.append(copy)

    n_steps = nz // 2
    chains = ((right, r_sems, -1, {}), (left, l_sems, 1, {}))

    def parts_of(chain, step):
        if nz % 2 == 0 and step == n_steps - 1:
            return (chain,)
        return (0, 1)

    for copy in spread[1] + own[heads:2 * heads]:
        copy.wait()
    sent = []
    for step in range(n_steps):
        for part in range(2):
            for chain, (side, sems, sign, copies) in enumerate(chains):
                if part not in parts_of(chain, step):
                    continue
                slot = lax.rem(z + sign * step + nz, nz)
                if step > 0:
                    copies.pop((step - 1, part)).wait_recv()
                elif part == 1 and chain == 0:
                    for copy in spread[2] + own[2 * heads:]:
                        copy.wait()
                buf = (k_out, v_out)[part]
                copy = pltpu.make_async_remote_copy(
                    src_ref=buf.at[:, slot], dst_ref=buf.at[:, slot],
                    send_sem=sems.at[0, step * 2 + part], recv_sem=sems.at[1, step * 2 + part],
                    device_id=(a, side, t), device_id_type=mesh_ids)
                copy.start()
                copies[(step, part)] = copy
                sent.append(copy)
    for side, sems, sign, copies in chains:
        for copy in copies.values():
            copy.wait_recv()
    for copy in sent:
        copy.wait_send()
    for copy in q_copies:
        copy.wait()


def exchange(query_vectors, key_vectors, value_vectors, na, nz, nt):
    rows, width = query_vectors.shape
    heads = width // nt // HD
    n_right = nz // 2
    n_left = (nz - 1) // 2
    dtype = query_vectors.dtype
    return pl.pallas_call(
        functools.partial(exchange_kernel, na, nz, nt),
        out_shape=(
            jax.ShapeDtypeStruct((heads, na, nt * rows, HD), dtype),
            jax.ShapeDtypeStruct((heads, nz, nt * rows, HD), dtype),
            jax.ShapeDtypeStruct((heads, nz, nt * rows, HD), dtype),
        ),
        in_specs=[pl.BlockSpec(memory_space=pl.ANY)] * 3,
        out_specs=tuple(pl.BlockSpec(memory_space=pl.ANY) for _ in range(3)),
        scratch_shapes=[
            pltpu.SemaphoreType.DMA((2, 3, heads, nt - 1)),
            pltpu.SemaphoreType.DMA((3, heads)),
            pltpu.SemaphoreType.DMA((2, na - 1)),
            pltpu.SemaphoreType.DMA((2, 2 * (nz // 2))),
            pltpu.SemaphoreType.DMA((2, 2 * (nz // 2))),
        ],
        compiler_params=pltpu.CompilerParams(collective_id=0, has_side_effects=True),
    )(query_vectors, key_vectors, value_vectors)


def project_kernel(na, n_hi, parts_ref, stats_ref, w_ref, out_ref, got_parts, got_stats, att_buf,
                   pick, send1, recv1, total, send2, recv2, part_sems, stat_sems, sems1, send_sems2,
                   recv_sems2, own_stat_sem):
    mesh_ids = pl.DeviceIdType.MESH
    a = lax.axis_index("ca")
    z = lax.axis_index("cz")
    t = lax.axis_index("tp")
    core = lax.rem(t, 2)
    hi = t // 2
    partner = (a, z, hi * 2 + 1 - core)
    rows = send2.shape[1]
    heads = parts_ref.shape[0]

    barrier = pltpu.get_barrier_semaphore()
    for off in range(1, na):
        pl.semaphore_signal(barrier, inc=1, device_id=(lax.rem(a + off, na), z, t),
                            device_id_type=mesh_ids)
    pl.semaphore_signal(barrier, inc=1, device_id=partner, device_id_type=mesh_ids)
    for off in range(1, n_hi):
        pl.semaphore_signal(barrier, inc=1, device_id=(a, z, lax.rem(hi + off, n_hi) * 2 + core),
                            device_id_type=mesh_ids)
    pl.semaphore_wait(barrier, na - 1 + n_hi)

    own_stats = pltpu.make_async_copy(stats_ref.at[:, :, a], got_stats.at[na - 1], own_stat_sem)
    own_stats.start()
    gathered = []
    for off in range(1, na):
        dest = lax.rem(a + off, na)
        for src, dst, sems in ((parts_ref.at[:, dest], got_parts, part_sems),
                               (stats_ref.at[:, :, dest], got_stats, stat_sems)):
            copy = pltpu.make_async_remote_copy(
                src_ref=src, dst_ref=dst.at[off - 1], send_sem=sems.at[0, off - 1],
                recv_sem=sems.at[1, off - 1], device_id=(dest, z, t), device_id_type=mesh_ids)
            copy.start()
            gathered.append(copy)
    for copy in gathered:
        copy.wait()
    own_stats.wait()

    peaks = [got_stats[na - 1, 0]] + [got_stats[off - 1, 0] for off in range(1, na)]
    sums = [got_stats[na - 1, 1]] + [got_stats[off - 1, 1] for off in range(1, na)]
    top = peaks[0]
    for peak in peaks[1:]:
        top = jnp.maximum(top, peak)
    factors = [jnp.exp(peak - top) for peak in peaks]
    totals = factors[0] * sums[0]
    for factor, part_sum in zip(factors[1:], sums[1:]):
        totals = totals + factor * part_sum
    for h in range(heads):
        numerator = parts_ref[h, a].astype(jnp.float32) * factors[0][h][:, None]
        for off in range(1, na):
            numerator = numerator + (
                got_parts[off - 1, h].astype(jnp.float32) * factors[off][h][:, None]
            )
        att_buf[:, pl.ds(h * HD, HD)] = (numerator / totals[h][:, None]).astype(jnp.bfloat16)

    for j in range(n_hi):
        their = pl.multiple_of((j * 2 + 1 - core) * rows, rows)
        mine = pl.multiple_of((j * 2 + core) * rows, rows)
        pick[0, pl.ds(j * rows, rows), :] = att_buf[pl.ds(their, rows), :]
        pick[1, pl.ds(j * rows, rows), :] = att_buf[pl.ds(mine, rows), :]
    cols = send1.shape[1]
    chunk = cols // STAGE_CHUNKS
    firsts = []
    for k in range(STAGE_CHUNKS):
        window = pl.ds(k * chunk, chunk)
        send1[:, window] = jnp.dot(
            pick[0], w_ref[:, window], preferred_element_type=jnp.float32).astype(jnp.bfloat16)
        copy = pltpu.make_async_remote_copy(
            src_ref=send1.at[:, window], dst_ref=recv1.at[:, window], send_sem=sems1.at[0, k],
            recv_sem=sems1.at[1, k], device_id=partner, device_id_type=mesh_ids)
        copy.start()
        firsts.append(copy)
    total[...] = jnp.dot(pick[1], w_ref[...], preferred_element_type=jnp.float32).astype(
        jnp.bfloat16).astype(jnp.float32)
    second = []
    for k in range(STAGE_CHUNKS):
        window = pl.ds(k * chunk, chunk)
        firsts[k].wait()
        for j in range(n_hi):
            block = pl.ds(j * rows, rows)
            send2[j, :, window] = (
                total[block, window] + recv1[block, window].astype(jnp.float32)
            ).astype(jnp.bfloat16)
        for off in range(1, n_hi):
            dest = lax.rem(hi + off, n_hi)
            copy = pltpu.make_async_remote_copy(
                src_ref=send2.at[dest, :, window], dst_ref=recv2.at[off - 1, :, window],
                send_sem=send_sems2.at[0, k, off - 1], recv_sem=send_sems2.at[1, k, off - 1],
                device_id=(a, z, dest * 2 + core), device_id_type=mesh_ids)
            copy.start()
            second.append(copy)
    own_rows = pl.ds(pl.multiple_of(hi * rows, rows), rows)
    own = total[own_rows, :] + recv1[own_rows, :].astype(jnp.float32)
    for copy in second:
        copy.wait()
    for off in range(1, n_hi):
        own = own + recv2[off - 1].astype(jnp.float32)
    out_ref[...] = own.astype(out_ref.dtype)


def project(parts, stats, out_weight, tp_count):
    heads, na, block_rows, _ = parts.shape
    n_hi = tp_count // 2
    rows = block_rows // tp_count
    cols = out_weight.shape[1]
    vmem = pl.BlockSpec(memory_space=pltpu.VMEM)
    return pl.pallas_call(
        functools.partial(project_kernel, na, n_hi),
        out_shape=jax.ShapeDtypeStruct((rows, cols), jnp.bfloat16),
        in_specs=[vmem, vmem, vmem],
        out_specs=vmem,
        scratch_shapes=[
            pltpu.VMEM((na - 1, heads, block_rows, HD), parts.dtype),
            pltpu.VMEM((na, 2, heads, block_rows), stats.dtype),
            pltpu.VMEM((block_rows, heads * HD), jnp.bfloat16),
            pltpu.VMEM((2, n_hi * rows, heads * HD), jnp.bfloat16),
            pltpu.VMEM((n_hi * rows, cols), jnp.bfloat16),
            pltpu.VMEM((n_hi * rows, cols), jnp.bfloat16),
            pltpu.VMEM((n_hi * rows, cols), jnp.float32),
            pltpu.VMEM((n_hi, rows, cols), jnp.bfloat16),
            pltpu.VMEM((n_hi - 1, rows, cols), jnp.bfloat16),
            pltpu.SemaphoreType.DMA((2, na - 1)),
            pltpu.SemaphoreType.DMA((2, na - 1)),
            pltpu.SemaphoreType.DMA((2, STAGE_CHUNKS)),
            pltpu.SemaphoreType.DMA((2, STAGE_CHUNKS, n_hi - 1)),
            pltpu.SemaphoreType.DMA((1,)),
            pltpu.SemaphoreType.DMA(()),
        ],
        compiler_params=pltpu.CompilerParams(collective_id=1, has_side_effects=True),
    )(parts, stats, out_weight)


def local(query_vectors, key_vectors, value_vectors, out_weight):
    score_scale = 1.0 / math.sqrt(HD)
    tp_count = lax.axis_size("tp")
    ca_count = lax.axis_size("ca")
    token_rows = query_vectors.shape[0]
    own_heads = query_vectors.shape[1] // HD // tp_count
    own_cols = own_heads * HD

    block_rows = token_rows * tp_count
    query_heads, key_heads, value_heads = exchange(
        query_vectors, key_vectors, value_vectors, ca_count, lax.axis_size("cz"), tp_count)
    row_peak, row_total, weighted = attend_local(
        query_heads.reshape(own_heads, -1, HD), key_heads.reshape(own_heads, -1, HD),
        value_heads.reshape(own_heads, -1, HD), score_scale)
    stats = jnp.stack([row_peak, row_total], axis=0).reshape(2, own_heads, ca_count, block_rows)
    parts = weighted.astype(jnp.bfloat16).reshape(own_heads, ca_count, block_rows, HD)
    return project(parts, stats, out_weight, tp_count)


def solution(mesh):
    ctx_count, tp_count = mesh.devices.shape
    split_mesh = Mesh(
        mesh.devices.reshape(ctx_count // KEY_SPLIT, KEY_SPLIT, tp_count), ("ca", "cz", "tp")
    )
    rows = P(("ca", "cz", "tp"), None)
    return jax.shard_map(
        local,
        mesh=split_mesh,
        in_specs=(rows, rows, rows, P("tp", None)),
        out_specs=rows,
        check_vma=False,
    )
```

```python
import functools
import math

import jax
import jax.numpy as jnp
from jax import lax
from jax.sharding import Mesh
from jax.sharding import PartitionSpec as P
from jax.experimental import pallas as pl
from jax.experimental.pallas import tpu as pltpu

HD = 128
KEY_SPLIT = 8
STAGE_CHUNKS = 4


def attend_local(query_heads, key_heads, value_heads, score_scale):
    scores = (
        jnp.einsum("hid,hjd->hij", query_heads, key_heads, preferred_element_type=jnp.float32)
        * score_scale
    )
    row_peak = jnp.max(scores, axis=-1)
    weights_low = jnp.exp(scores - row_peak[..., None]).astype(jnp.bfloat16)
    row_total = jnp.sum(weights_low.astype(jnp.float32), axis=-1)
    weighted = jnp.einsum(
        "hij,hjd->hid", weights_low, value_heads, preferred_element_type=jnp.float32
    )
    return row_peak, row_total, weighted


def gather_by_exchange(block, axis_name):
    count = lax.axis_size(axis_name)
    spread = jnp.broadcast_to(block[None], (count,) + block.shape)
    return lax.all_to_all(spread, axis_name, 0, 0, tiled=True)


def exchange_kernel(na, nz, nt, q_ref, k_ref, v_ref, q_out, k_out, v_out, spread_sems,
                    own_sems, q_sems, r_sems, l_sems):
    mesh_ids = pl.DeviceIdType.MESH
    a = lax.axis_index("ca")
    z = lax.axis_index("cz")
    t = lax.axis_index("tp")
    right = lax.rem(z + 1, nz)
    left = lax.rem(z + nz - 1, nz)
    rows = q_ref.shape[0]
    heads = q_out.shape[0]

    barrier = pltpu.get_barrier_semaphore()
    for off in range(1, nt):
        pl.semaphore_signal(barrier, inc=1, device_id=(a, z, lax.rem(t + off, nt)),
                            device_id_type=mesh_ids)
    for off in range(1, na):
        pl.semaphore_signal(barrier, inc=1, device_id=(lax.rem(a + off, na), z, t),
                            device_id_type=mesh_ids)
    for side in (left, right):
        pl.semaphore_signal(barrier, inc=1, device_id=(a, side, t), device_id_type=mesh_ids)
    pl.semaphore_wait(barrier, nt - 1 + na - 1 + 2)

    mine = pl.ds(pl.multiple_of(t * rows, rows), rows)
    sources = (q_ref, k_ref, v_ref)

    def target(i, h):
        if i == 0:
            return q_out.at[h, a, mine]
        return (k_out, v_out)[i - 1].at[h, z, mine]

    def columns(dest, h):
        return pl.ds(pl.multiple_of((dest * heads + h) * HD, HD), HD)

    own = []
    for i in range(3):
        for h in range(heads):
            copy = pltpu.make_async_copy(
                sources[i].at[:, columns(t, h)], target(i, h), own_sems.at[i, h])
            copy.start()
            own.append(copy)
    spread = [[], [], []]
    for off in range(1, nt):
        dest = lax.rem(t + off, nt)
        for i in range(3):
            for h in range(heads):
                spread[i].append(pltpu.make_async_remote_copy(
                    src_ref=sources[i].at[:, columns(dest, h)], dst_ref=target(i, h),
                    send_sem=spread_sems.at[0, i, h, off - 1],
                    recv_sem=spread_sems.at[1, i, h, off - 1],
                    device_id=(a, z, dest), device_id_type=mesh_ids))
    for group in spread:
        for copy in group:
            copy.start()
    for copy in spread[0] + own[:heads]:
        copy.wait()

    q_copies = []
    for off in range(1, na):
        copy = pltpu.make_async_remote_copy(
            src_ref=q_out.at[:, a], dst_ref=q_out.at[:, a], send_sem=q_sems.at[0, off - 1],
            recv_sem=q_sems.at[1, off - 1], device_id=(lax.rem(a + off, na), z, t),
            device_id_type=mesh_ids)
        copy.start()
        q_copies.append(copy)

    n_steps = nz // 2
    chains = ((right, r_sems, -1, {}), (left, l_sems, 1, {}))

    def parts_of(chain, step):
        if nz % 2 == 0 and step == n_steps - 1:
            return (chain,)
        return (0, 1)

    for copy in spread[1] + own[heads:2 * heads]:
        copy.wait()
    sent = []
    for step in range(n_steps):
        for part in range(2):
            for chain, (side, sems, sign, copies) in enumerate(chains):
                if part not in parts_of(chain, step):
                    continue
                slot = lax.rem(z + sign * step + nz, nz)
                if step > 0:
                    copies.pop((step - 1, part)).wait_recv()
                elif part == 1 and chain == 0:
                    for copy in spread[2] + own[2 * heads:]:
                        copy.wait()
                buf = (k_out, v_out)[part]
                copy = pltpu.make_async_remote_copy(
                    src_ref=buf.at[:, slot], dst_ref=buf.at[:, slot],
                    send_sem=sems.at[0, step * 2 + part], recv_sem=sems.at[1, step * 2 + part],
                    device_id=(a, side, t), device_id_type=mesh_ids)
                copy.start()
                copies[(step, part)] = copy
                sent.append(copy)
    for side, sems, sign, copies in chains:
        for copy in copies.values():
            copy.wait_recv()
    for copy in sent:
        copy.wait_send()
    for copy in q_copies:
        copy.wait()


def exchange(query_vectors, key_vectors, value_vectors, na, nz, nt):
    rows, width = query_vectors.shape
    heads = width // nt // HD
    n_right = nz // 2
    n_left = (nz - 1) // 2
    dtype = query_vectors.dtype
    return pl.pallas_call(
        functools.partial(exchange_kernel, na, nz, nt),
        out_shape=(
            jax.ShapeDtypeStruct((heads, na, nt * rows, HD), dtype),
            jax.ShapeDtypeStruct((heads, nz, nt * rows, HD), dtype),
            jax.ShapeDtypeStruct((heads, nz, nt * rows, HD), dtype),
        ),
        in_specs=[pl.BlockSpec(memory_space=pl.ANY)] * 3,
        out_specs=tuple(pl.BlockSpec(memory_space=pl.ANY) for _ in range(3)),
        scratch_shapes=[
            pltpu.SemaphoreType.DMA((2, 3, heads, nt - 1)),
            pltpu.SemaphoreType.DMA((3, heads)),
            pltpu.SemaphoreType.DMA((2, na - 1)),
            pltpu.SemaphoreType.DMA((2, 2 * (nz // 2))),
            pltpu.SemaphoreType.DMA((2, 2 * (nz // 2))),
        ],
        compiler_params=pltpu.CompilerParams(collective_id=0, has_side_effects=True),
    )(query_vectors, key_vectors, value_vectors)


def project_kernel(na, n_hi, parts_ref, stats_ref, w_ref, out_ref, got_parts, got_stats, att_buf,
                   pick, send1, recv1, total, send2, recv2, part_sems, stat_sems, sems1, send_sems2,
                   recv_sems2, own_stat_sem):
    mesh_ids = pl.DeviceIdType.MESH
    a = lax.axis_index("ca")
    z = lax.axis_index("cz")
    t = lax.axis_index("tp")
    core = lax.rem(t, 2)
    hi = t // 2
    partner = (a, z, hi * 2 + 1 - core)
    rows = send2.shape[1]
    heads = parts_ref.shape[0]

    barrier = pltpu.get_barrier_semaphore()
    for off in range(1, na):
        pl.semaphore_signal(barrier, inc=1, device_id=(lax.rem(a + off, na), z, t),
                            device_id_type=mesh_ids)
    pl.semaphore_signal(barrier, inc=1, device_id=partner, device_id_type=mesh_ids)
    for off in range(1, n_hi):
        pl.semaphore_signal(barrier, inc=1, device_id=(a, z, lax.rem(hi + off, n_hi) * 2 + core),
                            device_id_type=mesh_ids)
    pl.semaphore_wait(barrier, na - 1 + n_hi)

    own_stats = pltpu.make_async_copy(stats_ref.at[:, :, a], got_stats.at[na - 1], own_stat_sem)
    own_stats.start()
    stat_copies = []
    for off in range(1, na):
        dest = lax.rem(a + off, na)
        copy = pltpu.make_async_remote_copy(
            src_ref=stats_ref.at[:, :, dest], dst_ref=got_stats.at[off - 1],
            send_sem=stat_sems.at[0, off - 1], recv_sem=stat_sems.at[1, off - 1],
            device_id=(dest, z, t), device_id_type=mesh_ids)
        copy.start()
        stat_copies.append(copy)
    part_copies = []
    for h in range(heads):
        per_head = []
        for off in range(1, na):
            dest = lax.rem(a + off, na)
            copy = pltpu.make_async_remote_copy(
                src_ref=parts_ref.at[h, dest], dst_ref=got_parts.at[off - 1, h],
                send_sem=part_sems.at[0, h, off - 1], recv_sem=part_sems.at[1, h, off - 1],
                device_id=(dest, z, t), device_id_type=mesh_ids)
            copy.start()
            per_head.append(copy)
        part_copies.append(per_head)
    for copy in stat_copies:
        copy.wait()
    own_stats.wait()

    peaks = [got_stats[na - 1, 0]] + [got_stats[off - 1, 0] for off in range(1, na)]
    sums = [got_stats[na - 1, 1]] + [got_stats[off - 1, 1] for off in range(1, na)]
    top = peaks[0]
    for peak in peaks[1:]:
        top = jnp.maximum(top, peak)
    factors = [jnp.exp(peak - top) for peak in peaks]
    totals = factors[0] * sums[0]
    for factor, part_sum in zip(factors[1:], sums[1:]):
        totals = totals + factor * part_sum
    for h in range(heads):
        for copy in part_copies[h]:
            copy.wait()
        numerator = parts_ref[h, a].astype(jnp.float32) * factors[0][h][:, None]
        for off in range(1, na):
            numerator = numerator + (
                got_parts[off - 1, h].astype(jnp.float32) * factors[off][h][:, None]
            )
        att_buf[:, pl.ds(h * HD, HD)] = (numerator / totals[h][:, None]).astype(jnp.bfloat16)

    for j in range(n_hi):
        their = pl.multiple_of((j * 2 + 1 - core) * rows, rows)
        mine = pl.multiple_of((j * 2 + core) * rows, rows)
        pick[0, pl.ds(j * rows, rows), :] = att_buf[pl.ds(their, rows), :]
        pick[1, pl.ds(j * rows, rows), :] = att_buf[pl.ds(mine, rows), :]
    cols = send1.shape[1]
    chunk = cols // STAGE_CHUNKS
    firsts = []
    for k in range(STAGE_CHUNKS):
        window = pl.ds(k * chunk, chunk)
        send1[:, window] = jnp.dot(
            pick[0], w_ref[:, window], preferred_element_type=jnp.float32).astype(jnp.bfloat16)
        copy = pltpu.make_async_remote_copy(
            src_ref=send1.at[:, window], dst_ref=recv1.at[:, window], send_sem=sems1.at[0, k],
            recv_sem=sems1.at[1, k], device_id=partner, device_id_type=mesh_ids)
        copy.start()
        firsts.append(copy)
    total[...] = jnp.dot(pick[1], w_ref[...], preferred_element_type=jnp.float32).astype(
        jnp.bfloat16).astype(jnp.float32)
    second = []
    for k in range(STAGE_CHUNKS):
        window = pl.ds(k * chunk, chunk)
        firsts[k].wait()
        for j in range(n_hi):
            block = pl.ds(j * rows, rows)
            send2[j, :, window] = (
                total[block, window] + recv1[block, window].astype(jnp.float32)
            ).astype(jnp.bfloat16)
        for off in range(1, n_hi):
            dest = lax.rem(hi + off, n_hi)
            copy = pltpu.make_async_remote_copy(
                src_ref=send2.at[dest, :, window], dst_ref=recv2.at[off - 1, :, window],
                send_sem=send_sems2.at[0, k, off - 1], recv_sem=send_sems2.at[1, k, off - 1],
                device_id=(a, z, dest * 2 + core), device_id_type=mesh_ids)
            copy.start()
            second.append(copy)
    own_rows = pl.ds(pl.multiple_of(hi * rows, rows), rows)
    own = total[own_rows, :] + recv1[own_rows, :].astype(jnp.float32)
    for copy in second:
        copy.wait()
    for off in range(1, n_hi):
        own = own + recv2[off - 1].astype(jnp.float32)
    out_ref[...] = own.astype(out_ref.dtype)


def project(parts, stats, out_weight, tp_count):
    heads, na, block_rows, _ = parts.shape
    n_hi = tp_count // 2
    rows = block_rows // tp_count
    cols = out_weight.shape[1]
    vmem = pl.BlockSpec(memory_space=pltpu.VMEM)
    return pl.pallas_call(
        functools.partial(project_kernel, na, n_hi),
        out_shape=jax.ShapeDtypeStruct((rows, cols), jnp.bfloat16),
        in_specs=[vmem, vmem, vmem],
        out_specs=vmem,
        scratch_shapes=[
            pltpu.VMEM((na - 1, heads, block_rows, HD), parts.dtype),
            pltpu.VMEM((na, 2, heads, block_rows), stats.dtype),
            pltpu.VMEM((block_rows, heads * HD), jnp.bfloat16),
            pltpu.VMEM((2, n_hi * rows, heads * HD), jnp.bfloat16),
            pltpu.VMEM((n_hi * rows, cols), jnp.bfloat16),
            pltpu.VMEM((n_hi * rows, cols), jnp.bfloat16),
            pltpu.VMEM((n_hi * rows, cols), jnp.float32),
            pltpu.VMEM((n_hi, rows, cols), jnp.bfloat16),
            pltpu.VMEM((n_hi - 1, rows, cols), jnp.bfloat16),
            pltpu.SemaphoreType.DMA((2, heads, na - 1)),
            pltpu.SemaphoreType.DMA((2, na - 1)),
            pltpu.SemaphoreType.DMA((2, STAGE_CHUNKS)),
            pltpu.SemaphoreType.DMA((2, STAGE_CHUNKS, n_hi - 1)),
            pltpu.SemaphoreType.DMA((1,)),
            pltpu.SemaphoreType.DMA(()),
        ],
        compiler_params=pltpu.CompilerParams(collective_id=1, has_side_effects=True),
    )(parts, stats, out_weight)


def local(query_vectors, key_vectors, value_vectors, out_weight):
    score_scale = 1.0 / math.sqrt(HD)
    tp_count = lax.axis_size("tp")
    ca_count = lax.axis_size("ca")
    token_rows = query_vectors.shape[0]
    own_heads = query_vectors.shape[1] // HD // tp_count
    own_cols = own_heads * HD

    block_rows = token_rows * tp_count
    query_heads, key_heads, value_heads = exchange(
        query_vectors, key_vectors, value_vectors, ca_count, lax.axis_size("cz"), tp_count)
    row_peak, row_total, weighted = attend_local(
        query_heads.reshape(own_heads, -1, HD), key_heads.reshape(own_heads, -1, HD),
        value_heads.reshape(own_heads, -1, HD), score_scale)
    stats = jnp.stack([row_peak, row_total], axis=0).reshape(2, own_heads, ca_count, block_rows)
    parts = weighted.astype(jnp.bfloat16).reshape(own_heads, ca_count, block_rows, HD)
    return project(parts, stats, out_weight, tp_count)


def solution(mesh):
    ctx_count, tp_count = mesh.devices.shape
    split_mesh = Mesh(
        mesh.devices.reshape(ctx_count // KEY_SPLIT, KEY_SPLIT, tp_count), ("ca", "cz", "tp")
    )
    rows = P(("ca", "cz", "tp"), None)
    return jax.shard_map(
        local,
        mesh=split_mesh,
        in_specs=(rows, rows, rows, P("tp", None)),
        out_specs=rows,
        check_vma=False,
    )
```

```python
import functools
import math

import jax
import jax.numpy as jnp
from jax import lax
from jax.sharding import Mesh
from jax.sharding import PartitionSpec as P
from jax.experimental import pallas as pl
from jax.experimental.pallas import tpu as pltpu

HD = 128
KEY_SPLIT = 8
STAGE_CHUNKS = 4


def attend_local(query_heads, key_heads, value_heads, score_scale):
    scores = (
        jnp.einsum("hid,hjd->hij", query_heads, key_heads, preferred_element_type=jnp.float32)
        * score_scale
    )
    row_peak = jnp.max(scores, axis=-1)
    weights_low = jnp.exp(scores - row_peak[..., None]).astype(jnp.bfloat16)
    with_ones = jnp.concatenate([value_heads, jnp.ones_like(value_heads)], axis=-1)
    weighted = jnp.einsum(
        "hij,hjd->hid", weights_low, with_ones, preferred_element_type=jnp.float32
    )
    return row_peak, weighted[..., HD], weighted[..., :HD]


def gather_by_exchange(block, axis_name):
    count = lax.axis_size(axis_name)
    spread = jnp.broadcast_to(block[None], (count,) + block.shape)
    return lax.all_to_all(spread, axis_name, 0, 0, tiled=True)


def exchange_kernel(na, nz, nt, q_ref, k_ref, v_ref, q_out, k_out, v_out, spread_sems,
                    own_sems, q_sems, r_sems, l_sems):
    mesh_ids = pl.DeviceIdType.MESH
    a = lax.axis_index("ca")
    z = lax.axis_index("cz")
    t = lax.axis_index("tp")
    right = lax.rem(z + 1, nz)
    left = lax.rem(z + nz - 1, nz)
    rows = q_ref.shape[0]
    heads = q_out.shape[0]

    barrier = pltpu.get_barrier_semaphore()
    for off in range(1, nt):
        pl.semaphore_signal(barrier, inc=1, device_id=(a, z, lax.rem(t + off, nt)),
                            device_id_type=mesh_ids)
    for off in range(1, na):
        pl.semaphore_signal(barrier, inc=1, device_id=(lax.rem(a + off, na), z, t),
                            device_id_type=mesh_ids)
    for side in (left, right):
        pl.semaphore_signal(barrier, inc=1, device_id=(a, side, t), device_id_type=mesh_ids)
    pl.semaphore_wait(barrier, nt - 1 + na - 1 + 2)

    mine = pl.ds(pl.multiple_of(t * rows, rows), rows)
    sources = (q_ref, k_ref, v_ref)

    def target(i, h):
        if i == 0:
            return q_out.at[h, a, mine]
        return (k_out, v_out)[i - 1].at[h, z, mine]

    def columns(dest, h):
        return pl.ds(pl.multiple_of((dest * heads + h) * HD, HD), HD)

    own = []
    for i in range(3):
        for h in range(heads):
            copy = pltpu.make_async_copy(
                sources[i].at[:, columns(t, h)], target(i, h), own_sems.at[i, h])
            copy.start()
            own.append(copy)
    spread = [[], [], []]
    for off in range(1, nt):
        dest = lax.rem(t + off, nt)
        for i in range(3):
            for h in range(heads):
                spread[i].append(pltpu.make_async_remote_copy(
                    src_ref=sources[i].at[:, columns(dest, h)], dst_ref=target(i, h),
                    send_sem=spread_sems.at[0, i, h, off - 1],
                    recv_sem=spread_sems.at[1, i, h, off - 1],
                    device_id=(a, z, dest), device_id_type=mesh_ids))
    for group in spread:
        for copy in group:
            copy.start()
    for copy in spread[0] + own[:heads]:
        copy.wait()

    q_copies = []
    for off in range(1, na):
        copy = pltpu.make_async_remote_copy(
            src_ref=q_out.at[:, a], dst_ref=q_out.at[:, a], send_sem=q_sems.at[0, off - 1],
            recv_sem=q_sems.at[1, off - 1], device_id=(lax.rem(a + off, na), z, t),
            device_id_type=mesh_ids)
        copy.start()
        q_copies.append(copy)

    n_steps = nz // 2
    chains = ((right, r_sems, -1, {}), (left, l_sems, 1, {}))

    def parts_of(chain, step):
        if nz % 2 == 0 and step == n_steps - 1:
            return (chain,)
        return (0, 1)

    for copy in spread[1] + own[heads:2 * heads]:
        copy.wait()
    sent = []
    for step in range(n_steps):
        for part in range(2):
            for chain, (side, sems, sign, copies) in enumerate(chains):
                if part not in parts_of(chain, step):
                    continue
                slot = lax.rem(z + sign * step + nz, nz)
                if step > 0:
                    copies.pop((step - 1, part)).wait_recv()
                elif part == 1 and chain == 0:
                    for copy in spread[2] + own[2 * heads:]:
                        copy.wait()
                buf = (k_out, v_out)[part]
                copy = pltpu.make_async_remote_copy(
                    src_ref=buf.at[:, slot], dst_ref=buf.at[:, slot],
                    send_sem=sems.at[0, step * 2 + part], recv_sem=sems.at[1, step * 2 + part],
                    device_id=(a, side, t), device_id_type=mesh_ids)
                copy.start()
                copies[(step, part)] = copy
                sent.append(copy)
    for side, sems, sign, copies in chains:
        for copy in copies.values():
            copy.wait_recv()
    for copy in sent:
        copy.wait_send()
    for copy in q_copies:
        copy.wait()


def exchange(query_vectors, key_vectors, value_vectors, na, nz, nt):
    rows, width = query_vectors.shape
    heads = width // nt // HD
    n_right = nz // 2
    n_left = (nz - 1) // 2
    dtype = query_vectors.dtype
    return pl.pallas_call(
        functools.partial(exchange_kernel, na, nz, nt),
        out_shape=(
            jax.ShapeDtypeStruct((heads, na, nt * rows, HD), dtype),
            jax.ShapeDtypeStruct((heads, nz, nt * rows, HD), dtype),
            jax.ShapeDtypeStruct((heads, nz, nt * rows, HD), dtype),
        ),
        in_specs=[pl.BlockSpec(memory_space=pl.ANY)] * 3,
        out_specs=tuple(pl.BlockSpec(memory_space=pl.ANY) for _ in range(3)),
        scratch_shapes=[
            pltpu.SemaphoreType.DMA((2, 3, heads, nt - 1)),
            pltpu.SemaphoreType.DMA((3, heads)),
            pltpu.SemaphoreType.DMA((2, na - 1)),
            pltpu.SemaphoreType.DMA((2, 2 * (nz // 2))),
            pltpu.SemaphoreType.DMA((2, 2 * (nz // 2))),
        ],
        compiler_params=pltpu.CompilerParams(collective_id=0, has_side_effects=True),
    )(query_vectors, key_vectors, value_vectors)


def project_kernel(na, n_hi, parts_ref, stats_ref, w_ref, out_ref, got_parts, got_stats, att_buf,
                   pick, send1, recv1, total, send2, recv2, part_sems, stat_sems, sems1, send_sems2,
                   recv_sems2, own_stat_sem):
    mesh_ids = pl.DeviceIdType.MESH
    a = lax.axis_index("ca")
    z = lax.axis_index("cz")
    t = lax.axis_index("tp")
    core = lax.rem(t, 2)
    hi = t // 2
    partner = (a, z, hi * 2 + 1 - core)
    rows = send2.shape[1]
    heads = parts_ref.shape[0]

    barrier = pltpu.get_barrier_semaphore()
    for off in range(1, na):
        pl.semaphore_signal(barrier, inc=1, device_id=(lax.rem(a + off, na), z, t),
                            device_id_type=mesh_ids)
    pl.semaphore_signal(barrier, inc=1, device_id=partner, device_id_type=mesh_ids)
    for off in range(1, n_hi):
        pl.semaphore_signal(barrier, inc=1, device_id=(a, z, lax.rem(hi + off, n_hi) * 2 + core),
                            device_id_type=mesh_ids)
    pl.semaphore_wait(barrier, na - 1 + n_hi)

    own_stats = pltpu.make_async_copy(stats_ref.at[:, :, a], got_stats.at[na - 1], own_stat_sem)
    own_stats.start()
    stat_copies = []
    for off in range(1, na):
        dest = lax.rem(a + off, na)
        copy = pltpu.make_async_remote_copy(
            src_ref=stats_ref.at[:, :, dest], dst_ref=got_stats.at[off - 1],
            send_sem=stat_sems.at[0, off - 1], recv_sem=stat_sems.at[1, off - 1],
            device_id=(dest, z, t), device_id_type=mesh_ids)
        copy.start()
        stat_copies.append(copy)
    part_copies = []
    for h in range(heads):
        per_head = []
        for off in range(1, na):
            dest = lax.rem(a + off, na)
            copy = pltpu.make_async_remote_copy(
                src_ref=parts_ref.at[h, dest], dst_ref=got_parts.at[off - 1, h],
                send_sem=part_sems.at[0, h, off - 1], recv_sem=part_sems.at[1, h, off - 1],
                device_id=(dest, z, t), device_id_type=mesh_ids)
            copy.start()
            per_head.append(copy)
        part_copies.append(per_head)
    for copy in stat_copies:
        copy.wait()
    own_stats.wait()

    peaks = [got_stats[na - 1, 0]] + [got_stats[off - 1, 0] for off in range(1, na)]
    sums = [got_stats[na - 1, 1]] + [got_stats[off - 1, 1] for off in range(1, na)]
    top = peaks[0]
    for peak in peaks[1:]:
        top = jnp.maximum(top, peak)
    factors = [jnp.exp(peak - top) for peak in peaks]
    totals = factors[0] * sums[0]
    for factor, part_sum in zip(factors[1:], sums[1:]):
        totals = totals + factor * part_sum
    for h in range(heads):
        for copy in part_copies[h]:
            copy.wait()
        numerator = parts_ref[h, a].astype(jnp.float32) * factors[0][h][:, None]
        for off in range(1, na):
            numerator = numerator + (
                got_parts[off - 1, h].astype(jnp.float32) * factors[off][h][:, None]
            )
        att_buf[:, pl.ds(h * HD, HD)] = (numerator / totals[h][:, None]).astype(jnp.bfloat16)

    for j in range(n_hi):
        their = pl.multiple_of((j * 2 + 1 - core) * rows, rows)
        mine = pl.multiple_of((j * 2 + core) * rows, rows)
        pick[0, pl.ds(j * rows, rows), :] = att_buf[pl.ds(their, rows), :]
        pick[1, pl.ds(j * rows, rows), :] = att_buf[pl.ds(mine, rows), :]
    cols = send1.shape[1]
    chunk = cols // STAGE_CHUNKS
    firsts = []
    for k in range(STAGE_CHUNKS):
        window = pl.ds(k * chunk, chunk)
        send1[:, window] = jnp.dot(
            pick[0], w_ref[:, window], preferred_element_type=jnp.float32).astype(jnp.bfloat16)
        copy = pltpu.make_async_remote_copy(
            src_ref=send1.at[:, window], dst_ref=recv1.at[:, window], send_sem=sems1.at[0, k],
            recv_sem=sems1.at[1, k], device_id=partner, device_id_type=mesh_ids)
        copy.start()
        firsts.append(copy)
    total[...] = jnp.dot(pick[1], w_ref[...], preferred_element_type=jnp.float32).astype(
        jnp.bfloat16).astype(jnp.float32)
    second = []
    for k in range(STAGE_CHUNKS):
        window = pl.ds(k * chunk, chunk)
        firsts[k].wait()
        for j in range(n_hi):
            block = pl.ds(j * rows, rows)
            send2[j, :, window] = (
                total[block, window] + recv1[block, window].astype(jnp.float32)
            ).astype(jnp.bfloat16)
        for off in range(1, n_hi):
            dest = lax.rem(hi + off, n_hi)
            copy = pltpu.make_async_remote_copy(
                src_ref=send2.at[dest, :, window], dst_ref=recv2.at[off - 1, :, window],
                send_sem=send_sems2.at[0, k, off - 1], recv_sem=send_sems2.at[1, k, off - 1],
                device_id=(a, z, dest * 2 + core), device_id_type=mesh_ids)
            copy.start()
            second.append(copy)
    own_rows = pl.ds(pl.multiple_of(hi * rows, rows), rows)
    own = total[own_rows, :] + recv1[own_rows, :].astype(jnp.float32)
    for copy in second:
        copy.wait()
    for off in range(1, n_hi):
        own = own + recv2[off - 1].astype(jnp.float32)
    out_ref[...] = own.astype(out_ref.dtype)


def project(parts, stats, out_weight, tp_count):
    heads, na, block_rows, _ = parts.shape
    n_hi = tp_count // 2
    rows = block_rows // tp_count
    cols = out_weight.shape[1]
    vmem = pl.BlockSpec(memory_space=pltpu.VMEM)
    return pl.pallas_call(
        functools.partial(project_kernel, na, n_hi),
        out_shape=jax.ShapeDtypeStruct((rows, cols), jnp.bfloat16),
        in_specs=[vmem, vmem, vmem],
        out_specs=vmem,
        scratch_shapes=[
            pltpu.VMEM((na - 1, heads, block_rows, HD), parts.dtype),
            pltpu.VMEM((na, 2, heads, block_rows), stats.dtype),
            pltpu.VMEM((block_rows, heads * HD), jnp.bfloat16),
            pltpu.VMEM((2, n_hi * rows, heads * HD), jnp.bfloat16),
            pltpu.VMEM((n_hi * rows, cols), jnp.bfloat16),
            pltpu.VMEM((n_hi * rows, cols), jnp.bfloat16),
            pltpu.VMEM((n_hi * rows, cols), jnp.float32),
            pltpu.VMEM((n_hi, rows, cols), jnp.bfloat16),
            pltpu.VMEM((n_hi - 1, rows, cols), jnp.bfloat16),
            pltpu.SemaphoreType.DMA((2, heads, na - 1)),
            pltpu.SemaphoreType.DMA((2, na - 1)),
            pltpu.SemaphoreType.DMA((2, STAGE_CHUNKS)),
            pltpu.SemaphoreType.DMA((2, STAGE_CHUNKS, n_hi - 1)),
            pltpu.SemaphoreType.DMA((1,)),
            pltpu.SemaphoreType.DMA(()),
        ],
        compiler_params=pltpu.CompilerParams(collective_id=1, has_side_effects=True),
    )(parts, stats, out_weight)


def local(query_vectors, key_vectors, value_vectors, out_weight):
    score_scale = 1.0 / math.sqrt(HD)
    tp_count = lax.axis_size("tp")
    ca_count = lax.axis_size("ca")
    token_rows = query_vectors.shape[0]
    own_heads = query_vectors.shape[1] // HD // tp_count
    own_cols = own_heads * HD

    block_rows = token_rows * tp_count
    query_heads, key_heads, value_heads = exchange(
        query_vectors, key_vectors, value_vectors, ca_count, lax.axis_size("cz"), tp_count)
    row_peak, row_total, weighted = attend_local(
        query_heads.reshape(own_heads, -1, HD), key_heads.reshape(own_heads, -1, HD),
        value_heads.reshape(own_heads, -1, HD), score_scale)
    stats = jnp.stack([row_peak, row_total], axis=0).reshape(2, own_heads, ca_count, block_rows)
    parts = weighted.astype(jnp.bfloat16).reshape(own_heads, ca_count, block_rows, HD)
    return project(parts, stats, out_weight, tp_count)


def solution(mesh):
    ctx_count, tp_count = mesh.devices.shape
    split_mesh = Mesh(
        mesh.devices.reshape(ctx_count // KEY_SPLIT, KEY_SPLIT, tp_count), ("ca", "cz", "tp")
    )
    rows = P(("ca", "cz", "tp"), None)
    return jax.shard_map(
        local,
        mesh=split_mesh,
        in_specs=(rows, rows, rows, P("tp", None)),
        out_specs=rows,
        check_vma=False,
    )
```

```python
import functools
import math

import jax
import jax.numpy as jnp
from jax import lax
from jax.sharding import Mesh
from jax.sharding import PartitionSpec as P
from jax.experimental import pallas as pl
from jax.experimental.pallas import tpu as pltpu

HD = 128
KEY_SPLIT = 8
STAGE_CHUNKS = 4


def attend_local(query_heads, key_heads, value_heads, score_scale):
    scores = (
        jnp.einsum("hid,hjd->hij", query_heads, key_heads, preferred_element_type=jnp.float32)
        * score_scale
    )
    row_peak = jnp.max(scores, axis=-1)
    weights_low = jnp.exp(scores - row_peak[..., None]).astype(jnp.bfloat16)
    row_total = jnp.sum(weights_low.astype(jnp.float32), axis=-1)
    weighted = jnp.einsum(
        "hij,hjd->hid", weights_low, value_heads, preferred_element_type=jnp.float32
    )
    return row_peak, row_total, weighted


def gather_by_exchange(block, axis_name):
    count = lax.axis_size(axis_name)
    spread = jnp.broadcast_to(block[None], (count,) + block.shape)
    return lax.all_to_all(spread, axis_name, 0, 0, tiled=True)


def exchange_kernel(na, nz, nt, q_ref, k_ref, v_ref, q_out, k_out, v_out, spread_sems,
                    own_sems, q_sems, r_sems, l_sems):
    mesh_ids = pl.DeviceIdType.MESH
    a = lax.axis_index("ca")
    z = lax.axis_index("cz")
    t = lax.axis_index("tp")
    right = lax.rem(z + 1, nz)
    left = lax.rem(z + nz - 1, nz)
    rows = q_ref.shape[0]
    heads = q_out.shape[0]

    barrier = pltpu.get_barrier_semaphore()
    for off in range(1, nt):
        pl.semaphore_signal(barrier, inc=1, device_id=(a, z, lax.rem(t + off, nt)),
                            device_id_type=mesh_ids)
    for off in range(1, na):
        pl.semaphore_signal(barrier, inc=1, device_id=(lax.rem(a + off, na), z, t),
                            device_id_type=mesh_ids)
    for side in (left, right):
        pl.semaphore_signal(barrier, inc=1, device_id=(a, side, t), device_id_type=mesh_ids)
    pl.semaphore_wait(barrier, nt - 1 + na - 1 + 2)

    mine = pl.ds(pl.multiple_of(t * rows, rows), rows)
    sources = (q_ref, k_ref, v_ref)

    def target(i, h):
        if i == 0:
            return q_out.at[h, a, mine]
        return (k_out, v_out)[i - 1].at[h, z, mine]

    def columns(dest, h):
        return pl.ds(pl.multiple_of((dest * heads + h) * HD, HD), HD)

    own = []
    for i in range(3):
        for h in range(heads):
            copy = pltpu.make_async_copy(
                sources[i].at[:, columns(t, h)], target(i, h), own_sems.at[i, h])
            copy.start()
            own.append(copy)
    spread = [[], [], []]
    for off in range(1, nt):
        dest = lax.rem(t + off, nt)
        for i in range(3):
            for h in range(heads):
                spread[i].append(pltpu.make_async_remote_copy(
                    src_ref=sources[i].at[:, columns(dest, h)], dst_ref=target(i, h),
                    send_sem=spread_sems.at[0, i, h, off - 1],
                    recv_sem=spread_sems.at[1, i, h, off - 1],
                    device_id=(a, z, dest), device_id_type=mesh_ids))
    for group in spread:
        for copy in group:
            copy.start()
    q_copies = []

    def push_queries():
        for copy in spread[0] + own[:heads]:
            copy.wait()
        for off in range(1, na):
            copy = pltpu.make_async_remote_copy(
                src_ref=q_out.at[:, a], dst_ref=q_out.at[:, a], send_sem=q_sems.at[0, off - 1],
                recv_sem=q_sems.at[1, off - 1], device_id=(lax.rem(a + off, na), z, t),
                device_id_type=mesh_ids)
            copy.start()
            q_copies.append(copy)

    n_steps = nz // 2
    chains = ((right, r_sems, -1, {}), (left, l_sems, 1, {}))

    def parts_of(chain, step):
        if nz % 2 == 0 and step == n_steps - 1:
            return (chain,)
        return (0, 1)

    for copy in spread[1] + own[heads:2 * heads]:
        copy.wait()
    sent = []
    for step in range(n_steps):
        for part in range(2):
            for chain, (side, sems, sign, copies) in enumerate(chains):
                if part not in parts_of(chain, step):
                    continue
                slot = lax.rem(z + sign * step + nz, nz)
                if step > 0:
                    copies.pop((step - 1, part)).wait_recv()
                elif part == 1 and chain == 0:
                    push_queries()
                    for copy in spread[2] + own[2 * heads:]:
                        copy.wait()
                buf = (k_out, v_out)[part]
                copy = pltpu.make_async_remote_copy(
                    src_ref=buf.at[:, slot], dst_ref=buf.at[:, slot],
                    send_sem=sems.at[0, step * 2 + part], recv_sem=sems.at[1, step * 2 + part],
                    device_id=(a, side, t), device_id_type=mesh_ids)
                copy.start()
                copies[(step, part)] = copy
                sent.append(copy)
    for side, sems, sign, copies in chains:
        for copy in copies.values():
            copy.wait_recv()
    for copy in sent:
        copy.wait_send()
    for copy in q_copies:
        copy.wait()


def exchange(query_vectors, key_vectors, value_vectors, na, nz, nt):
    rows, width = query_vectors.shape
    heads = width // nt // HD
    n_right = nz // 2
    n_left = (nz - 1) // 2
    dtype = query_vectors.dtype
    return pl.pallas_call(
        functools.partial(exchange_kernel, na, nz, nt),
        out_shape=(
            jax.ShapeDtypeStruct((heads, na, nt * rows, HD), dtype),
            jax.ShapeDtypeStruct((heads, nz, nt * rows, HD), dtype),
            jax.ShapeDtypeStruct((heads, nz, nt * rows, HD), dtype),
        ),
        in_specs=[pl.BlockSpec(memory_space=pl.ANY)] * 3,
        out_specs=tuple(pl.BlockSpec(memory_space=pl.ANY) for _ in range(3)),
        scratch_shapes=[
            pltpu.SemaphoreType.DMA((2, 3, heads, nt - 1)),
            pltpu.SemaphoreType.DMA((3, heads)),
            pltpu.SemaphoreType.DMA((2, na - 1)),
            pltpu.SemaphoreType.DMA((2, 2 * (nz // 2))),
            pltpu.SemaphoreType.DMA((2, 2 * (nz // 2))),
        ],
        compiler_params=pltpu.CompilerParams(collective_id=0, has_side_effects=True),
    )(query_vectors, key_vectors, value_vectors)


def project_kernel(na, n_hi, parts_ref, stats_ref, w_ref, out_ref, got_parts, got_stats, att_buf,
                   pick, send1, recv1, total, send2, recv2, part_sems, stat_sems, sems1, send_sems2,
                   recv_sems2, own_stat_sem):
    mesh_ids = pl.DeviceIdType.MESH
    a = lax.axis_index("ca")
    z = lax.axis_index("cz")
    t = lax.axis_index("tp")
    core = lax.rem(t, 2)
    hi = t // 2
    partner = (a, z, hi * 2 + 1 - core)
    rows = send2.shape[1]
    heads = parts_ref.shape[0]

    barrier = pltpu.get_barrier_semaphore()
    for off in range(1, na):
        pl.semaphore_signal(barrier, inc=1, device_id=(lax.rem(a + off, na), z, t),
                            device_id_type=mesh_ids)
    pl.semaphore_signal(barrier, inc=1, device_id=partner, device_id_type=mesh_ids)
    for off in range(1, n_hi):
        pl.semaphore_signal(barrier, inc=1, device_id=(a, z, lax.rem(hi + off, n_hi) * 2 + core),
                            device_id_type=mesh_ids)
    pl.semaphore_wait(barrier, na - 1 + n_hi)

    own_stats = pltpu.make_async_copy(stats_ref.at[:, :, a], got_stats.at[na - 1], own_stat_sem)
    own_stats.start()
    stat_copies = []
    for off in range(1, na):
        dest = lax.rem(a + off, na)
        copy = pltpu.make_async_remote_copy(
            src_ref=stats_ref.at[:, :, dest], dst_ref=got_stats.at[off - 1],
            send_sem=stat_sems.at[0, off - 1], recv_sem=stat_sems.at[1, off - 1],
            device_id=(dest, z, t), device_id_type=mesh_ids)
        copy.start()
        stat_copies.append(copy)
    part_copies = []
    for h in range(heads):
        per_head = []
        for off in range(1, na):
            dest = lax.rem(a + off, na)
            copy = pltpu.make_async_remote_copy(
                src_ref=parts_ref.at[h, dest], dst_ref=got_parts.at[off - 1, h],
                send_sem=part_sems.at[0, h, off - 1], recv_sem=part_sems.at[1, h, off - 1],
                device_id=(dest, z, t), device_id_type=mesh_ids)
            copy.start()
            per_head.append(copy)
        part_copies.append(per_head)
    for copy in stat_copies:
        copy.wait()
    own_stats.wait()

    peaks = [got_stats[na - 1, 0]] + [got_stats[off - 1, 0] for off in range(1, na)]
    sums = [got_stats[na - 1, 1]] + [got_stats[off - 1, 1] for off in range(1, na)]
    top = peaks[0]
    for peak in peaks[1:]:
        top = jnp.maximum(top, peak)
    factors = [jnp.exp(peak - top) for peak in peaks]
    totals = factors[0] * sums[0]
    for factor, part_sum in zip(factors[1:], sums[1:]):
        totals = totals + factor * part_sum
    for h in range(heads):
        for copy in part_copies[h]:
            copy.wait()
        numerator = parts_ref[h, a].astype(jnp.float32) * factors[0][h][:, None]
        for off in range(1, na):
            numerator = numerator + (
                got_parts[off - 1, h].astype(jnp.float32) * factors[off][h][:, None]
            )
        att_buf[:, pl.ds(h * HD, HD)] = (numerator / totals[h][:, None]).astype(jnp.bfloat16)

    for j in range(n_hi):
        their = pl.multiple_of((j * 2 + 1 - core) * rows, rows)
        mine = pl.multiple_of((j * 2 + core) * rows, rows)
        pick[0, pl.ds(j * rows, rows), :] = att_buf[pl.ds(their, rows), :]
        pick[1, pl.ds(j * rows, rows), :] = att_buf[pl.ds(mine, rows), :]
    cols = send1.shape[1]
    chunk = cols // STAGE_CHUNKS
    firsts = []
    for k in range(STAGE_CHUNKS):
        window = pl.ds(k * chunk, chunk)
        send1[:, window] = jnp.dot(
            pick[0], w_ref[:, window], preferred_element_type=jnp.float32).astype(jnp.bfloat16)
        copy = pltpu.make_async_remote_copy(
            src_ref=send1.at[:, window], dst_ref=recv1.at[:, window], send_sem=sems1.at[0, k],
            recv_sem=sems1.at[1, k], device_id=partner, device_id_type=mesh_ids)
        copy.start()
        firsts.append(copy)
    total[...] = jnp.dot(pick[1], w_ref[...], preferred_element_type=jnp.float32).astype(
        jnp.bfloat16).astype(jnp.float32)
    second = []
    for k in range(STAGE_CHUNKS):
        window = pl.ds(k * chunk, chunk)
        firsts[k].wait()
        for j in range(n_hi):
            block = pl.ds(j * rows, rows)
            send2[j, :, window] = (
                total[block, window] + recv1[block, window].astype(jnp.float32)
            ).astype(jnp.bfloat16)
        for off in range(1, n_hi):
            dest = lax.rem(hi + off, n_hi)
            copy = pltpu.make_async_remote_copy(
                src_ref=send2.at[dest, :, window], dst_ref=recv2.at[off - 1, :, window],
                send_sem=send_sems2.at[0, k, off - 1], recv_sem=send_sems2.at[1, k, off - 1],
                device_id=(a, z, dest * 2 + core), device_id_type=mesh_ids)
            copy.start()
            second.append(copy)
    own_rows = pl.ds(pl.multiple_of(hi * rows, rows), rows)
    own = total[own_rows, :] + recv1[own_rows, :].astype(jnp.float32)
    for copy in second:
        copy.wait()
    for off in range(1, n_hi):
        own = own + recv2[off - 1].astype(jnp.float32)
    out_ref[...] = own.astype(out_ref.dtype)


def project(parts, stats, out_weight, tp_count):
    heads, na, block_rows, _ = parts.shape
    n_hi = tp_count // 2
    rows = block_rows // tp_count
    cols = out_weight.shape[1]
    vmem = pl.BlockSpec(memory_space=pltpu.VMEM)
    return pl.pallas_call(
        functools.partial(project_kernel, na, n_hi),
        out_shape=jax.ShapeDtypeStruct((rows, cols), jnp.bfloat16),
        in_specs=[vmem, vmem, vmem],
        out_specs=vmem,
        scratch_shapes=[
            pltpu.VMEM((na - 1, heads, block_rows, HD), parts.dtype),
            pltpu.VMEM((na, 2, heads, block_rows), stats.dtype),
            pltpu.VMEM((block_rows, heads * HD), jnp.bfloat16),
            pltpu.VMEM((2, n_hi * rows, heads * HD), jnp.bfloat16),
            pltpu.VMEM((n_hi * rows, cols), jnp.bfloat16),
            pltpu.VMEM((n_hi * rows, cols), jnp.bfloat16),
            pltpu.VMEM((n_hi * rows, cols), jnp.float32),
            pltpu.VMEM((n_hi, rows, cols), jnp.bfloat16),
            pltpu.VMEM((n_hi - 1, rows, cols), jnp.bfloat16),
            pltpu.SemaphoreType.DMA((2, heads, na - 1)),
            pltpu.SemaphoreType.DMA((2, na - 1)),
            pltpu.SemaphoreType.DMA((2, STAGE_CHUNKS)),
            pltpu.SemaphoreType.DMA((2, STAGE_CHUNKS, n_hi - 1)),
            pltpu.SemaphoreType.DMA((1,)),
            pltpu.SemaphoreType.DMA(()),
        ],
        compiler_params=pltpu.CompilerParams(collective_id=1, has_side_effects=True),
    )(parts, stats, out_weight)


def local(query_vectors, key_vectors, value_vectors, out_weight):
    score_scale = 1.0 / math.sqrt(HD)
    tp_count = lax.axis_size("tp")
    ca_count = lax.axis_size("ca")
    token_rows = query_vectors.shape[0]
    own_heads = query_vectors.shape[1] // HD // tp_count
    own_cols = own_heads * HD

    block_rows = token_rows * tp_count
    query_heads, key_heads, value_heads = exchange(
        query_vectors, key_vectors, value_vectors, ca_count, lax.axis_size("cz"), tp_count)
    row_peak, row_total, weighted = attend_local(
        query_heads.reshape(own_heads, -1, HD), key_heads.reshape(own_heads, -1, HD),
        value_heads.reshape(own_heads, -1, HD), score_scale)
    stats = jnp.stack([row_peak, row_total], axis=0).reshape(2, own_heads, ca_count, block_rows)
    parts = weighted.astype(jnp.bfloat16).reshape(own_heads, ca_count, block_rows, HD)
    return project(parts, stats, out_weight, tp_count)


def solution(mesh):
    ctx_count, tp_count = mesh.devices.shape
    split_mesh = Mesh(
        mesh.devices.reshape(ctx_count // KEY_SPLIT, KEY_SPLIT, tp_count), ("ca", "cz", "tp")
    )
    rows = P(("ca", "cz", "tp"), None)
    return jax.shard_map(
        local,
        mesh=split_mesh,
        in_specs=(rows, rows, rows, P("tp", None)),
        out_specs=rows,
        check_vma=False,
    )
```

```python
import functools
import math

import jax
import jax.numpy as jnp
from jax import lax
from jax.sharding import Mesh
from jax.sharding import PartitionSpec as P
from jax.experimental import pallas as pl
from jax.experimental.pallas import tpu as pltpu

HD = 128
KEY_SPLIT = 8
STAGE_CHUNKS = 4


def attend_local(query_heads, key_heads, value_heads, score_scale):
    scores = (
        jnp.einsum("hid,hjd->hij", query_heads, key_heads, preferred_element_type=jnp.float32)
        * score_scale
    )
    row_peak = jnp.max(scores, axis=-1)
    weights_low = jnp.exp(scores - row_peak[..., None]).astype(jnp.bfloat16)
    row_total = jnp.sum(weights_low.astype(jnp.float32), axis=-1)
    weighted = jnp.einsum(
        "hij,hjd->hid", weights_low, value_heads, preferred_element_type=jnp.float32
    )
    return row_peak, row_total, weighted


def gather_by_exchange(block, axis_name):
    count = lax.axis_size(axis_name)
    spread = jnp.broadcast_to(block[None], (count,) + block.shape)
    return lax.all_to_all(spread, axis_name, 0, 0, tiled=True)


def exchange_kernel(na, nz, nt, q_ref, k_ref, v_ref, q_out, k_out, v_out, spread_sems,
                    own_sems, q_sems, r_sems, l_sems):
    mesh_ids = pl.DeviceIdType.MESH
    a = lax.axis_index("ca")
    z = lax.axis_index("cz")
    t = lax.axis_index("tp")
    right = lax.rem(z + 1, nz)
    left = lax.rem(z + nz - 1, nz)
    rows = q_ref.shape[0]
    heads = q_out.shape[0]

    barrier = pltpu.get_barrier_semaphore()
    for off in range(1, nt):
        pl.semaphore_signal(barrier, inc=1, device_id=(a, z, lax.rem(t + off, nt)),
                            device_id_type=mesh_ids)
    for off in range(1, na):
        pl.semaphore_signal(barrier, inc=1, device_id=(lax.rem(a + off, na), z, t),
                            device_id_type=mesh_ids)
    for side in (left, right):
        pl.semaphore_signal(barrier, inc=1, device_id=(a, side, t), device_id_type=mesh_ids)
    pl.semaphore_wait(barrier, nt - 1 + na - 1 + 2)

    mine = pl.ds(pl.multiple_of(t * rows, rows), rows)
    sources = (q_ref, k_ref, v_ref)

    def target(i, h):
        if i == 0:
            return q_out.at[h, a, mine]
        return (k_out, v_out)[i - 1].at[h, z, mine]

    def columns(dest, h):
        return pl.ds(pl.multiple_of((dest * heads + h) * HD, HD), HD)

    own = []
    for i in range(3):
        for h in range(heads):
            copy = pltpu.make_async_copy(
                sources[i].at[:, columns(t, h)], target(i, h), own_sems.at[i, h])
            copy.start()
            own.append(copy)
    spread = [[], [], []]
    for off in range(1, nt):
        dest = lax.rem(t + off, nt)
        for i in range(3):
            for h in range(heads):
                spread[i].append(pltpu.make_async_remote_copy(
                    src_ref=sources[i].at[:, columns(dest, h)], dst_ref=target(i, h),
                    send_sem=spread_sems.at[0, i, h, off - 1],
                    recv_sem=spread_sems.at[1, i, h, off - 1],
                    device_id=(a, z, dest), device_id_type=mesh_ids))
    for group in spread:
        for copy in group:
            copy.start()
    q_copies = []

    def push_queries():
        for copy in spread[0] + own[:heads]:
            copy.wait()
        for off in range(1, na):
            copy = pltpu.make_async_remote_copy(
                src_ref=q_out.at[:, a], dst_ref=q_out.at[:, a], send_sem=q_sems.at[0, off - 1],
                recv_sem=q_sems.at[1, off - 1], device_id=(lax.rem(a + off, na), z, t),
                device_id_type=mesh_ids)
            copy.start()
            q_copies.append(copy)

    n_steps = nz // 2
    chains = ((right, r_sems, -1, {}), (left, l_sems, 1, {}))

    def parts_of(chain, step):
        if nz % 2 == 0 and step == n_steps - 1:
            return (chain,)
        return (0, 1)

    for copy in spread[1] + own[heads:2 * heads]:
        copy.wait()
    sent = []
    for step in range(n_steps):
        for part in range(2):
            for chain, (side, sems, sign, copies) in enumerate(chains):
                if part not in parts_of(chain, step):
                    continue
                slot = lax.rem(z + sign * step + nz, nz)
                if step > 0:
                    copies.pop((step - 1, part)).wait_recv()
                elif part == 1 and chain == 0:
                    push_queries()
                    for copy in spread[2] + own[2 * heads:]:
                        copy.wait()
                buf = (k_out, v_out)[part]
                copy = pltpu.make_async_remote_copy(
                    src_ref=buf.at[:, slot], dst_ref=buf.at[:, slot],
                    send_sem=sems.at[0, step * 2 + part], recv_sem=sems.at[1, step * 2 + part],
                    device_id=(a, side, t), device_id_type=mesh_ids)
                copy.start()
                copies[(step, part)] = copy
                sent.append(copy)
    for side, sems, sign, copies in chains:
        for copy in copies.values():
            copy.wait_recv()
    for copy in sent:
        copy.wait_send()
    for copy in q_copies:
        copy.wait()


def exchange(query_vectors, key_vectors, value_vectors, na, nz, nt):
    rows, width = query_vectors.shape
    heads = width // nt // HD
    n_right = nz // 2
    n_left = (nz - 1) // 2
    dtype = query_vectors.dtype
    return pl.pallas_call(
        functools.partial(exchange_kernel, na, nz, nt),
        out_shape=(
            jax.ShapeDtypeStruct((heads, na, nt * rows, HD), dtype),
            jax.ShapeDtypeStruct((heads, nz, nt * rows, HD), dtype),
            jax.ShapeDtypeStruct((heads, nz, nt * rows, HD), dtype),
        ),
        in_specs=[pl.BlockSpec(memory_space=pl.ANY)] * 3,
        out_specs=tuple(pl.BlockSpec(memory_space=pl.ANY) for _ in range(3)),
        scratch_shapes=[
            pltpu.SemaphoreType.DMA((2, 3, heads, nt - 1)),
            pltpu.SemaphoreType.DMA((3, heads)),
            pltpu.SemaphoreType.DMA((2, na - 1)),
            pltpu.SemaphoreType.DMA((2, 2 * (nz // 2))),
            pltpu.SemaphoreType.DMA((2, 2 * (nz // 2))),
        ],
        compiler_params=pltpu.CompilerParams(collective_id=0, has_side_effects=True),
    )(query_vectors, key_vectors, value_vectors)


def project_kernel(na, n_hi, parts_ref, peak_ref, sum_ref, w_ref, out_ref, got_parts, got_stats, att_buf,
                   pick, send1, recv1, total, send2, recv2, part_sems, stat_sems, sems1, send_sems2,
                   recv_sems2, own_stat_sem):
    mesh_ids = pl.DeviceIdType.MESH
    a = lax.axis_index("ca")
    z = lax.axis_index("cz")
    t = lax.axis_index("tp")
    core = lax.rem(t, 2)
    hi = t // 2
    partner = (a, z, hi * 2 + 1 - core)
    rows = send2.shape[1]
    heads = parts_ref.shape[0]

    barrier = pltpu.get_barrier_semaphore()
    for off in range(1, na):
        pl.semaphore_signal(barrier, inc=1, device_id=(lax.rem(a + off, na), z, t),
                            device_id_type=mesh_ids)
    pl.semaphore_signal(barrier, inc=1, device_id=partner, device_id_type=mesh_ids)
    for off in range(1, n_hi):
        pl.semaphore_signal(barrier, inc=1, device_id=(a, z, lax.rem(hi + off, n_hi) * 2 + core),
                            device_id_type=mesh_ids)
    pl.semaphore_wait(barrier, na - 1 + n_hi)

    stat_refs = (peak_ref, sum_ref)
    own_stats = []
    for k in range(2):
        copy = pltpu.make_async_copy(
            stat_refs[k].at[:, a], got_stats.at[na - 1, k], own_stat_sem.at[k])
        copy.start()
        own_stats.append(copy)
    stat_copies = []
    for off in range(1, na):
        dest = lax.rem(a + off, na)
        for k in range(2):
            copy = pltpu.make_async_remote_copy(
                src_ref=stat_refs[k].at[:, dest], dst_ref=got_stats.at[off - 1, k],
                send_sem=stat_sems.at[0, k, off - 1], recv_sem=stat_sems.at[1, k, off - 1],
                device_id=(dest, z, t), device_id_type=mesh_ids)
            copy.start()
            stat_copies.append(copy)
    part_copies = []
    for h in range(heads):
        per_head = []
        for off in range(1, na):
            dest = lax.rem(a + off, na)
            copy = pltpu.make_async_remote_copy(
                src_ref=parts_ref.at[h, dest], dst_ref=got_parts.at[off - 1, h],
                send_sem=part_sems.at[0, h, off - 1], recv_sem=part_sems.at[1, h, off - 1],
                device_id=(dest, z, t), device_id_type=mesh_ids)
            copy.start()
            per_head.append(copy)
        part_copies.append(per_head)
    for copy in stat_copies + own_stats:
        copy.wait()

    peaks = [got_stats[na - 1, 0]] + [got_stats[off - 1, 0] for off in range(1, na)]
    sums = [got_stats[na - 1, 1]] + [got_stats[off - 1, 1] for off in range(1, na)]
    top = peaks[0]
    for peak in peaks[1:]:
        top = jnp.maximum(top, peak)
    factors = [jnp.exp(peak - top) for peak in peaks]
    totals = factors[0] * sums[0]
    for factor, part_sum in zip(factors[1:], sums[1:]):
        totals = totals + factor * part_sum
    for h in range(heads):
        for copy in part_copies[h]:
            copy.wait()
        numerator = parts_ref[h, a].astype(jnp.float32) * factors[0][h][:, None]
        for off in range(1, na):
            numerator = numerator + (
                got_parts[off - 1, h].astype(jnp.float32) * factors[off][h][:, None]
            )
        att_buf[:, pl.ds(h * HD, HD)] = (numerator / totals[h][:, None]).astype(jnp.bfloat16)

    for j in range(n_hi):
        their = pl.multiple_of((j * 2 + 1 - core) * rows, rows)
        mine = pl.multiple_of((j * 2 + core) * rows, rows)
        pick[0, pl.ds(j * rows, rows), :] = att_buf[pl.ds(their, rows), :]
        pick[1, pl.ds(j * rows, rows), :] = att_buf[pl.ds(mine, rows), :]
    cols = send1.shape[1]
    chunk = cols // STAGE_CHUNKS
    firsts = []
    for k in range(STAGE_CHUNKS):
        window = pl.ds(k * chunk, chunk)
        send1[:, window] = jnp.dot(
            pick[0], w_ref[:, window], preferred_element_type=jnp.float32).astype(jnp.bfloat16)
        copy = pltpu.make_async_remote_copy(
            src_ref=send1.at[:, window], dst_ref=recv1.at[:, window], send_sem=sems1.at[0, k],
            recv_sem=sems1.at[1, k], device_id=partner, device_id_type=mesh_ids)
        copy.start()
        firsts.append(copy)
    total[...] = jnp.dot(pick[1], w_ref[...], preferred_element_type=jnp.float32).astype(
        jnp.bfloat16).astype(jnp.float32)
    second = []
    for k in range(STAGE_CHUNKS):
        window = pl.ds(k * chunk, chunk)
        firsts[k].wait()
        for j in range(n_hi):
            block = pl.ds(j * rows, rows)
            send2[j, :, window] = (
                total[block, window] + recv1[block, window].astype(jnp.float32)
            ).astype(jnp.bfloat16)
        for off in range(1, n_hi):
            dest = lax.rem(hi + off, n_hi)
            copy = pltpu.make_async_remote_copy(
                src_ref=send2.at[dest, :, window], dst_ref=recv2.at[off - 1, :, window],
                send_sem=send_sems2.at[0, k, off - 1], recv_sem=send_sems2.at[1, k, off - 1],
                device_id=(a, z, dest * 2 + core), device_id_type=mesh_ids)
            copy.start()
            second.append(copy)
    own_rows = pl.ds(pl.multiple_of(hi * rows, rows), rows)
    own = total[own_rows, :] + recv1[own_rows, :].astype(jnp.float32)
    for copy in second:
        copy.wait()
    for off in range(1, n_hi):
        own = own + recv2[off - 1].astype(jnp.float32)
    out_ref[...] = own.astype(out_ref.dtype)


def project(parts, peak, row_sum, out_weight, tp_count):
    heads, na, block_rows, _ = parts.shape
    n_hi = tp_count // 2
    rows = block_rows // tp_count
    cols = out_weight.shape[1]
    vmem = pl.BlockSpec(memory_space=pltpu.VMEM)
    return pl.pallas_call(
        functools.partial(project_kernel, na, n_hi),
        out_shape=jax.ShapeDtypeStruct((rows, cols), jnp.bfloat16),
        in_specs=[vmem, vmem, vmem, vmem],
        out_specs=vmem,
        scratch_shapes=[
            pltpu.VMEM((na - 1, heads, block_rows, HD), parts.dtype),
            pltpu.VMEM((na, 2, heads, block_rows), peak.dtype),
            pltpu.VMEM((block_rows, heads * HD), jnp.bfloat16),
            pltpu.VMEM((2, n_hi * rows, heads * HD), jnp.bfloat16),
            pltpu.VMEM((n_hi * rows, cols), jnp.bfloat16),
            pltpu.VMEM((n_hi * rows, cols), jnp.bfloat16),
            pltpu.VMEM((n_hi * rows, cols), jnp.float32),
            pltpu.VMEM((n_hi, rows, cols), jnp.bfloat16),
            pltpu.VMEM((n_hi - 1, rows, cols), jnp.bfloat16),
            pltpu.SemaphoreType.DMA((2, heads, na - 1)),
            pltpu.SemaphoreType.DMA((2, 2, na - 1)),
            pltpu.SemaphoreType.DMA((2, STAGE_CHUNKS)),
            pltpu.SemaphoreType.DMA((2, STAGE_CHUNKS, n_hi - 1)),
            pltpu.SemaphoreType.DMA((1,)),
            pltpu.SemaphoreType.DMA((2,)),
        ],
        compiler_params=pltpu.CompilerParams(collective_id=1, has_side_effects=True),
    )(parts, peak, row_sum, out_weight)


def local(query_vectors, key_vectors, value_vectors, out_weight):
    score_scale = 1.0 / math.sqrt(HD)
    tp_count = lax.axis_size("tp")
    ca_count = lax.axis_size("ca")
    token_rows = query_vectors.shape[0]
    own_heads = query_vectors.shape[1] // HD // tp_count
    own_cols = own_heads * HD

    block_rows = token_rows * tp_count
    query_heads, key_heads, value_heads = exchange(
        query_vectors, key_vectors, value_vectors, ca_count, lax.axis_size("cz"), tp_count)
    row_peak, row_total, weighted = attend_local(
        query_heads.reshape(own_heads, -1, HD), key_heads.reshape(own_heads, -1, HD),
        value_heads.reshape(own_heads, -1, HD), score_scale)
    peak = row_peak.reshape(own_heads, ca_count, block_rows)
    row_sum = row_total.reshape(own_heads, ca_count, block_rows)
    parts = weighted.astype(jnp.bfloat16).reshape(own_heads, ca_count, block_rows, HD)
    return project(parts, peak, row_sum, out_weight, tp_count)


def solution(mesh):
    ctx_count, tp_count = mesh.devices.shape
    split_mesh = Mesh(
        mesh.devices.reshape(ctx_count // KEY_SPLIT, KEY_SPLIT, tp_count), ("ca", "cz", "tp")
    )
    rows = P(("ca", "cz", "tp"), None)
    return jax.shard_map(
        local,
        mesh=split_mesh,
        in_specs=(rows, rows, rows, P("tp", None)),
        out_specs=rows,
        check_vma=False,
    )
```

```python
import functools
import math

import jax
import jax.numpy as jnp
from jax import lax
from jax.sharding import Mesh
from jax.sharding import PartitionSpec as P
from jax.experimental import pallas as pl
from jax.experimental.pallas import tpu as pltpu

HD = 128
KEY_SPLIT = 8
STAGE_CHUNKS = 4


def attend_local(query_heads, key_heads, value_heads, score_scale):
    scores = (
        jnp.einsum("hid,hjd->hij", query_heads, key_heads, preferred_element_type=jnp.float32)
        * score_scale
    )
    row_peak = jnp.max(scores, axis=-1)
    weights_low = jnp.exp(scores - row_peak[..., None]).astype(jnp.bfloat16)
    row_total = jnp.sum(weights_low.astype(jnp.float32), axis=-1)
    weighted = jnp.einsum(
        "hij,hjd->hid", weights_low, value_heads, preferred_element_type=jnp.float32
    )
    return row_peak, row_total, weighted


def gather_by_exchange(block, axis_name):
    count = lax.axis_size(axis_name)
    spread = jnp.broadcast_to(block[None], (count,) + block.shape)
    return lax.all_to_all(spread, axis_name, 0, 0, tiled=True)


def exchange_kernel(na, nz, nt, q_ref, k_ref, v_ref, q_out, k_out, v_out, spread_sems,
                    own_sems, q_sems, r_sems, l_sems):
    mesh_ids = pl.DeviceIdType.MESH
    a = lax.axis_index("ca")
    z = lax.axis_index("cz")
    t = lax.axis_index("tp")
    right = lax.rem(z + 1, nz)
    left = lax.rem(z + nz - 1, nz)
    rows = q_ref.shape[0]
    heads = q_out.shape[0]

    barrier = pltpu.get_barrier_semaphore()
    for off in range(1, nt):
        pl.semaphore_signal(barrier, inc=1, device_id=(a, z, lax.rem(t + off, nt)),
                            device_id_type=mesh_ids)
    for off in range(1, na):
        pl.semaphore_signal(barrier, inc=1, device_id=(lax.rem(a + off, na), z, t),
                            device_id_type=mesh_ids)
    for side in (left, right):
        pl.semaphore_signal(barrier, inc=1, device_id=(a, side, t), device_id_type=mesh_ids)
    pl.semaphore_wait(barrier, nt - 1 + na - 1 + 2)

    mine = pl.ds(pl.multiple_of(t * rows, rows), rows)
    sources = (q_ref, k_ref, v_ref)

    def target(i, h):
        if i == 0:
            return q_out.at[h, a, mine]
        return (k_out, v_out)[i - 1].at[h, z, mine]

    def columns(dest, h):
        return pl.ds(pl.multiple_of((dest * heads + h) * HD, HD), HD)

    own = []
    for i in range(3):
        for h in range(heads):
            copy = pltpu.make_async_copy(
                sources[i].at[:, columns(t, h)], target(i, h), own_sems.at[i, h])
            copy.start()
            own.append(copy)
    spread = [[], [], []]
    for off in range(1, nt):
        dest = lax.rem(t + off, nt)
        for i in range(3):
            for h in range(heads):
                spread[i].append(pltpu.make_async_remote_copy(
                    src_ref=sources[i].at[:, columns(dest, h)], dst_ref=target(i, h),
                    send_sem=spread_sems.at[0, i, h, off - 1],
                    recv_sem=spread_sems.at[1, i, h, off - 1],
                    device_id=(a, z, dest), device_id_type=mesh_ids))
    for group in spread:
        for copy in group:
            copy.start()
    q_copies = []

    def push_queries():
        for copy in spread[0] + own[:heads]:
            copy.wait()
        for off in range(1, na):
            copy = pltpu.make_async_remote_copy(
                src_ref=q_out.at[:, a], dst_ref=q_out.at[:, a], send_sem=q_sems.at[0, off - 1],
                recv_sem=q_sems.at[1, off - 1], device_id=(lax.rem(a + off, na), z, t),
                device_id_type=mesh_ids)
            copy.start()
            q_copies.append(copy)

    n_steps = nz // 2
    chains = ((right, r_sems, -1, {}), (left, l_sems, 1, {}))

    def parts_of(chain, step):
        if nz % 2 == 0 and step == n_steps - 1:
            return (chain,)
        return (0, 1)

    for copy in spread[1] + own[heads:2 * heads]:
        copy.wait()
    sent = []
    for step in range(n_steps):
        for part in range(2):
            for chain, (side, sems, sign, copies) in enumerate(chains):
                if part not in parts_of(chain, step):
                    continue
                slot = lax.rem(z + sign * step + nz, nz)
                if step > 0:
                    copies.pop((step - 1, part)).wait_recv()
                elif part == 1 and chain == 0:
                    push_queries()
                    for copy in spread[2] + own[2 * heads:]:
                        copy.wait()
                buf = (k_out, v_out)[part]
                copy = pltpu.make_async_remote_copy(
                    src_ref=buf.at[:, slot], dst_ref=buf.at[:, slot],
                    send_sem=sems.at[0, step * 2 + part], recv_sem=sems.at[1, step * 2 + part],
                    device_id=(a, side, t), device_id_type=mesh_ids)
                copy.start()
                copies[(step, part)] = copy
                sent.append(copy)
    for side, sems, sign, copies in chains:
        for copy in copies.values():
            copy.wait_recv()
    for copy in sent:
        copy.wait_send()
    for copy in q_copies:
        copy.wait()


def exchange(query_vectors, key_vectors, value_vectors, na, nz, nt):
    rows, width = query_vectors.shape
    heads = width // nt // HD
    n_right = nz // 2
    n_left = (nz - 1) // 2
    dtype = query_vectors.dtype
    return pl.pallas_call(
        functools.partial(exchange_kernel, na, nz, nt),
        out_shape=(
            jax.ShapeDtypeStruct((heads, na, nt * rows, HD), dtype),
            jax.ShapeDtypeStruct((heads, nz, nt * rows, HD), dtype),
            jax.ShapeDtypeStruct((heads, nz, nt * rows, HD), dtype),
        ),
        in_specs=[pl.BlockSpec(memory_space=pl.ANY)] * 3,
        out_specs=tuple(pl.BlockSpec(memory_space=pltpu.VMEM) for _ in range(3)),
        scratch_shapes=[
            pltpu.SemaphoreType.DMA((2, 3, heads, nt - 1)),
            pltpu.SemaphoreType.DMA((3, heads)),
            pltpu.SemaphoreType.DMA((2, na - 1)),
            pltpu.SemaphoreType.DMA((2, 2 * (nz // 2))),
            pltpu.SemaphoreType.DMA((2, 2 * (nz // 2))),
        ],
        compiler_params=pltpu.CompilerParams(collective_id=0, has_side_effects=True),
    )(query_vectors, key_vectors, value_vectors)


def project_kernel(na, n_hi, parts_ref, stats_ref, w_ref, out_ref, got_parts, got_stats, att_buf,
                   pick, send1, recv1, total, send2, recv2, part_sems, stat_sems, sems1, send_sems2,
                   recv_sems2, own_stat_sem):
    mesh_ids = pl.DeviceIdType.MESH
    a = lax.axis_index("ca")
    z = lax.axis_index("cz")
    t = lax.axis_index("tp")
    core = lax.rem(t, 2)
    hi = t // 2
    partner = (a, z, hi * 2 + 1 - core)
    rows = send2.shape[1]
    heads = parts_ref.shape[0]

    barrier = pltpu.get_barrier_semaphore()
    for off in range(1, na):
        pl.semaphore_signal(barrier, inc=1, device_id=(lax.rem(a + off, na), z, t),
                            device_id_type=mesh_ids)
    pl.semaphore_signal(barrier, inc=1, device_id=partner, device_id_type=mesh_ids)
    for off in range(1, n_hi):
        pl.semaphore_signal(barrier, inc=1, device_id=(a, z, lax.rem(hi + off, n_hi) * 2 + core),
                            device_id_type=mesh_ids)
    pl.semaphore_wait(barrier, na - 1 + n_hi)

    own_stats = pltpu.make_async_copy(stats_ref.at[:, :, a], got_stats.at[na - 1], own_stat_sem)
    own_stats.start()
    stat_copies = []
    for off in range(1, na):
        dest = lax.rem(a + off, na)
        copy = pltpu.make_async_remote_copy(
            src_ref=stats_ref.at[:, :, dest], dst_ref=got_stats.at[off - 1],
            send_sem=stat_sems.at[0, off - 1], recv_sem=stat_sems.at[1, off - 1],
            device_id=(dest, z, t), device_id_type=mesh_ids)
        copy.start()
        stat_copies.append(copy)
    part_copies = []
    for h in range(heads):
        per_head = []
        for off in range(1, na):
            dest = lax.rem(a + off, na)
            copy = pltpu.make_async_remote_copy(
                src_ref=parts_ref.at[h, dest], dst_ref=got_parts.at[off - 1, h],
                send_sem=part_sems.at[0, h, off - 1], recv_sem=part_sems.at[1, h, off - 1],
                device_id=(dest, z, t), device_id_type=mesh_ids)
            copy.start()
            per_head.append(copy)
        part_copies.append(per_head)
    for copy in stat_copies:
        copy.wait()
    own_stats.wait()

    peaks = [got_stats[na - 1, 0]] + [got_stats[off - 1, 0] for off in range(1, na)]
    sums = [got_stats[na - 1, 1]] + [got_stats[off - 1, 1] for off in range(1, na)]
    top = peaks[0]
    for peak in peaks[1:]:
        top = jnp.maximum(top, peak)
    factors = [jnp.exp(peak - top) for peak in peaks]
    totals = factors[0] * sums[0]
    for factor, part_sum in zip(factors[1:], sums[1:]):
        totals = totals + factor * part_sum
    for h in range(heads):
        for copy in part_copies[h]:
            copy.wait()
        numerator = parts_ref[h, a].astype(jnp.float32) * factors[0][h][:, None]
        for off in range(1, na):
            numerator = numerator + (
                got_parts[off - 1, h].astype(jnp.float32) * factors[off][h][:, None]
            )
        att_buf[:, pl.ds(h * HD, HD)] = (numerator / totals[h][:, None]).astype(jnp.bfloat16)

    for j in range(n_hi):
        their = pl.multiple_of((j * 2 + 1 - core) * rows, rows)
        mine = pl.multiple_of((j * 2 + core) * rows, rows)
        pick[0, pl.ds(j * rows, rows), :] = att_buf[pl.ds(their, rows), :]
        pick[1, pl.ds(j * rows, rows), :] = att_buf[pl.ds(mine, rows), :]
    cols = send1.shape[1]
    chunk = cols // STAGE_CHUNKS
    firsts = []
    for k in range(STAGE_CHUNKS):
        window = pl.ds(k * chunk, chunk)
        send1[:, window] = jnp.dot(
            pick[0], w_ref[:, window], preferred_element_type=jnp.float32).astype(jnp.bfloat16)
        copy = pltpu.make_async_remote_copy(
            src_ref=send1.at[:, window], dst_ref=recv1.at[:, window], send_sem=sems1.at[0, k],
            recv_sem=sems1.at[1, k], device_id=partner, device_id_type=mesh_ids)
        copy.start()
        firsts.append(copy)
    total[...] = jnp.dot(pick[1], w_ref[...], preferred_element_type=jnp.float32).astype(
        jnp.bfloat16).astype(jnp.float32)
    second = []
    for k in range(STAGE_CHUNKS):
        window = pl.ds(k * chunk, chunk)
        firsts[k].wait()
        for j in range(n_hi):
            block = pl.ds(j * rows, rows)
            send2[j, :, window] = (
                total[block, window] + recv1[block, window].astype(jnp.float32)
            ).astype(jnp.bfloat16)
        for off in range(1, n_hi):
            dest = lax.rem(hi + off, n_hi)
            copy = pltpu.make_async_remote_copy(
                src_ref=send2.at[dest, :, window], dst_ref=recv2.at[off - 1, :, window],
                send_sem=send_sems2.at[0, k, off - 1], recv_sem=send_sems2.at[1, k, off - 1],
                device_id=(a, z, dest * 2 + core), device_id_type=mesh_ids)
            copy.start()
            second.append(copy)
    own_rows = pl.ds(pl.multiple_of(hi * rows, rows), rows)
    own = total[own_rows, :] + recv1[own_rows, :].astype(jnp.float32)
    for copy in second:
        copy.wait()
    for off in range(1, n_hi):
        own = own + recv2[off - 1].astype(jnp.float32)
    out_ref[...] = own.astype(out_ref.dtype)


def project(parts, stats, out_weight, tp_count):
    heads, na, block_rows, _ = parts.shape
    n_hi = tp_count // 2
    rows = block_rows // tp_count
    cols = out_weight.shape[1]
    vmem = pl.BlockSpec(memory_space=pltpu.VMEM)
    return pl.pallas_call(
        functools.partial(project_kernel, na, n_hi),
        out_shape=jax.ShapeDtypeStruct((rows, cols), jnp.bfloat16),
        in_specs=[vmem, vmem, vmem],
        out_specs=vmem,
        scratch_shapes=[
            pltpu.VMEM((na - 1, heads, block_rows, HD), parts.dtype),
            pltpu.VMEM((na, 2, heads, block_rows), stats.dtype),
            pltpu.VMEM((block_rows, heads * HD), jnp.bfloat16),
            pltpu.VMEM((2, n_hi * rows, heads * HD), jnp.bfloat16),
            pltpu.VMEM((n_hi * rows, cols), jnp.bfloat16),
            pltpu.VMEM((n_hi * rows, cols), jnp.bfloat16),
            pltpu.VMEM((n_hi * rows, cols), jnp.float32),
            pltpu.VMEM((n_hi, rows, cols), jnp.bfloat16),
            pltpu.VMEM((n_hi - 1, rows, cols), jnp.bfloat16),
            pltpu.SemaphoreType.DMA((2, heads, na - 1)),
            pltpu.SemaphoreType.DMA((2, na - 1)),
            pltpu.SemaphoreType.DMA((2, STAGE_CHUNKS)),
            pltpu.SemaphoreType.DMA((2, STAGE_CHUNKS, n_hi - 1)),
            pltpu.SemaphoreType.DMA((1,)),
            pltpu.SemaphoreType.DMA(()),
        ],
        compiler_params=pltpu.CompilerParams(collective_id=1, has_side_effects=True),
    )(parts, stats, out_weight)


def local(query_vectors, key_vectors, value_vectors, out_weight):
    score_scale = 1.0 / math.sqrt(HD)
    tp_count = lax.axis_size("tp")
    ca_count = lax.axis_size("ca")
    token_rows = query_vectors.shape[0]
    own_heads = query_vectors.shape[1] // HD // tp_count
    own_cols = own_heads * HD

    block_rows = token_rows * tp_count
    query_heads, key_heads, value_heads = exchange(
        query_vectors, key_vectors, value_vectors, ca_count, lax.axis_size("cz"), tp_count)
    row_peak, row_total, weighted = attend_local(
        query_heads.reshape(own_heads, -1, HD), key_heads.reshape(own_heads, -1, HD),
        value_heads.reshape(own_heads, -1, HD), score_scale)
    stats = jnp.stack([row_peak, row_total], axis=0).reshape(2, own_heads, ca_count, block_rows)
    parts = weighted.astype(jnp.bfloat16).reshape(own_heads, ca_count, block_rows, HD)
    return project(parts, stats, out_weight, tp_count)


def solution(mesh):
    ctx_count, tp_count = mesh.devices.shape
    split_mesh = Mesh(
        mesh.devices.reshape(ctx_count // KEY_SPLIT, KEY_SPLIT, tp_count), ("ca", "cz", "tp")
    )
    rows = P(("ca", "cz", "tp"), None)
    return jax.shard_map(
        local,
        mesh=split_mesh,
        in_specs=(rows, rows, rows, P("tp", None)),
        out_specs=rows,
        check_vma=False,
    )
```

```python
import functools
import math

import jax
import jax.numpy as jnp
from jax import lax
from jax.sharding import Mesh
from jax.sharding import PartitionSpec as P
from jax.experimental import pallas as pl
from jax.experimental.pallas import tpu as pltpu

HD = 128
KEY_SPLIT = 8
STAGE_CHUNKS = 4


def attend_local(query_heads, key_heads, value_heads, score_scale):
    scores = (
        jnp.einsum("hid,hjd->hij", query_heads, key_heads, preferred_element_type=jnp.float32)
        * score_scale
    )
    row_peak = jnp.max(scores, axis=-1)
    weights_low = jnp.exp(scores - row_peak[..., None]).astype(jnp.bfloat16)
    row_total = jnp.sum(weights_low.astype(jnp.float32), axis=-1)
    weighted = jnp.einsum(
        "hij,hjd->hid", weights_low, value_heads, preferred_element_type=jnp.float32
    )
    return row_peak, row_total, weighted


def gather_by_exchange(block, axis_name):
    count = lax.axis_size(axis_name)
    spread = jnp.broadcast_to(block[None], (count,) + block.shape)
    return lax.all_to_all(spread, axis_name, 0, 0, tiled=True)


def exchange_kernel(na, nz, nt, q_ref, k_ref, v_ref, q_out, k_out, v_out, spread_sems,
                    own_sems, q_sems, r_sems, l_sems):
    mesh_ids = pl.DeviceIdType.MESH
    a = lax.axis_index("ca")
    z = lax.axis_index("cz")
    t = lax.axis_index("tp")
    right = lax.rem(z + 1, nz)
    left = lax.rem(z + nz - 1, nz)
    rows = q_ref.shape[0]
    heads = q_out.shape[0]

    barrier = pltpu.get_barrier_semaphore()
    for off in range(1, nt):
        pl.semaphore_signal(barrier, inc=1, device_id=(a, z, lax.rem(t + off, nt)),
                            device_id_type=mesh_ids)
    for off in range(1, na):
        pl.semaphore_signal(barrier, inc=1, device_id=(lax.rem(a + off, na), z, t),
                            device_id_type=mesh_ids)
    for side in (left, right):
        pl.semaphore_signal(barrier, inc=1, device_id=(a, side, t), device_id_type=mesh_ids)
    pl.semaphore_wait(barrier, nt - 1 + na - 1 + 2)

    mine = pl.ds(pl.multiple_of(t * rows, rows), rows)
    sources = (q_ref, k_ref, v_ref)

    def target(i, h):
        if i == 0:
            return q_out.at[h, a, mine]
        return (k_out, v_out)[i - 1].at[h, z, mine]

    def columns(dest, h):
        return pl.ds(pl.multiple_of((dest * heads + h) * HD, HD), HD)

    own = []
    for i in range(3):
        for h in range(heads):
            copy = pltpu.make_async_copy(
                sources[i].at[:, columns(t, h)], target(i, h), own_sems.at[i, h])
            copy.start()
            own.append(copy)
    spread = [[], [], []]
    for off in range(1, nt):
        dest = lax.rem(t + off, nt)
        for i in range(3):
            for h in range(heads):
                spread[i].append(pltpu.make_async_remote_copy(
                    src_ref=sources[i].at[:, columns(dest, h)], dst_ref=target(i, h),
                    send_sem=spread_sems.at[0, i, h, off - 1],
                    recv_sem=spread_sems.at[1, i, h, off - 1],
                    device_id=(a, z, dest), device_id_type=mesh_ids))
    for group in (spread[1], spread[2], spread[0]):
        for copy in group:
            copy.start()
    q_copies = []

    def push_queries():
        for copy in spread[0] + own[:heads]:
            copy.wait()
        for off in range(1, na):
            copy = pltpu.make_async_remote_copy(
                src_ref=q_out.at[:, a], dst_ref=q_out.at[:, a], send_sem=q_sems.at[0, off - 1],
                recv_sem=q_sems.at[1, off - 1], device_id=(lax.rem(a + off, na), z, t),
                device_id_type=mesh_ids)
            copy.start()
            q_copies.append(copy)

    n_steps = nz // 2
    chains = ((right, r_sems, -1, {}), (left, l_sems, 1, {}))

    def parts_of(chain, step):
        if nz % 2 == 0 and step == n_steps - 1:
            return (chain,)
        return (0, 1)

    for copy in spread[1] + own[heads:2 * heads]:
        copy.wait()
    sent = []
    for step in range(n_steps):
        for part in range(2):
            for chain, (side, sems, sign, copies) in enumerate(chains):
                if part not in parts_of(chain, step):
                    continue
                slot = lax.rem(z + sign * step + nz, nz)
                if step > 0:
                    copies.pop((step - 1, part)).wait_recv()
                elif part == 1 and chain == 0:
                    push_queries()
                    for copy in spread[2] + own[2 * heads:]:
                        copy.wait()
                buf = (k_out, v_out)[part]
                copy = pltpu.make_async_remote_copy(
                    src_ref=buf.at[:, slot], dst_ref=buf.at[:, slot],
                    send_sem=sems.at[0, step * 2 + part], recv_sem=sems.at[1, step * 2 + part],
                    device_id=(a, side, t), device_id_type=mesh_ids)
                copy.start()
                copies[(step, part)] = copy
                sent.append(copy)
    for side, sems, sign, copies in chains:
        for copy in copies.values():
            copy.wait_recv()
    for copy in sent:
        copy.wait_send()
    for copy in q_copies:
        copy.wait()


def exchange(query_vectors, key_vectors, value_vectors, na, nz, nt):
    rows, width = query_vectors.shape
    heads = width // nt // HD
    n_right = nz // 2
    n_left = (nz - 1) // 2
    dtype = query_vectors.dtype
    return pl.pallas_call(
        functools.partial(exchange_kernel, na, nz, nt),
        out_shape=(
            jax.ShapeDtypeStruct((heads, na, nt * rows, HD), dtype),
            jax.ShapeDtypeStruct((heads, nz, nt * rows, HD), dtype),
            jax.ShapeDtypeStruct((heads, nz, nt * rows, HD), dtype),
        ),
        in_specs=[pl.BlockSpec(memory_space=pl.ANY)] * 3,
        out_specs=tuple(pl.BlockSpec(memory_space=pl.ANY) for _ in range(3)),
        scratch_shapes=[
            pltpu.SemaphoreType.DMA((2, 3, heads, nt - 1)),
            pltpu.SemaphoreType.DMA((3, heads)),
            pltpu.SemaphoreType.DMA((2, na - 1)),
            pltpu.SemaphoreType.DMA((2, 2 * (nz // 2))),
            pltpu.SemaphoreType.DMA((2, 2 * (nz // 2))),
        ],
        compiler_params=pltpu.CompilerParams(collective_id=0, has_side_effects=True),
    )(query_vectors, key_vectors, value_vectors)


def project_kernel(na, n_hi, parts_ref, stats_ref, w_ref, out_ref, got_parts, got_stats, att_buf,
                   pick, send1, recv1, total, send2, recv2, part_sems, stat_sems, sems1, send_sems2,
                   recv_sems2, own_stat_sem):
    mesh_ids = pl.DeviceIdType.MESH
    a = lax.axis_index("ca")
    z = lax.axis_index("cz")
    t = lax.axis_index("tp")
    core = lax.rem(t, 2)
    hi = t // 2
    partner = (a, z, hi * 2 + 1 - core)
    rows = send2.shape[1]
    heads = parts_ref.shape[0]

    barrier = pltpu.get_barrier_semaphore()
    for off in range(1, na):
        pl.semaphore_signal(barrier, inc=1, device_id=(lax.rem(a + off, na), z, t),
                            device_id_type=mesh_ids)
    pl.semaphore_signal(barrier, inc=1, device_id=partner, device_id_type=mesh_ids)
    for off in range(1, n_hi):
        pl.semaphore_signal(barrier, inc=1, device_id=(a, z, lax.rem(hi + off, n_hi) * 2 + core),
                            device_id_type=mesh_ids)
    pl.semaphore_wait(barrier, na - 1 + n_hi)

    own_stats = pltpu.make_async_copy(stats_ref.at[:, :, a], got_stats.at[na - 1], own_stat_sem)
    own_stats.start()
    stat_copies = []
    for off in range(1, na):
        dest = lax.rem(a + off, na)
        copy = pltpu.make_async_remote_copy(
            src_ref=stats_ref.at[:, :, dest], dst_ref=got_stats.at[off - 1],
            send_sem=stat_sems.at[0, off - 1], recv_sem=stat_sems.at[1, off - 1],
            device_id=(dest, z, t), device_id_type=mesh_ids)
        copy.start()
        stat_copies.append(copy)
    part_copies = []
    for h in range(heads):
        per_head = []
        for off in range(1, na):
            dest = lax.rem(a + off, na)
            copy = pltpu.make_async_remote_copy(
                src_ref=parts_ref.at[h, dest], dst_ref=got_parts.at[off - 1, h],
                send_sem=part_sems.at[0, h, off - 1], recv_sem=part_sems.at[1, h, off - 1],
                device_id=(dest, z, t), device_id_type=mesh_ids)
            copy.start()
            per_head.append(copy)
        part_copies.append(per_head)
    for copy in stat_copies:
        copy.wait()
    own_stats.wait()

    peaks = [got_stats[na - 1, 0]] + [got_stats[off - 1, 0] for off in range(1, na)]
    sums = [got_stats[na - 1, 1]] + [got_stats[off - 1, 1] for off in range(1, na)]
    top = peaks[0]
    for peak in peaks[1:]:
        top = jnp.maximum(top, peak)
    factors = [jnp.exp(peak - top) for peak in peaks]
    totals = factors[0] * sums[0]
    for factor, part_sum in zip(factors[1:], sums[1:]):
        totals = totals + factor * part_sum
    for h in range(heads):
        for copy in part_copies[h]:
            copy.wait()
        numerator = parts_ref[h, a].astype(jnp.float32) * factors[0][h][:, None]
        for off in range(1, na):
            numerator = numerator + (
                got_parts[off - 1, h].astype(jnp.float32) * factors[off][h][:, None]
            )
        att_buf[:, pl.ds(h * HD, HD)] = (numerator / totals[h][:, None]).astype(jnp.bfloat16)

    for j in range(n_hi):
        their = pl.multiple_of((j * 2 + 1 - core) * rows, rows)
        mine = pl.multiple_of((j * 2 + core) * rows, rows)
        pick[0, pl.ds(j * rows, rows), :] = att_buf[pl.ds(their, rows), :]
        pick[1, pl.ds(j * rows, rows), :] = att_buf[pl.ds(mine, rows), :]
    cols = send1.shape[1]
    chunk = cols // STAGE_CHUNKS
    firsts = []
    for k in range(STAGE_CHUNKS):
        window = pl.ds(k * chunk, chunk)
        send1[:, window] = jnp.dot(
            pick[0], w_ref[:, window], preferred_element_type=jnp.float32).astype(jnp.bfloat16)
        copy = pltpu.make_async_remote_copy(
            src_ref=send1.at[:, window], dst_ref=recv1.at[:, window], send_sem=sems1.at[0, k],
            recv_sem=sems1.at[1, k], device_id=partner, device_id_type=mesh_ids)
        copy.start()
        firsts.append(copy)
    total[...] = jnp.dot(pick[1], w_ref[...], preferred_element_type=jnp.float32).astype(
        jnp.bfloat16).astype(jnp.float32)
    second = []
    for k in range(STAGE_CHUNKS):
        window = pl.ds(k * chunk, chunk)
        firsts[k].wait()
        for j in range(n_hi):
            block = pl.ds(j * rows, rows)
            send2[j, :, window] = (
                total[block, window] + recv1[block, window].astype(jnp.float32)
            ).astype(jnp.bfloat16)
        for off in range(1, n_hi):
            dest = lax.rem(hi + off, n_hi)
            copy = pltpu.make_async_remote_copy(
                src_ref=send2.at[dest, :, window], dst_ref=recv2.at[off - 1, :, window],
                send_sem=send_sems2.at[0, k, off - 1], recv_sem=send_sems2.at[1, k, off - 1],
                device_id=(a, z, dest * 2 + core), device_id_type=mesh_ids)
            copy.start()
            second.append(copy)
    own_rows = pl.ds(pl.multiple_of(hi * rows, rows), rows)
    own = total[own_rows, :] + recv1[own_rows, :].astype(jnp.float32)
    for copy in second:
        copy.wait()
    for off in range(1, n_hi):
        own = own + recv2[off - 1].astype(jnp.float32)
    out_ref[...] = own.astype(out_ref.dtype)


def project(parts, stats, out_weight, tp_count):
    heads, na, block_rows, _ = parts.shape
    n_hi = tp_count // 2
    rows = block_rows // tp_count
    cols = out_weight.shape[1]
    vmem = pl.BlockSpec(memory_space=pltpu.VMEM)
    return pl.pallas_call(
        functools.partial(project_kernel, na, n_hi),
        out_shape=jax.ShapeDtypeStruct((rows, cols), jnp.bfloat16),
        in_specs=[vmem, vmem, vmem],
        out_specs=vmem,
        scratch_shapes=[
            pltpu.VMEM((na - 1, heads, block_rows, HD), parts.dtype),
            pltpu.VMEM((na, 2, heads, block_rows), stats.dtype),
            pltpu.VMEM((block_rows, heads * HD), jnp.bfloat16),
            pltpu.VMEM((2, n_hi * rows, heads * HD), jnp.bfloat16),
            pltpu.VMEM((n_hi * rows, cols), jnp.bfloat16),
            pltpu.VMEM((n_hi * rows, cols), jnp.bfloat16),
            pltpu.VMEM((n_hi * rows, cols), jnp.float32),
            pltpu.VMEM((n_hi, rows, cols), jnp.bfloat16),
            pltpu.VMEM((n_hi - 1, rows, cols), jnp.bfloat16),
            pltpu.SemaphoreType.DMA((2, heads, na - 1)),
            pltpu.SemaphoreType.DMA((2, na - 1)),
            pltpu.SemaphoreType.DMA((2, STAGE_CHUNKS)),
            pltpu.SemaphoreType.DMA((2, STAGE_CHUNKS, n_hi - 1)),
            pltpu.SemaphoreType.DMA((1,)),
            pltpu.SemaphoreType.DMA(()),
        ],
        compiler_params=pltpu.CompilerParams(collective_id=1, has_side_effects=True),
    )(parts, stats, out_weight)


def local(query_vectors, key_vectors, value_vectors, out_weight):
    score_scale = 1.0 / math.sqrt(HD)
    tp_count = lax.axis_size("tp")
    ca_count = lax.axis_size("ca")
    token_rows = query_vectors.shape[0]
    own_heads = query_vectors.shape[1] // HD // tp_count
    own_cols = own_heads * HD

    block_rows = token_rows * tp_count
    query_heads, key_heads, value_heads = exchange(
        query_vectors, key_vectors, value_vectors, ca_count, lax.axis_size("cz"), tp_count)
    row_peak, row_total, weighted = attend_local(
        query_heads.reshape(own_heads, -1, HD), key_heads.reshape(own_heads, -1, HD),
        value_heads.reshape(own_heads, -1, HD), score_scale)
    stats = jnp.stack([row_peak, row_total], axis=0).reshape(2, own_heads, ca_count, block_rows)
    parts = weighted.astype(jnp.bfloat16).reshape(own_heads, ca_count, block_rows, HD)
    return project(parts, stats, out_weight, tp_count)


def solution(mesh):
    ctx_count, tp_count = mesh.devices.shape
    split_mesh = Mesh(
        mesh.devices.reshape(ctx_count // KEY_SPLIT, KEY_SPLIT, tp_count), ("ca", "cz", "tp")
    )
    rows = P(("ca", "cz", "tp"), None)
    return jax.shard_map(
        local,
        mesh=split_mesh,
        in_specs=(rows, rows, rows, P("tp", None)),
        out_specs=rows,
        check_vma=False,
    )
```

```python
import functools
import math

import jax
import jax.numpy as jnp
from jax import lax
from jax.sharding import Mesh
from jax.sharding import PartitionSpec as P
from jax.experimental import pallas as pl
from jax.experimental.pallas import tpu as pltpu

HD = 128
KEY_SPLIT = 8
STAGE_CHUNKS = 4


def attend_local(query_heads, key_heads, value_heads, score_scale):
    scores = (
        jnp.einsum("hid,hjd->hij", query_heads, key_heads, preferred_element_type=jnp.float32)
        * score_scale
    )
    row_peak = jnp.max(scores, axis=-1)
    weights_low = jnp.exp(scores - row_peak[..., None]).astype(jnp.bfloat16)
    row_total = jnp.sum(weights_low.astype(jnp.float32), axis=-1)
    weighted = jnp.einsum(
        "hij,hjd->hid", weights_low, value_heads, preferred_element_type=jnp.float32
    )
    return row_peak, row_total, weighted


def gather_by_exchange(block, axis_name):
    count = lax.axis_size(axis_name)
    spread = jnp.broadcast_to(block[None], (count,) + block.shape)
    return lax.all_to_all(spread, axis_name, 0, 0, tiled=True)


def exchange_kernel(na, nz, nt, q_ref, k_ref, v_ref, q_out, k_out, v_out, spread_sems,
                    own_sems, q_sems, r_sems, l_sems):
    mesh_ids = pl.DeviceIdType.MESH
    a = lax.axis_index("ca")
    z = lax.axis_index("cz")
    t = lax.axis_index("tp")
    right = lax.rem(z + 1, nz)
    left = lax.rem(z + nz - 1, nz)
    rows = q_ref.shape[0]
    heads = q_out.shape[0]

    barrier = pltpu.get_barrier_semaphore()
    for off in range(1, nt):
        pl.semaphore_signal(barrier, inc=1, device_id=(a, z, lax.rem(t + off, nt)),
                            device_id_type=mesh_ids)
    for off in range(1, na):
        pl.semaphore_signal(barrier, inc=1, device_id=(lax.rem(a + off, na), z, t),
                            device_id_type=mesh_ids)
    for side in (left, right):
        pl.semaphore_signal(barrier, inc=1, device_id=(a, side, t), device_id_type=mesh_ids)
    pl.semaphore_wait(barrier, nt - 1 + na - 1 + 2)

    mine = pl.ds(pl.multiple_of(t * rows, rows), rows)
    sources = (q_ref, k_ref, v_ref)

    def target(i, h):
        if i == 0:
            return q_out.at[h, a, mine]
        return (k_out, v_out)[i - 1].at[h, z, mine]

    def columns(dest, h):
        return pl.ds(pl.multiple_of((dest * heads + h) * HD, HD), HD)

    own = []
    for i in range(3):
        for h in range(heads):
            copy = pltpu.make_async_copy(
                sources[i].at[:, columns(t, h)], target(i, h), own_sems.at[i, h])
            copy.start()
            own.append(copy)
    spread = [[], [], []]
    for off in range(1, nt):
        dest = lax.rem(t + off, nt)
        for i in range(3):
            for h in range(heads):
                spread[i].append(pltpu.make_async_remote_copy(
                    src_ref=sources[i].at[:, columns(dest, h)], dst_ref=target(i, h),
                    send_sem=spread_sems.at[0, i, h, off - 1],
                    recv_sem=spread_sems.at[1, i, h, off - 1],
                    device_id=(a, z, dest), device_id_type=mesh_ids))
    for group in spread:
        for copy in group:
            copy.start()
    q_copies = []

    def push_queries():
        for copy in spread[0] + own[:heads]:
            copy.wait()
        for off in range(1, na):
            copy = pltpu.make_async_remote_copy(
                src_ref=q_out.at[:, a], dst_ref=q_out.at[:, a], send_sem=q_sems.at[0, off - 1],
                recv_sem=q_sems.at[1, off - 1], device_id=(lax.rem(a + off, na), z, t),
                device_id_type=mesh_ids)
            copy.start()
            q_copies.append(copy)

    n_steps = nz // 2
    chains = ((right, r_sems, -1, {}), (left, l_sems, 1, {}))

    def parts_of(chain, step):
        if nz % 2 == 0 and step == n_steps - 1:
            return (chain,)
        return (0, 1)

    for copy in spread[1] + own[heads:2 * heads]:
        copy.wait()
    sent = []
    for step in range(n_steps):
        for part in range(2):
            for chain, (side, sems, sign, copies) in enumerate(chains):
                if part not in parts_of(chain, step):
                    continue
                slot = lax.rem(z + sign * step + nz, nz)
                if step > 0:
                    copies.pop((step - 1, part)).wait_recv()
                elif part == 1 and chain == 0:
                    push_queries()
                    for copy in spread[2] + own[2 * heads:]:
                        copy.wait()
                buf = (k_out, v_out)[part]
                copy = pltpu.make_async_remote_copy(
                    src_ref=buf.at[:, slot], dst_ref=buf.at[:, slot],
                    send_sem=sems.at[0, step * 2 + part], recv_sem=sems.at[1, step * 2 + part],
                    device_id=(a, side, t), device_id_type=mesh_ids)
                copy.start()
                copies[(step, part)] = copy
                sent.append(copy)
    for side, sems, sign, copies in chains:
        for copy in copies.values():
            copy.wait_recv()
    for copy in sent:
        copy.wait_send()
    for copy in q_copies:
        copy.wait()


def exchange(query_vectors, key_vectors, value_vectors, na, nz, nt):
    rows, width = query_vectors.shape
    heads = width // nt // HD
    n_right = nz // 2
    n_left = (nz - 1) // 2
    dtype = query_vectors.dtype
    return pl.pallas_call(
        functools.partial(exchange_kernel, na, nz, nt),
        out_shape=(
            jax.ShapeDtypeStruct((heads, na, nt * rows, HD), dtype),
            jax.ShapeDtypeStruct((heads, nz, nt * rows, HD), dtype),
            jax.ShapeDtypeStruct((heads, nz, nt * rows, HD), dtype),
        ),
        in_specs=[pl.BlockSpec(memory_space=pl.ANY)] * 3,
        out_specs=tuple(pl.BlockSpec(memory_space=pl.ANY) for _ in range(3)),
        scratch_shapes=[
            pltpu.SemaphoreType.DMA((2, 3, heads, nt - 1)),
            pltpu.SemaphoreType.DMA((3, heads)),
            pltpu.SemaphoreType.DMA((2, na - 1)),
            pltpu.SemaphoreType.DMA((2, 2 * (nz // 2))),
            pltpu.SemaphoreType.DMA((2, 2 * (nz // 2))),
        ],
        compiler_params=pltpu.CompilerParams(collective_id=0, has_side_effects=True),
    )(query_vectors, key_vectors, value_vectors)


def project_kernel(na, n_hi, parts_ref, stats_ref, w_ref, out_ref, got_parts, got_stats, att_buf,
                   pick, send1, recv1, total, send2, recv2, part_sems, stat_sems, sems1, send_sems2,
                   recv_sems2, own_stat_sem):
    mesh_ids = pl.DeviceIdType.MESH
    a = lax.axis_index("ca")
    z = lax.axis_index("cz")
    t = lax.axis_index("tp")
    core = lax.rem(t, 2)
    hi = t // 2
    partner = (a, z, hi * 2 + 1 - core)
    rows = send2.shape[1]
    heads = parts_ref.shape[0]

    barrier = pltpu.get_barrier_semaphore()
    for off in range(1, na):
        pl.semaphore_signal(barrier, inc=1, device_id=(lax.rem(a + off, na), z, t),
                            device_id_type=mesh_ids)
    pl.semaphore_signal(barrier, inc=1, device_id=partner, device_id_type=mesh_ids)
    for off in range(1, n_hi):
        pl.semaphore_signal(barrier, inc=1, device_id=(a, z, lax.rem(hi + off, n_hi) * 2 + core),
                            device_id_type=mesh_ids)
    pl.semaphore_wait(barrier, na - 1 + n_hi)

    own_stats = pltpu.make_async_copy(stats_ref.at[:, :, a], got_stats.at[na - 1], own_stat_sem)
    own_stats.start()
    stat_copies = []
    for off in range(1, na):
        dest = lax.rem(a + off, na)
        copy = pltpu.make_async_remote_copy(
            src_ref=stats_ref.at[:, :, dest], dst_ref=got_stats.at[off - 1],
            send_sem=stat_sems.at[0, off - 1], recv_sem=stat_sems.at[1, off - 1],
            device_id=(dest, z, t), device_id_type=mesh_ids)
        copy.start()
        stat_copies.append(copy)
    part_copies = []
    for h in range(heads):
        per_head = []
        for off in range(1, na):
            dest = lax.rem(a + off, na)
            copy = pltpu.make_async_remote_copy(
                src_ref=parts_ref.at[h, dest], dst_ref=got_parts.at[off - 1, h],
                send_sem=part_sems.at[0, h, off - 1], recv_sem=part_sems.at[1, h, off - 1],
                device_id=(dest, z, t), device_id_type=mesh_ids)
            copy.start()
            per_head.append(copy)
        part_copies.append(per_head)
    for copy in stat_copies:
        copy.wait()
    own_stats.wait()

    peaks = [got_stats[na - 1, 0]] + [got_stats[off - 1, 0] for off in range(1, na)]
    sums = [got_stats[na - 1, 1]] + [got_stats[off - 1, 1] for off in range(1, na)]
    top = peaks[0]
    for peak in peaks[1:]:
        top = jnp.maximum(top, peak)
    factors = [jnp.exp(peak - top) for peak in peaks]
    totals = factors[0] * sums[0]
    for factor, part_sum in zip(factors[1:], sums[1:]):
        totals = totals + factor * part_sum
    for h in range(heads):
        for copy in part_copies[h]:
            copy.wait()
        numerator = parts_ref[h, a].astype(jnp.float32) * factors[0][h][:, None]
        for off in range(1, na):
            numerator = numerator + (
                got_parts[off - 1, h].astype(jnp.float32) * factors[off][h][:, None]
            )
        att_buf[:, pl.ds(h * HD, HD)] = (numerator / totals[h][:, None]).astype(jnp.bfloat16)

    for j in range(n_hi):
        their = pl.multiple_of((j * 2 + 1 - core) * rows, rows)
        mine = pl.multiple_of((j * 2 + core) * rows, rows)
        pick[0, pl.ds(j * rows, rows), :] = att_buf[pl.ds(their, rows), :]
        pick[1, pl.ds(j * rows, rows), :] = att_buf[pl.ds(mine, rows), :]
    cols = send1.shape[1]
    chunk = cols // STAGE_CHUNKS
    firsts = []
    for k in range(STAGE_CHUNKS):
        window = pl.ds(k * chunk, chunk)
        send1[:, window] = jnp.dot(
            pick[0], w_ref[:, window], preferred_element_type=jnp.float32).astype(jnp.bfloat16)
        copy = pltpu.make_async_remote_copy(
            src_ref=send1.at[:, window], dst_ref=recv1.at[:, window], send_sem=sems1.at[0, k],
            recv_sem=sems1.at[1, k], device_id=partner, device_id_type=mesh_ids)
        copy.start()
        firsts.append(copy)
    total[...] = jnp.dot(pick[1], w_ref[...], preferred_element_type=jnp.float32).astype(
        jnp.bfloat16).astype(jnp.float32)
    second = []
    for k in range(STAGE_CHUNKS):
        window = pl.ds(k * chunk, chunk)
        firsts[k].wait()
        for j in range(n_hi):
            block = pl.ds(j * rows, rows)
            send2[j, :, window] = (
                total[block, window] + recv1[block, window].astype(jnp.float32)
            ).astype(jnp.bfloat16)
        for off in sorted(range(1, n_hi), key=lambda o: -min(o, n_hi - o)):
            dest = lax.rem(hi + off, n_hi)
            copy = pltpu.make_async_remote_copy(
                src_ref=send2.at[dest, :, window], dst_ref=recv2.at[off - 1, :, window],
                send_sem=send_sems2.at[0, k, off - 1], recv_sem=send_sems2.at[1, k, off - 1],
                device_id=(a, z, dest * 2 + core), device_id_type=mesh_ids)
            copy.start()
            second.append(copy)
    own_rows = pl.ds(pl.multiple_of(hi * rows, rows), rows)
    own = total[own_rows, :] + recv1[own_rows, :].astype(jnp.float32)
    for copy in second:
        copy.wait()
    for off in range(1, n_hi):
        own = own + recv2[off - 1].astype(jnp.float32)
    out_ref[...] = own.astype(out_ref.dtype)


def project(parts, stats, out_weight, tp_count):
    heads, na, block_rows, _ = parts.shape
    n_hi = tp_count // 2
    rows = block_rows // tp_count
    cols = out_weight.shape[1]
    vmem = pl.BlockSpec(memory_space=pltpu.VMEM)
    return pl.pallas_call(
        functools.partial(project_kernel, na, n_hi),
        out_shape=jax.ShapeDtypeStruct((rows, cols), jnp.bfloat16),
        in_specs=[vmem, vmem, vmem],
        out_specs=vmem,
        scratch_shapes=[
            pltpu.VMEM((na - 1, heads, block_rows, HD), parts.dtype),
            pltpu.VMEM((na, 2, heads, block_rows), stats.dtype),
            pltpu.VMEM((block_rows, heads * HD), jnp.bfloat16),
            pltpu.VMEM((2, n_hi * rows, heads * HD), jnp.bfloat16),
            pltpu.VMEM((n_hi * rows, cols), jnp.bfloat16),
            pltpu.VMEM((n_hi * rows, cols), jnp.bfloat16),
            pltpu.VMEM((n_hi * rows, cols), jnp.float32),
            pltpu.VMEM((n_hi, rows, cols), jnp.bfloat16),
            pltpu.VMEM((n_hi - 1, rows, cols), jnp.bfloat16),
            pltpu.SemaphoreType.DMA((2, heads, na - 1)),
            pltpu.SemaphoreType.DMA((2, na - 1)),
            pltpu.SemaphoreType.DMA((2, STAGE_CHUNKS)),
            pltpu.SemaphoreType.DMA((2, STAGE_CHUNKS, n_hi - 1)),
            pltpu.SemaphoreType.DMA((1,)),
            pltpu.SemaphoreType.DMA(()),
        ],
        compiler_params=pltpu.CompilerParams(collective_id=1, has_side_effects=True),
    )(parts, stats, out_weight)


def local(query_vectors, key_vectors, value_vectors, out_weight):
    score_scale = 1.0 / math.sqrt(HD)
    tp_count = lax.axis_size("tp")
    ca_count = lax.axis_size("ca")
    token_rows = query_vectors.shape[0]
    own_heads = query_vectors.shape[1] // HD // tp_count
    own_cols = own_heads * HD

    block_rows = token_rows * tp_count
    query_heads, key_heads, value_heads = exchange(
        query_vectors, key_vectors, value_vectors, ca_count, lax.axis_size("cz"), tp_count)
    row_peak, row_total, weighted = attend_local(
        query_heads.reshape(own_heads, -1, HD), key_heads.reshape(own_heads, -1, HD),
        value_heads.reshape(own_heads, -1, HD), score_scale)
    stats = jnp.stack([row_peak, row_total], axis=0).reshape(2, own_heads, ca_count, block_rows)
    parts = weighted.astype(jnp.bfloat16).reshape(own_heads, ca_count, block_rows, HD)
    return project(parts, stats, out_weight, tp_count)


def solution(mesh):
    ctx_count, tp_count = mesh.devices.shape
    split_mesh = Mesh(
        mesh.devices.reshape(ctx_count // KEY_SPLIT, KEY_SPLIT, tp_count), ("ca", "cz", "tp")
    )
    rows = P(("ca", "cz", "tp"), None)
    return jax.shard_map(
        local,
        mesh=split_mesh,
        in_specs=(rows, rows, rows, P("tp", None)),
        out_specs=rows,
        check_vma=False,
    )
```
